32 devices in a mesh: row: 8 (over y, x, core), col: 4 (over z).
Axes of the slice: x: 2, y: 2, z: 4, core: 2. Of those that a mesh axis runs over, the one named last changes fastest.
Arguments:
- mixture_fractions: float32 [54, 64, 512], P(None, 'row', 'col'), may hold values from -6 to 6
- spreading_coefficient: float32 [64, 512], P('row', 'col'), may hold values from 0.02 to 0.12
- flow_speed_vector: float32 [2, 64, 512], P(None, 'row', 'col'), may hold values from -0.15 to 0.15
- thermal_state: float32 [64, 512], P('row', 'col'), may hold values from -6 to 6
- chemistry_active_indicator: int32 [64, 512], P('row', 'col'), may hold values from 0 to 1, as said below
- entry_level_matrix: bfloat16 [256, 55], replicated, may hold values from -0.875 to 0.875
- entry_level_offset: float32 [256], replicated, may hold values from -3 to 3
- hidden_level_matrix: bfloat16 [256, 256], replicated, may hold values from -0.375 to 0.375
- hidden_level_offset: float32 [256], replicated, may hold values from -3 to 3
- final_level_matrix: bfloat16 [54, 256], replicated, may hold values from -0.375 to 0.375
- final_level_offset: float32 [54], replicated, may hold values from -3 to 3
Outputs:
- species_next: float32 [54, 64, 512], P(None, 'row', 'col')
The draws below stay inside these ranges and needn't reach their ends.
Inputs may be any that keep to these rules, and one draw needn't show every extreme that they name: `chemistry_active_indicator`: split the grid into tiles of 8 x 128 cells and bands of 8 rows. Every tile holds at most 384 flagged cells, and in every band some tile holds exactly 384; every band holds exactly 512 flagged cells.
All inputs are finite; a program needn't handle non-finite values.
Results may differ from the reference program's by a relative error of at most 0.0003.
Values sent between devices are 32-bit elements; how exact they have to be, the bound alone decides.
A program may use at most 64 MiB of HBM per device.

```python
import math
import jax
import jax.numpy as jnp
from jax import lax

CHEMICAL_KINDS = 54
HID = 256
SUBSTEPS = 8
TRANSPORT_STEPS = 3
CY = 8
CX = 128
MESH_HEIGHT = 64
MESH_WIDTH = 512
ROW_SHARE = 128
N_ROW = 8
N_COL = 4


def draw_chemistry_active_indicator(key, part):
    first_key, second_key, third_key = jax.random.split(key, 3)
    share_cells = CY * CX // 8
    cell_capacity = 3 * share_cells
    cell_total = CY * CX
    remainder = N_COL * share_cells - cell_capacity
    weights = jax.random.randint(first_key, (N_ROW, N_COL), 2, 6)
    busiest = jax.random.randint(second_key, (N_ROW,), 0, N_COL)
    holds_most_work = jnp.arange(N_COL)[None, :] == busiest[:, None]
    weights = jnp.where(holds_most_work, 0, weights)
    lowest_share = remainder * weights // jnp.sum(weights, axis=1, keepdims=True)
    leftover_cells = remainder - jnp.sum(lowest_share, axis=1, keepdims=True)
    drawn_position = jnp.cumsum(jnp.where(holds_most_work, 0, 1), axis=1) - 1
    extra_cell = jnp.where(jnp.logical_and(jnp.logical_not(holds_most_work), drawn_position < leftover_cells), 1, 0)
    flagged_counts = jnp.where(holds_most_work, cell_capacity, lowest_share + extra_cell).reshape(-1, 1)
    subkeys = jax.random.split(third_key, N_ROW * N_COL)
    orders = jax.vmap(lambda single: jax.random.permutation(single, cell_total))(subkeys)
    active = (orders < flagged_counts).astype(jnp.int32)
    active = active.reshape(N_ROW, N_COL, CY, CX).transpose(0, 2, 1, 3)
    return active.reshape(CY * N_ROW, CX * N_COL)


def level_of(stream_key, shape, pieces, low, high):
    level = 1.0
    for dim, parts in pieces:
        steps = jax.random.uniform(jax.random.fold_in(jax.random.fold_in(stream_key, 6), dim), (parts,), jnp.float32, low / len(pieces), high / len(pieces))
        level = level * jnp.repeat(jnp.exp(steps), shape[dim] // parts).reshape((-1,) + (1,) * (len(shape) - 1 - dim))
    return level


def noise(rng, shape, width, limit, cuts=(), kind=jnp.bfloat16):
    values = width * jax.random.normal(rng, shape, jnp.float32)
    if cuts:
        values = values * level_of(rng, shape, cuts, -0.22, 0.18)
    return jnp.clip(values, -limit, limit).astype(kind)


def setup_inputs(seed: int = 0) -> dict:
    key_list = jax.random.split(jax.random.key(seed), 12)
    mixture_fractions = noise(key_list[0], (CHEMICAL_KINDS, MESH_HEIGHT, MESH_WIDTH), 1.0, 6.0, ((1, 8), (2, 4)), jnp.float32)
    spreading_coefficient = jnp.clip(jnp.exp(math.log(0.12) - 1.7917595 * jax.random.uniform(key_list[1], (MESH_HEIGHT, MESH_WIDTH), jnp.float32) ** level_of(key_list[1], (MESH_HEIGHT, MESH_WIDTH), ((0, 8), (1, 4)), -0.2, 0.2)), 0.02, 0.12)
    flow_speed_vector = jnp.clip(jax.random.uniform(key_list[2], (2, MESH_HEIGHT, MESH_WIDTH), jnp.float32, -0.15, 0.15) * level_of(key_list[2], (2, MESH_HEIGHT, MESH_WIDTH), ((1, 8), (2, 4)), -0.4, 0.0), -0.15, 0.15)
    thermal_state = noise(key_list[3], (MESH_HEIGHT, MESH_WIDTH), 1.0, 6.0, ((0, 8), (1, 4)), jnp.float32)
    chemistry_active_indicator = draw_chemistry_active_indicator(jax.random.fold_in(key_list[11], 71), 0)
    entry_level_matrix = noise(key_list[5], (HID, CHEMICAL_KINDS + 1), (CHEMICAL_KINDS + 1) ** -0.5, 0.875)
    entry_level_offset = noise(key_list[6], (HID,), 0.5, 3.0, (), jnp.float32)
    hidden_level_matrix = noise(key_list[7], (HID, HID), HID ** -0.5, 0.375)
    hidden_level_offset = noise(key_list[8], (HID,), 0.5, 3.0, (), jnp.float32)
    final_level_matrix = noise(key_list[9], (CHEMICAL_KINDS, HID), HID ** -0.5, 0.375)
    final_level_offset = noise(key_list[10], (CHEMICAL_KINDS,), 0.5, 3.0, (), jnp.float32)
    return {"mixture_fractions": mixture_fractions, "spreading_coefficient": spreading_coefficient, "flow_speed_vector": flow_speed_vector, "thermal_state": thermal_state, "chemistry_active_indicator": chemistry_active_indicator, "entry_level_matrix": entry_level_matrix, "entry_level_offset": entry_level_offset, "hidden_level_matrix": hidden_level_matrix, "hidden_level_offset": hidden_level_offset, "final_level_matrix": final_level_matrix, "final_level_offset": final_level_offset}


time_step = 1.0
chem_step = 0.0625


def advance(padded, pad_diff, speed_cols, speed_rows):
    left_vals = padded[..., 1:-1, :-1]
    right_vals = padded[..., 1:-1, 1:]
    face_diff = 0.5 * (pad_diff[1:-1, :-1] + pad_diff[1:-1, 1:])
    face_speed = 0.5 * (speed_cols[1:-1, :-1] + speed_cols[1:-1, 1:])
    flux_cols = face_diff * (right_vals - left_vals) - (jnp.maximum(face_speed, 0.0) * left_vals + jnp.minimum(face_speed, 0.0) * right_vals)
    lower_vals = padded[..., :-1, 1:-1]
    upper_vals = padded[..., 1:, 1:-1]
    face_diff = 0.5 * (pad_diff[:-1, 1:-1] + pad_diff[1:, 1:-1])
    face_speed = 0.5 * (speed_rows[:-1, 1:-1] + speed_rows[1:, 1:-1])
    flux_rows = face_diff * (upper_vals - lower_vals) - (jnp.maximum(face_speed, 0.0) * lower_vals + jnp.minimum(face_speed, 0.0) * upper_vals)
    change = flux_cols[..., 1:] - flux_cols[..., :-1] + flux_rows[..., 1:, :] - flux_rows[..., :-1, :]
    return padded[..., 1:-1, 1:-1] + time_step * change


def network(inputs, entry_level_matrix, entry_level_offset, hidden_level_matrix, hidden_level_offset, final_level_matrix, final_level_offset):
    hidden = jnp.tanh(jnp.dot(entry_level_matrix, inputs, preferred_element_type=jnp.float32) + entry_level_offset[:, None]).astype(jnp.bfloat16)
    hidden = jnp.tanh(jnp.dot(hidden_level_matrix, hidden, preferred_element_type=jnp.float32) + hidden_level_offset[:, None]).astype(jnp.bfloat16)
    return jnp.dot(final_level_matrix, hidden, preferred_element_type=jnp.float32) + final_level_offset[:, None]


def integrate(state, heat, entry_level_matrix, entry_level_offset, hidden_level_matrix, hidden_level_offset, final_level_matrix, final_level_offset):
    total = jnp.zeros(state.shape, jnp.float32)
    for index in range(SUBSTEPS):
        inputs = jnp.concatenate([state + chem_step * total, heat[None]], 0).astype(jnp.bfloat16)
        total = total + network(inputs, entry_level_matrix, entry_level_offset, hidden_level_matrix, hidden_level_offset, final_level_matrix, final_level_offset)
    return chem_step * total


def reference(mixture_fractions, spreading_coefficient, flow_speed_vector, thermal_state, chemistry_active_indicator, entry_level_matrix, entry_level_offset, hidden_level_matrix, hidden_level_offset, final_level_matrix, final_level_offset):
    pad_diff = jnp.pad(spreading_coefficient, 1)
    pad_speed = jnp.pad(flow_speed_vector, ((0, 0), (1, 1), (1, 1)))
    carried_quantity = mixture_fractions
    for section in range(TRANSPORT_STEPS):
        carried_quantity = lax.map(lambda field: advance(jnp.pad(field, 1), pad_diff, pad_speed[0], pad_speed[1]), carried_quantity)
    predictor_vector = jnp.concatenate([carried_quantity, thermal_state[None]], 0).reshape(CHEMICAL_KINDS + 1, MESH_HEIGHT * MESH_WIDTH)
    cell_total = MESH_HEIGHT * MESH_WIDTH
    chosen = jnp.nonzero(chemistry_active_indicator.reshape(-1), size=cell_total // 8, fill_value=cell_total)[0].astype(jnp.int32)
    blocks = chosen.reshape(-1, ROW_SHARE)

    def per_block(cells_here):
        inputs = jnp.take(predictor_vector, cells_here, axis=1, mode="fill", fill_value=0)
        return integrate(inputs[:CHEMICAL_KINDS], inputs[CHEMICAL_KINDS], entry_level_matrix, entry_level_offset, hidden_level_matrix, hidden_level_offset, final_level_matrix, final_level_offset)

    rates = lax.map(per_block, blocks)
    rates = jnp.transpose(rates, (1, 0, 2)).reshape(CHEMICAL_KINDS, -1)
    increments = jnp.zeros((CHEMICAL_KINDS, cell_total + 1), jnp.float32).at[:, chosen].add(rates)[:, :cell_total]
    return (carried_quantity.reshape(CHEMICAL_KINDS, cell_total) + increments).reshape(CHEMICAL_KINDS, MESH_HEIGHT, MESH_WIDTH)
```

```python
import functools

import jax
import jax.numpy as jnp
from jax import lax
from jax.experimental import pallas as pl
from jax.experimental.pallas import tpu as pltpu
from jax.sharding import PartitionSpec as P

SUBSTEPS = 8
TRANSPORT_STEPS = 3
CHEM_STEP = 0.0625
GROUP = 4
SLOT = 8
CHUNKS = 4
WIDTH = 64
PIECE = 7
PARTS = 3
MESH_ID = pl.DeviceIdType.MESH
DIRECTIONS = tuple((dr, dc) for dr in (-1, 0, 1) for dc in (-1, 0, 1) if (dr, dc) != (0, 0))


def roll_lanes(x, shift):
    return pltpu.roll(x, shift % x.shape[-1], x.ndim - 1)


def roll_rows(x, shift):
    return pltpu.roll(x, shift % x.shape[-2], x.ndim - 2)


def around_rows(centre, outer, first, last):
    cu, hu = roll_rows(centre, -1), roll_rows(outer, -1)
    cd, hd = roll_rows(centre, 1), roll_rows(outer, 1)
    return (
        jnp.where(last, hu, cu),
        jnp.where(first, hd, cd),
        jnp.where(last, cu, hu),
        jnp.where(first, cd, hd),
    )


def coefficients(d, u, v, de, dw, dn, ds, ue, uw, vn, vs):
    de, dw, dn, ds = (0.5 * (d + x) for x in (de, dw, dn, ds))
    ue, uw, vn, vs = 0.5 * (u + ue), 0.5 * (u + uw), 0.5 * (v + vn), 0.5 * (v + vs)
    own = (
        1.0
        - (de + jnp.maximum(ue, 0.0))
        - (dw - jnp.minimum(uw, 0.0))
        - (dn + jnp.maximum(vn, 0.0))
        - (ds - jnp.minimum(vs, 0.0))
    )
    return (
        own,
        de - jnp.minimum(ue, 0.0),
        dw + jnp.maximum(uw, 0.0),
        dn - jnp.minimum(vn, 0.0),
        ds + jnp.maximum(vs, 0.0),
    )


def apply_step(w, own, east, west, north, south):
    return w[0] * own + w[1] * east + w[2] * west + w[3] * north + w[4] * south


def transport_kernel(
    rows, cols, species,
    mix_hbm, diff_hbm, speed_hbm, heat_hbm, active_hbm, w1_hbm, w2_hbm, w3_hbm,
    b1_hbm, b2_hbm, b3_hbm,
    adv, chosen, w1_p, w2_p, w13_p, w3_p, b13_p, b2_ref, b3_p,
    b1_ref, b3_ref,
    field, halo, side, corner, weight, joins, heat_v, active_v, w1_v, w2_v, w3_v,
    local_sem, send_sem, recv_sem,
):
    r, c = lax.axis_index("row"), lax.axis_index("col")
    padded = pl.cdiv(species, GROUP) * GROUP
    slots = padded // GROUP
    coef = padded
    packed = padded + GROUP

    loads = [
        pltpu.make_async_copy(mix_hbm, field.at[pl.ds(0, species)], local_sem.at[0]),
        pltpu.make_async_copy(diff_hbm, field.at[coef], local_sem.at[1]),
        pltpu.make_async_copy(speed_hbm, field.at[pl.ds(coef + 1, 2)], local_sem.at[2]),
        pltpu.make_async_copy(heat_hbm, heat_v, local_sem.at[3]),
        pltpu.make_async_copy(active_hbm, active_v, local_sem.at[4]),
        pltpu.make_async_copy(w1_hbm, w1_v, local_sem.at[5]),
        pltpu.make_async_copy(w2_hbm, w2_v, local_sem.at[6]),
        pltpu.make_async_copy(w3_hbm, w3_v, local_sem.at[7]),
        pltpu.make_async_copy(b1_hbm, b1_ref, local_sem.at[8]),
        pltpu.make_async_copy(b2_hbm, b2_ref, local_sem.at[9]),
        pltpu.make_async_copy(b3_hbm, b3_ref, local_sem.at[10]),
    ]
    for load in loads:
        load.start()
    halo[...] = jnp.zeros_like(halo)
    side[...] = jnp.zeros_like(side)
    corner[...] = jnp.zeros_like(corner)

    def there(dr, dc):
        ok = jnp.bool_(True)
        if dr:
            ok = jnp.logical_and(ok, r + dr < rows if dr > 0 else r + dr >= 0)
        if dc:
            ok = jnp.logical_and(ok, c + dc < cols if dc > 0 else c + dc >= 0)
        return ok

    barrier = pltpu.get_barrier_semaphore()
    for dr, dc in DIRECTIONS:
        @pl.when(there(dr, dc))
        def _(dr=dr, dc=dc):
            pl.semaphore_signal(barrier, inc=1, device_id=(r + dr, c + dc), device_id_type=MESH_ID)

    for s in [*range(species, padded), coef + 3]:
        field[s] = jnp.zeros(field.shape[1:], jnp.float32)
    lane = lax.broadcasted_iota(jnp.int32, (8, 128), 1)
    row = lax.broadcasted_iota(jnp.int32, (8, 128), 0)
    first, last = row == 0, row == 7
    west_end, east_end = lane == 0, lane == 127
    in_slot = lane % SLOT
    slot = lane // SLOT
    for load in loads[:3]:
        load.wait()
    pack = jnp.zeros((GROUP, 8, 128), jnp.float32)
    for k in range(slots + 1):
        pack = jnp.where(slot == k, roll_lanes(field[pl.ds(GROUP * k, GROUP)], SLOT * k + 3), pack)
    field[pl.ds(packed, GROUP)] = pack

    one = lambda ok: jnp.where(ok, 1, 0)
    row_sides, col_sides = one(r > 0) + one(r < rows - 1), one(c > 0) + one(c < cols - 1)
    pl.semaphore_wait(barrier, (1 + row_sides) * (1 + col_sides) - 1)

    pieces = [(packed - GROUP, 2 * GROUP)] + [
        (GROUP * k, GROUP * min(PIECE, slots - k)) for k in range(0, slots, PIECE)
    ]

    def message(index, piece=0):
        dr, dc = DIRECTIONS[index]
        number = index if piece == 0 else 6 + 2 * piece + (dr + 1) // 2
        strip = {1: pl.ds(5, 3), -1: pl.ds(0, 3), 0: pl.ds(0, 8)}[dr]
        if dc == 0:
            some = pl.ds(*pieces[piece])
            src, dst = field.at[some, strip, :], halo.at[some, strip, :]
        else:
            target = side if dr == 0 else corner
            src = field.at[pl.ds(packed, GROUP), strip, :]
            dst = target.at[pl.ds(0 if dc > 0 else GROUP, GROUP), strip, :]
        return pltpu.make_async_remote_copy(
            src_ref=src, dst_ref=dst, send_sem=send_sem.at[number], recv_sem=recv_sem.at[number],
            device_id=(r + dr, c + dc), device_id_type=MESH_ID,
        )

    def for_each(action, numbers, sign):
        for number in numbers:
            for index, (dr, dc) in enumerate(DIRECTIONS):
                if number and dc:
                    continue

                @pl.when(there(sign * dr, sign * dc))
                def _(index=index, number=number):
                    action(message(index, number))

    def arrive(begin):
        for_each(lambda m: m.wait_recv(), [1 + begin // PIECE], -1)

    everything = range(len(pieces))
    for_each(lambda m: m.start(), everything, 1)

    for load in loads[3:]:
        load.wait()
    w1_p[...] = jnp.zeros_like(w1_p)
    w1_p[pl.ds(0, species + 1), :] = w1_v[...]
    w1_p[pl.ds(WIDTH, species), :] = w1_v[pl.ds(0, species), :]
    rest = b1_ref[...]
    for i in range(3):
        term = rest.astype(jnp.bfloat16)
        w1_p[pl.ds(species + 1 + i, 1), :] = term
        rest = rest - term.astype(jnp.float32)
    w2_p[...] = jnp.transpose(w2_v[...].astype(jnp.float32)).astype(jnp.bfloat16)
    w3_p[...] = jnp.zeros_like(w3_p)
    w3_p[pl.ds(0, species), :] = (CHEM_STEP * w3_v[...].astype(jnp.float32)).astype(jnp.bfloat16)
    w13_p[...] = lax.dot_general(
        w3_p[pl.ds(0, species), :], w1_v[pl.ds(0, species), :], (((0,), (0,)), ((), ())),
        preferred_element_type=jnp.float32,
    ).astype(jnp.bfloat16)
    b3_row = jnp.concatenate([CHEM_STEP * b3_ref[...], jnp.zeros((1, 128 - species), jnp.float32)], axis=1)
    rest, terms = b3_row, []
    for _ in range(3):
        terms.append(rest.astype(jnp.bfloat16).astype(jnp.float32))
        rest = rest - terms[-1]
    terms = jnp.concatenate(terms + [jnp.zeros((5, 128), jnp.float32)], axis=0).astype(jnp.bfloat16)
    b13_p[...] = jnp.sum(jnp.dot(terms[:, :species], w1_v[pl.ds(0, species), :], preferred_element_type=jnp.float32), axis=0, keepdims=True)
    b3_p[...] = SUBSTEPS * jnp.transpose(jnp.broadcast_to(b3_row, (128, 128)))[:WIDTH]

    capacity = chosen.shape[0]
    flags = jnp.where(active_v[...] == 1, 1.0, 0.0)
    upto = lax.broadcasted_iota(jnp.int32, (128, 128), 0) <= lax.broadcasted_iota(jnp.int32, (128, 128), 1)
    upto = jnp.where(upto, 1.0, 0.0).astype(jnp.bfloat16)
    within = jnp.dot(flags.astype(jnp.bfloat16), upto, preferred_element_type=jnp.float32)
    offset = jnp.dot(flags.astype(jnp.bfloat16), jnp.ones((128, 128), jnp.bfloat16), preferred_element_type=jnp.float32)
    offset = jnp.where(row >= 1, roll_rows(offset, 1), 0.0)
    for shift in (1, 2, 4):
        offset = offset + jnp.where(row >= shift, roll_rows(offset, shift), 0.0)
    place = jnp.where(flags > 0.0, within + offset - 1.0, -1.0)
    index = lax.broadcasted_iota(jnp.int32, (capacity, 128), 0).astype(jnp.float32)
    for q in range(8):
        hit = index == place[q : q + 1]
        chosen[:, 128 * q : 128 * (q + 1)] = jnp.where(hit, 1.0, 0.0).astype(jnp.bfloat16)

    for_each(lambda m: m.wait_recv(), [0], -1)

    own_c, own_h = field[pl.ds(packed, GROUP)], halo[pl.ds(packed, GROUP)]
    lower = in_slot < 3
    faces = [
        (jnp.where(lower, side[:GROUP], own_c), jnp.where(lower, corner[:GROUP], own_h)),
        (jnp.where(lower, own_c, side[GROUP:]), jnp.where(lower, own_h, corner[GROUP:])),
    ]
    in_outer = jnp.where(row < 4, jnp.where(r < rows - 1, 1.0, 0.0), jnp.where(r > 0, 1.0, 0.0))
    in_left = jnp.where(lower, jnp.where(c > 0, 1.0, 0.0), 1.0)
    in_right = jnp.where(lower, 1.0, jnp.where(c < cols - 1, 1.0, 0.0))

    def joined(left, right):
        return jnp.where(in_slot == 7, roll_lanes(right, -4), roll_lanes(left, -2))

    def around_lanes(x, join, k):
        moved = roll_lanes(join, -SLOT * k)
        return jnp.where(east_end, moved, roll_lanes(x, -1)), jnp.where(west_end, moved, roll_lanes(x, 1))

    def replicate(x):
        x = jnp.where(slot == slots, x, 0.0)
        for step in (8, 16, 32, 64):
            x = x + roll_lanes(x, step)
        return x

    def weights(dc_, uc, vc, dh, uh, vh, lanes_c, lanes_h, mask_c, mask_h):
        dnc, dsc, dnh, dsh = around_rows(dc_, dh, first, last)
        vnc, vsc, vnh, vsh = around_rows(vc, vh, first, last)
        (dec, dwc), (uec, uwc) = lanes_c
        (deh, dwh), (ueh, uwh) = lanes_h
        wc = coefficients(dc_, uc, vc, dec, dwc, dnc, dsc, uec, uwc, vnc, vsc)
        wh = coefficients(dh, uh, vh, deh, dwh, dnh, dsh, ueh, uwh, vnh, vsh)
        if mask_c is not None:
            wc = tuple(w * mask_c for w in wc)
        return wc, tuple(w * mask_h for w in wh)

    face_w = []
    for (fc, fh), mask in zip(faces, (in_left, in_right)):
        dc_, uc, vc = (replicate(fc[i]) for i in range(3))
        dh, uh, vh = (replicate(fh[i]) for i in range(3))
        pair = lambda x: (roll_lanes(x, -1), roll_lanes(x, 1))
        face_w.append(weights(dc_, uc, vc, dh, uh, vh, (pair(dc_), pair(uc)), (pair(dh), pair(uh)), mask, mask * in_outer))
    join_c, join_h = joined(faces[0][0], faces[1][0]), joined(faces[0][1], faces[1][1])
    tile_c, tile_h = field[pl.ds(coef, 3)], halo[pl.ds(coef, 3)]
    lanes_c = tuple(around_lanes(tile_c[i], join_c[i], slots) for i in range(2))
    lanes_h = tuple(around_lanes(tile_h[i], join_h[i], slots) for i in range(2))
    wc, wh = weights(*(tile_c[i] for i in range(3)), *(tile_h[i] for i in range(3)), lanes_c, lanes_h, None, in_outer)

    for i in range(5):
        weight[i] = wc[i]
        weight[5 + i] = wh[i]
    for step in range(TRANSPORT_STEPS):
        joins[2 * step] = joined(faces[0][0], faces[1][0])
        joins[2 * step + 1] = joined(faces[0][1], faces[1][1])
        if step < TRANSPORT_STEPS - 1:
            moved = []
            for (fc, fh), (fwc, fwh) in zip(faces, face_w):
                nc, sc, nh, sh = around_rows(fc, fh, first, last)
                moved.append((
                    apply_step(fwc, fc, roll_lanes(fc, -1), roll_lanes(fc, 1), nc, sc),
                    apply_step(fwh, fh, roll_lanes(fh, -1), roll_lanes(fh, 1), nh, sh),
                ))
            faces = moved

    def advance_group(k):
        here = pl.ds(GROUP * k, GROUP)
        xc, xh = field[here], halo[here]
        for step in range(TRANSPORT_STEPS):
            nc, sc, nh, sh = around_rows(xc, xh, first, last)
            ec, wcc = around_lanes(xc, joins[2 * step], k)
            new = apply_step([weight[i] for i in range(5)], xc, ec, wcc, nc, sc)
            if step < TRANSPORT_STEPS - 1:
                eh, whh = around_lanes(xh, joins[2 * step + 1], k)
                xh = apply_step([weight[5 + i] for i in range(5)], xh, eh, whh, nh, sh)
            xc = new
        adv[pl.ds(8 * GROUP * k, 8 * GROUP), :] = xc.reshape(8 * GROUP, 128)

    for begin in range(0, slots, PIECE):
        arrive(begin)
        for k in range(begin, min(begin + PIECE, slots)):
            advance_group(k)

    adv[pl.ds(8 * species, 8), :] = heat_v[...]
    adv[pl.ds(8 * (species + 1), 24), :] = jnp.ones((24, 128), jnp.float32)
    adv[pl.ds(8 * (species + 4), 8 * (WIDTH - species - 4)), :] = jnp.zeros((8 * (WIDTH - species - 4), 128), jnp.float32)
    for_each(lambda m: m.wait_send(), everything, 1)


def chemistry_kernel(
    species, adv, chosen, w1_p, w2_p, w13_p, w3_p, b13_p, b2_ref, b3_p, out_hbm,
    pre, sums, spread, out_v, sem,
):
    capacity, cells = chosen.shape
    hidden = w2_p.shape[0]
    chunk = capacity // CHUNKS
    tail = 2 * hidden - capacity
    f32, bf16 = jnp.float32, jnp.bfloat16
    rows = lambda i: pl.ds(chunk * i, chunk)

    def features(p):
        x = jnp.concatenate([adv[pl.ds(2 * p + j, WIDTH, stride=8), :] for j in range(2)], axis=1)
        high = x.astype(bf16)
        low = (x - high.astype(f32)).astype(bf16)
        return jnp.concatenate([high, low, jnp.zeros((hidden - 2 * WIDTH, 2 * 128), bf16)], axis=0)

    def cell_tile(x, tile):
        if tile == 0:
            return x[:hidden]
        return jnp.concatenate([x[hidden:], jnp.zeros((tail, x.shape[1]), x.dtype)], axis=0)

    def body(*acc):
        acc0, acc1 = acc[:CHUNKS], acc[CHUNKS : 2 * CHUNKS]
        totals, parts = acc[2 * CHUNKS : 2 * CHUNKS + 2], acc[2 * CHUNKS + 2 :]
        for j in range(2):
            for m in range(2):
                pltpu.matmul_push_rhs(features(2 * m + j), j, m, transpose=True)
        for j in range(2):
            for i in range(CHUNKS):
                for m, accs in enumerate((acc0, acc1)):
                    p = 2 * m + j
                    pltpu.matmul_acc_lhs(accs[i], chosen[rows(i), pl.ds(256 * p, 256)], load_staged_rhs=None if i else j)
        pltpu.matmul_push_rhs(w1_p[...], 0, 1)
        pltpu.matmul_push_rhs(w2_p[...], 0, 0)
        pltpu.matmul_push_rhs(w13_p[...], 1, 1)
        for i in range(CHUNKS):
            x = (pltpu.matmul_pop(acc0[i]) + pltpu.matmul_pop(acc1[i])).astype(bf16)
            pltpu.matmul_acc_lhs(acc1[i], x, load_staged_rhs=None if i else 0)
        last = []
        for step in range(SUBSTEPS):
            for i in range(CHUNKS):
                x = pltpu.matmul_pop(acc1[i])
                if step:
                    x = x + pre[rows(i), :]
                if step < SUBSTEPS - 1:
                    pre[rows(i), :] = x + b13_p[...]
                pltpu.matmul_acc_lhs(acc0[i], jnp.tanh(x).astype(bf16), load_staged_rhs=None if step or i else 0)
            if step == SUBSTEPS - 1:
                x = sums[...]
                high = x.astype(bf16)
                low = (x - high.astype(f32)).astype(bf16)
                for tile in range(2):
                    for j, x in enumerate((high, low)):
                        pltpu.matmul_push_rhs(cell_tile(x, tile), j, 1, transpose=True)
                        pltpu.matmul_acc_lhs(totals[tile], w3_p[...], load_staged_rhs=j)
            for i in range(CHUNKS):
                h = jnp.tanh(pltpu.matmul_pop(acc0[i]) + b2_ref[...]).astype(bf16)
                if step == SUBSTEPS - 1:
                    last.append(h)
                    continue
                pltpu.matmul_acc_lhs(acc1[i], h, load_staged_rhs=None if step or i else 1)
                h = h.astype(f32)
                sums[rows(i), :] = h if step == 0 else sums[rows(i), :] + h
        h = jnp.concatenate(last, axis=0)
        for tile in range(2):
            pltpu.matmul_push_rhs(cell_tile(h, tile), tile, 1, transpose=True)
        for tile in range(2):
            pltpu.matmul_acc_lhs(totals[tile], w3_p[...], load_staged_rhs=tile)

        def place(m, j, tile):
            flags = chosen[:, pl.ds(256 * (2 * m + j), 256)]
            pltpu.matmul_push_rhs(cell_tile(flags, tile), tile, m)

        for tile in range(2):
            for m in range(2):
                place(m, 0, tile)
        terms = []
        for tile in range(2):
            x = pltpu.matmul_pop(totals[tile]) + jnp.concatenate([b3_p[...]] * 2, axis=1)
            high = x.astype(bf16)
            terms.append((high, (x - high.astype(f32)).astype(bf16)))
        for j in range(2):
            for tile in range(2):
                for m in range(2):
                    pltpu.matmul_acc_lhs(parts[2 * m + j], terms[tile][0], load_staged_rhs=tile)
                    pltpu.matmul_acc_lhs(parts[2 * m + j], terms[tile][1])
                    if j == 0:
                        place(m, 1, tile)
        for j in range(2):
            for m in range(2):
                x = pltpu.matmul_pop(parts[2 * m + j])
                for k in range(2):
                    spread[pl.ds(WIDTH * (2 * (2 * m + j) + k), WIDTH), :] = x[:, 128 * k : 128 * (k + 1)]

    accs = [pltpu.ACC(m)((chunk, hidden), f32) for m in (0, 1) for _ in range(CHUNKS)]
    accs += [pltpu.ACC(1)((WIDTH, hidden), f32) for _ in range(2)]
    accs += [pltpu.ACC(m)((WIDTH, hidden), f32) for m in (0, 1) for _ in range(2)]
    pl.run_scoped(body, *accs)
    part = pl.cdiv(species, PARTS)
    copies = []
    for n, begin in enumerate(range(0, species, part)):
        size = min(part, species - begin)
        for s in range(begin, begin + size):
            out_v[s] = adv[pl.ds(8 * s, 8), :] + spread[pl.ds(s, 8, stride=WIDTH), :]
        some = pl.ds(begin, size)
        copies.append(pltpu.make_async_copy(out_v.at[some], out_hbm.at[some], sem.at[n]))
        copies[-1].start()
    for copy in copies:
        copy.wait()


def shards(rows, cols, mix, diff, speed, heat, active, w1, b1, w2, b2, w3, b3):
    species, height, width = mix.shape
    padded = pl.cdiv(species, GROUP) * GROUP
    fields = padded + 2 * GROUP
    hidden, features = w1.shape
    parts = 1 + pl.cdiv(padded // GROUP, PIECE)
    vm = pltpu.VMEM
    f32, bf16 = jnp.float32, jnp.bfloat16
    held = lambda x: pltpu.with_memory_space_constraint(x, pltpu.HBM)
    capacity = 3 * (height * width // 8)
    middle = [
        ((WIDTH * height, width), f32),
        ((capacity, height * width), bf16),
        ((hidden, hidden), bf16),
        ((hidden, hidden), bf16),
        ((hidden, hidden), bf16),
        ((WIDTH, hidden), bf16),
        ((1, hidden), f32),
        ((1, hidden), f32),
        ((WIDTH, 128), f32),
    ]
    made = pl.pallas_call(
        functools.partial(transport_kernel, rows, cols, species),
        out_shape=[jax.ShapeDtypeStruct(*x) for x in middle],
        in_specs=[pl.BlockSpec(memory_space=pltpu.HBM)] * 11,
        out_specs=[pl.BlockSpec(memory_space=vm)] * len(middle),
        scratch_shapes=[
            vm((1, hidden), f32),
            vm((1, species), f32),
            vm((fields, height, width), f32),
            vm((fields, height, width), f32),
            vm((2 * GROUP, height, width), f32),
            vm((2 * GROUP, height, width), f32),
            vm((10, height, width), f32),
            vm((2 * TRANSPORT_STEPS, GROUP, height, width), f32),
            vm((height, width), f32),
            vm((height, width), jnp.int32),
            vm((features, hidden), bf16),
            vm(w2.shape, bf16),
            vm(w3.shape, bf16),
            pltpu.SemaphoreType.DMA((11,)),
            pltpu.SemaphoreType.DMA((6 + 2 * parts,)),
            pltpu.SemaphoreType.DMA((6 + 2 * parts,)),
        ],
        compiler_params=pltpu.CompilerParams(collective_id=0, has_side_effects=True, vmem_limit_bytes=16 << 20),
    )(*(held(x) for x in (mix, diff, speed, heat, active, w1.T, w2, w3, b1[None], b2[None], b3[None])))
    return pl.pallas_call(
        functools.partial(chemistry_kernel, species),
        out_shape=jax.ShapeDtypeStruct(mix.shape, mix.dtype),
        in_specs=[pl.BlockSpec(memory_space=vm)] * len(middle),
        out_specs=pl.BlockSpec(memory_space=pltpu.HBM),
        scratch_shapes=[
            vm((capacity, hidden), f32),
            vm((capacity, hidden), f32),
            vm((WIDTH * height, width), f32),
            vm(mix.shape, f32),
            pltpu.SemaphoreType.DMA((PARTS,)),
        ],
        compiler_params=pltpu.CompilerParams(vmem_limit_bytes=16 << 20),
    )(*made)


def solution(mesh):
    tile = P(None, "row", "col")
    plane = P("row", "col")
    mapped = jax.shard_map(
        functools.partial(shards, mesh.shape["row"], mesh.shape["col"]),
        mesh=mesh,
        in_specs=(tile, plane, tile, plane, plane, P(), P(), P(), P(), P(), P()),
        out_specs=tile,
        check_vma=False,
    )

    def run(*args):
        with jax.sharding.use_abstract_mesh(mesh.abstract_mesh):
            return mapped(*args)

    return run
```

```python
import functools

import jax
import jax.numpy as jnp
from jax import lax
from jax.experimental import pallas as pl
from jax.experimental.pallas import tpu as pltpu
from jax.sharding import PartitionSpec as P

SUBSTEPS = 8
TRANSPORT_STEPS = 3
CHEM_STEP = 0.0625
GROUP = 4
SLOT = 8
CHUNKS = 4
WIDTH = 64
PIECE = 7
PARTS = 3
MESH_ID = pl.DeviceIdType.MESH
DIRECTIONS = tuple((dr, dc) for dr in (-1, 0, 1) for dc in (-1, 0, 1) if (dr, dc) != (0, 0))
ABOVE = tuple((dr, dc) for dr, dc in DIRECTIONS if (dc, dr) > (0, 0))
BELOW = tuple((-dr, -dc) for dr, dc in ABOVE)


def roll_lanes(x, shift):
    return pltpu.roll(x, shift % x.shape[-1], x.ndim - 1)


def roll_rows(x, shift):
    return pltpu.roll(x, shift % x.shape[-2], x.ndim - 2)


def around_rows(centre, outer, first, last):
    cu, hu = roll_rows(centre, -1), roll_rows(outer, -1)
    cd, hd = roll_rows(centre, 1), roll_rows(outer, 1)
    return (
        jnp.where(last, hu, cu),
        jnp.where(first, hd, cd),
        jnp.where(last, cu, hu),
        jnp.where(first, cd, hd),
    )


def coefficients(d, u, v, de, dw, dn, ds, ue, uw, vn, vs):
    de, dw, dn, ds = (0.5 * (d + x) for x in (de, dw, dn, ds))
    ue, uw, vn, vs = 0.5 * (u + ue), 0.5 * (u + uw), 0.5 * (v + vn), 0.5 * (v + vs)
    own = (
        1.0
        - (de + jnp.maximum(ue, 0.0))
        - (dw - jnp.minimum(uw, 0.0))
        - (dn + jnp.maximum(vn, 0.0))
        - (ds - jnp.minimum(vs, 0.0))
    )
    return (
        own,
        de - jnp.minimum(ue, 0.0),
        dw + jnp.maximum(uw, 0.0),
        dn - jnp.minimum(vn, 0.0),
        ds + jnp.maximum(vs, 0.0),
    )


def apply_step(w, own, east, west, north, south):
    return w[0] * own + w[1] * east + w[2] * west + w[3] * north + w[4] * south


def transport_kernel(
    rows, cols, species,
    mix_hbm, diff_hbm, speed_hbm, heat_hbm, active_hbm, w1_hbm, w2_hbm, w3_hbm,
    b1_hbm, b2_hbm, b3_hbm,
    adv, chosen, w1_p, w2_p, w13_p, w3_p, b13_p, b2_ref, b3_p,
    b1_ref, b3_ref,
    field, halo, side, corner, weight, joins, heat_v, active_v, w1_v, w2_v, w3_v,
    local_sem, send_sem, recv_sem, ready_sem,
):
    r, c = lax.axis_index("row"), lax.axis_index("col")
    padded = pl.cdiv(species, GROUP) * GROUP
    slots = padded // GROUP
    coef = padded
    packed = padded + GROUP

    loads = [
        pltpu.make_async_copy(mix_hbm, field.at[pl.ds(0, species)], local_sem.at[0]),
        pltpu.make_async_copy(diff_hbm, field.at[coef], local_sem.at[1]),
        pltpu.make_async_copy(speed_hbm, field.at[pl.ds(coef + 1, 2)], local_sem.at[2]),
        pltpu.make_async_copy(heat_hbm, heat_v, local_sem.at[3]),
        pltpu.make_async_copy(active_hbm, active_v, local_sem.at[4]),
        pltpu.make_async_copy(w1_hbm, w1_v, local_sem.at[5]),
        pltpu.make_async_copy(w2_hbm, w2_v, local_sem.at[6]),
        pltpu.make_async_copy(w3_hbm, w3_v, local_sem.at[7]),
        pltpu.make_async_copy(b1_hbm, b1_ref, local_sem.at[8]),
        pltpu.make_async_copy(b2_hbm, b2_ref, local_sem.at[9]),
        pltpu.make_async_copy(b3_hbm, b3_ref, local_sem.at[10]),
    ]
    for load in loads:
        load.start()
    halo[...] = jnp.zeros_like(halo)
    side[...] = jnp.zeros_like(side)
    corner[...] = jnp.zeros_like(corner)

    def there(dr, dc):
        ok = jnp.bool_(True)
        if dr:
            ok = jnp.logical_and(ok, r + dr < rows if dr > 0 else r + dr >= 0)
        if dc:
            ok = jnp.logical_and(ok, c + dc < cols if dc > 0 else c + dc >= 0)
        return ok

    barrier = pltpu.get_barrier_semaphore()
    for dr, dc in ABOVE:
        @pl.when(there(dr, dc))
        def _(dr=dr, dc=dc):
            pl.semaphore_signal(barrier, inc=1, device_id=(r + dr, c + dc), device_id_type=MESH_ID)

    one = lambda ok: jnp.where(ok, 1, 0)
    below = sum(one(there(dr, dc)) for dr, dc in BELOW)

    @pl.when(below > 0)
    def _():
        pl.semaphore_wait(barrier, below)

    for n, (dr, dc) in enumerate(BELOW):
        @pl.when(there(dr, dc))
        def _(n=n, dr=dr, dc=dc):
            pl.semaphore_signal(ready_sem.at[n], inc=1, device_id=(r + dr, c + dc), device_id_type=MESH_ID)

    for s in [*range(species, padded), coef + 3]:
        field[s] = jnp.zeros(field.shape[1:], jnp.float32)
    lane = lax.broadcasted_iota(jnp.int32, (8, 128), 1)
    row = lax.broadcasted_iota(jnp.int32, (8, 128), 0)
    first, last = row == 0, row == 7
    west_end, east_end = lane == 0, lane == 127
    in_slot = lane % SLOT
    slot = lane // SLOT
    for load in loads[:3]:
        load.wait()
    pack = jnp.zeros((GROUP, 8, 128), jnp.float32)
    for k in range(slots + 1):
        pack = jnp.where(slot == k, roll_lanes(field[pl.ds(GROUP * k, GROUP)], SLOT * k + 3), pack)
    field[pl.ds(packed, GROUP)] = pack

    pieces = [(packed - GROUP, 2 * GROUP)] + [
        (GROUP * k, GROUP * min(PIECE, slots - k)) for k in range(0, slots, PIECE)
    ]

    def message(index, piece=0):
        dr, dc = DIRECTIONS[index]
        number = index if piece == 0 else 6 + 2 * piece + (dr + 1) // 2
        strip = {1: pl.ds(5, 3), -1: pl.ds(0, 3), 0: pl.ds(0, 8)}[dr]
        if dc == 0:
            some = pl.ds(*pieces[piece])
            src, dst = field.at[some, strip, :], halo.at[some, strip, :]
        else:
            target = side if dr == 0 else corner
            src = field.at[pl.ds(packed, GROUP), strip, :]
            dst = target.at[pl.ds(0 if dc > 0 else GROUP, GROUP), strip, :]
        return pltpu.make_async_remote_copy(
            src_ref=src, dst_ref=dst, send_sem=send_sem.at[number], recv_sem=recv_sem.at[number],
            device_id=(r + dr, c + dc), device_id_type=MESH_ID,
        )

    def for_each(action, numbers, sign):
        for number in numbers:
            for index, (dr, dc) in enumerate(DIRECTIONS):
                if number and dc:
                    continue

                @pl.when(there(sign * dr, sign * dc))
                def _(index=index, number=number):
                    action(message(index, number))

    def arrive(begin):
        for_each(lambda m: m.wait_recv(), [1 + begin // PIECE], -1)

    everything = range(len(pieces))
    for n, (dr, dc) in [(None, way) for way in BELOW] + list(enumerate(ABOVE)):
        @pl.when(there(dr, dc))
        def _(n=n, dr=dr, dc=dc):
            if n is not None:
                pl.semaphore_wait(ready_sem.at[n], 1)
            for number in everything if dc == 0 else [0]:
                message(DIRECTIONS.index((dr, dc)), number).start()


    for load in loads[3:]:
        load.wait()
    w1_p[...] = jnp.zeros_like(w1_p)
    w1_p[pl.ds(0, species + 1), :] = w1_v[...]
    w1_p[pl.ds(WIDTH, species), :] = w1_v[pl.ds(0, species), :]
    rest = b1_ref[...]
    for i in range(3):
        term = rest.astype(jnp.bfloat16)
        w1_p[pl.ds(species + 1 + i, 1), :] = term
        rest = rest - term.astype(jnp.float32)
    w2_p[...] = jnp.transpose(w2_v[...].astype(jnp.float32)).astype(jnp.bfloat16)
    w3_p[...] = jnp.zeros_like(w3_p)
    w3_p[pl.ds(0, species), :] = (CHEM_STEP * w3_v[...].astype(jnp.float32)).astype(jnp.bfloat16)
    w13_p[...] = lax.dot_general(
        w3_p[pl.ds(0, species), :], w1_v[pl.ds(0, species), :], (((0,), (0,)), ((), ())),
        preferred_element_type=jnp.float32,
    ).astype(jnp.bfloat16)
    b3_row = jnp.concatenate([CHEM_STEP * b3_ref[...], jnp.zeros((1, 128 - species), jnp.float32)], axis=1)
    rest, terms = b3_row, []
    for _ in range(3):
        terms.append(rest.astype(jnp.bfloat16).astype(jnp.float32))
        rest = rest - terms[-1]
    terms = jnp.concatenate(terms + [jnp.zeros((5, 128), jnp.float32)], axis=0).astype(jnp.bfloat16)
    b13_p[...] = jnp.sum(jnp.dot(terms[:, :species], w1_v[pl.ds(0, species), :], preferred_element_type=jnp.float32), axis=0, keepdims=True)
    b3_p[...] = SUBSTEPS * jnp.transpose(jnp.broadcast_to(b3_row, (128, 128)))[:WIDTH]

    capacity = chosen.shape[0]
    flags = jnp.where(active_v[...] == 1, 1.0, 0.0)
    upto = lax.broadcasted_iota(jnp.int32, (128, 128), 0) <= lax.broadcasted_iota(jnp.int32, (128, 128), 1)
    upto = jnp.where(upto, 1.0, 0.0).astype(jnp.bfloat16)
    within = jnp.dot(flags.astype(jnp.bfloat16), upto, preferred_element_type=jnp.float32)
    offset = jnp.dot(flags.astype(jnp.bfloat16), jnp.ones((128, 128), jnp.bfloat16), preferred_element_type=jnp.float32)
    offset = jnp.where(row >= 1, roll_rows(offset, 1), 0.0)
    for shift in (1, 2, 4):
        offset = offset + jnp.where(row >= shift, roll_rows(offset, shift), 0.0)
    place = jnp.where(flags > 0.0, within + offset - 1.0, -1.0)
    index = lax.broadcasted_iota(jnp.int32, (capacity, 128), 0).astype(jnp.float32)
    for q in range(8):
        hit = index == place[q : q + 1]
        chosen[:, 128 * q : 128 * (q + 1)] = jnp.where(hit, 1.0, 0.0).astype(jnp.bfloat16)

    for_each(lambda m: m.wait_recv(), [0], -1)

    own_c, own_h = field[pl.ds(packed, GROUP)], halo[pl.ds(packed, GROUP)]
    lower = in_slot < 3
    faces = [
        (jnp.where(lower, side[:GROUP], own_c), jnp.where(lower, corner[:GROUP], own_h)),
        (jnp.where(lower, own_c, side[GROUP:]), jnp.where(lower, own_h, corner[GROUP:])),
    ]
    in_outer = jnp.where(row < 4, jnp.where(r < rows - 1, 1.0, 0.0), jnp.where(r > 0, 1.0, 0.0))
    in_left = jnp.where(lower, jnp.where(c > 0, 1.0, 0.0), 1.0)
    in_right = jnp.where(lower, 1.0, jnp.where(c < cols - 1, 1.0, 0.0))

    def joined(left, right):
        return jnp.where(in_slot == 7, roll_lanes(right, -4), roll_lanes(left, -2))

    def around_lanes(x, join, k):
        moved = roll_lanes(join, -SLOT * k)
        return jnp.where(east_end, moved, roll_lanes(x, -1)), jnp.where(west_end, moved, roll_lanes(x, 1))

    def replicate(x):
        x = jnp.where(slot == slots, x, 0.0)
        for step in (8, 16, 32, 64):
            x = x + roll_lanes(x, step)
        return x

    def weights(dc_, uc, vc, dh, uh, vh, lanes_c, lanes_h, mask_c, mask_h):
        dnc, dsc, dnh, dsh = around_rows(dc_, dh, first, last)
        vnc, vsc, vnh, vsh = around_rows(vc, vh, first, last)
        (dec, dwc), (uec, uwc) = lanes_c
        (deh, dwh), (ueh, uwh) = lanes_h
        wc = coefficients(dc_, uc, vc, dec, dwc, dnc, dsc, uec, uwc, vnc, vsc)
        wh = coefficients(dh, uh, vh, deh, dwh, dnh, dsh, ueh, uwh, vnh, vsh)
        if mask_c is not None:
            wc = tuple(w * mask_c for w in wc)
        return wc, tuple(w * mask_h for w in wh)

    face_w = []
    for (fc, fh), mask in zip(faces, (in_left, in_right)):
        dc_, uc, vc = (replicate(fc[i]) for i in range(3))
        dh, uh, vh = (replicate(fh[i]) for i in range(3))
        pair = lambda x: (roll_lanes(x, -1), roll_lanes(x, 1))
        face_w.append(weights(dc_, uc, vc, dh, uh, vh, (pair(dc_), pair(uc)), (pair(dh), pair(uh)), mask, mask * in_outer))
    join_c, join_h = joined(faces[0][0], faces[1][0]), joined(faces[0][1], faces[1][1])
    tile_c, tile_h = field[pl.ds(coef, 3)], halo[pl.ds(coef, 3)]
    lanes_c = tuple(around_lanes(tile_c[i], join_c[i], slots) for i in range(2))
    lanes_h = tuple(around_lanes(tile_h[i], join_h[i], slots) for i in range(2))
    wc, wh = weights(*(tile_c[i] for i in range(3)), *(tile_h[i] for i in range(3)), lanes_c, lanes_h, None, in_outer)

    for i in range(5):
        weight[i] = wc[i]
        weight[5 + i] = wh[i]
    for step in range(TRANSPORT_STEPS):
        joins[2 * step] = joined(faces[0][0], faces[1][0])
        joins[2 * step + 1] = joined(faces[0][1], faces[1][1])
        if step < TRANSPORT_STEPS - 1:
            moved = []
            for (fc, fh), (fwc, fwh) in zip(faces, face_w):
                nc, sc, nh, sh = around_rows(fc, fh, first, last)
                moved.append((
                    apply_step(fwc, fc, roll_lanes(fc, -1), roll_lanes(fc, 1), nc, sc),
                    apply_step(fwh, fh, roll_lanes(fh, -1), roll_lanes(fh, 1), nh, sh),
                ))
            faces = moved

    def advance_group(k):
        here = pl.ds(GROUP * k, GROUP)
        xc, xh = field[here], halo[here]
        for step in range(TRANSPORT_STEPS):
            nc, sc, nh, sh = around_rows(xc, xh, first, last)
            ec, wcc = around_lanes(xc, joins[2 * step], k)
            new = apply_step([weight[i] for i in range(5)], xc, ec, wcc, nc, sc)
            if step < TRANSPORT_STEPS - 1:
                eh, whh = around_lanes(xh, joins[2 * step + 1], k)
                xh = apply_step([weight[5 + i] for i in range(5)], xh, eh, whh, nh, sh)
            xc = new
        adv[pl.ds(8 * GROUP * k, 8 * GROUP), :] = xc.reshape(8 * GROUP, 128)

    for begin in range(0, slots, PIECE):
        arrive(begin)
        for k in range(begin, min(begin + PIECE, slots)):
            advance_group(k)

    adv[pl.ds(8 * species, 8), :] = heat_v[...]
    adv[pl.ds(8 * (species + 1), 24), :] = jnp.ones((24, 128), jnp.float32)
    adv[pl.ds(8 * (species + 4), 8 * (WIDTH - species - 4)), :] = jnp.zeros((8 * (WIDTH - species - 4), 128), jnp.float32)
    for_each(lambda m: m.wait_send(), everything, 1)


def chemistry_kernel(
    species, adv, chosen, w1_p, w2_p, w13_p, w3_p, b13_p, b2_ref, b3_p, out_hbm,
    pre, sums, spread, out_v, sem,
):
    capacity, cells = chosen.shape
    hidden = w2_p.shape[0]
    chunk = capacity // CHUNKS
    tail = 2 * hidden - capacity
    f32, bf16 = jnp.float32, jnp.bfloat16
    rows = lambda i: pl.ds(chunk * i, chunk)

    def features(p):
        x = jnp.concatenate([adv[pl.ds(2 * p + j, WIDTH, stride=8), :] for j in range(2)], axis=1)
        high = x.astype(bf16)
        low = (x - high.astype(f32)).astype(bf16)
        return jnp.concatenate([high, low, jnp.zeros((hidden - 2 * WIDTH, 2 * 128), bf16)], axis=0)

    def cell_tile(x, tile):
        if tile == 0:
            return x[:hidden]
        return jnp.concatenate([x[hidden:], jnp.zeros((tail, x.shape[1]), x.dtype)], axis=0)

    def body(*acc):
        acc0, acc1 = acc[:CHUNKS], acc[CHUNKS : 2 * CHUNKS]
        totals, parts = acc[2 * CHUNKS : 2 * CHUNKS + 2], acc[2 * CHUNKS + 2 :]
        for j in range(2):
            for m in range(2):
                pltpu.matmul_push_rhs(features(2 * m + j), j, m, transpose=True)
        for j in range(2):
            for i in range(CHUNKS):
                for m, accs in enumerate((acc0, acc1)):
                    p = 2 * m + j
                    pltpu.matmul_acc_lhs(accs[i], chosen[rows(i), pl.ds(256 * p, 256)], load_staged_rhs=None if i else j)
        pltpu.matmul_push_rhs(w1_p[...], 0, 1)
        pltpu.matmul_push_rhs(w2_p[...], 0, 0)
        pltpu.matmul_push_rhs(w13_p[...], 1, 1)
        for i in range(CHUNKS):
            x = (pltpu.matmul_pop(acc0[i]) + pltpu.matmul_pop(acc1[i])).astype(bf16)
            pltpu.matmul_acc_lhs(acc1[i], x, load_staged_rhs=None if i else 0)
        last = []
        for step in range(SUBSTEPS):
            for i in range(CHUNKS):
                x = pltpu.matmul_pop(acc1[i])
                if step:
                    x = x + pre[rows(i), :]
                if step < SUBSTEPS - 1:
                    pre[rows(i), :] = x + b13_p[...]
                pltpu.matmul_acc_lhs(acc0[i], jnp.tanh(x).astype(bf16), load_staged_rhs=None if step or i else 0)
            if step == SUBSTEPS - 1:
                x = sums[...]
                high = x.astype(bf16)
                low = (x - high.astype(f32)).astype(bf16)
                for tile in range(2):
                    for j, x in enumerate((high, low)):
                        pltpu.matmul_push_rhs(cell_tile(x, tile), j, 1, transpose=True)
                        pltpu.matmul_acc_lhs(totals[tile], w3_p[...], load_staged_rhs=j)
            for i in range(CHUNKS):
                h = jnp.tanh(pltpu.matmul_pop(acc0[i]) + b2_ref[...]).astype(bf16)
                if step == SUBSTEPS - 1:
                    last.append(h)
                    continue
                pltpu.matmul_acc_lhs(acc1[i], h, load_staged_rhs=None if step or i else 1)
                h = h.astype(f32)
                sums[rows(i), :] = h if step == 0 else sums[rows(i), :] + h
        h = jnp.concatenate(last, axis=0)
        for tile in range(2):
            pltpu.matmul_push_rhs(cell_tile(h, tile), tile, 1, transpose=True)
        for tile in range(2):
            pltpu.matmul_acc_lhs(totals[tile], w3_p[...], load_staged_rhs=tile)

        def place(m, j, tile):
            flags = chosen[:, pl.ds(256 * (2 * m + j), 256)]
            pltpu.matmul_push_rhs(cell_tile(flags, tile), tile, m)

        for tile in range(2):
            for m in range(2):
                place(m, 0, tile)
        terms = []
        for tile in range(2):
            x = pltpu.matmul_pop(totals[tile]) + jnp.concatenate([b3_p[...]] * 2, axis=1)
            high = x.astype(bf16)
            terms.append((high, (x - high.astype(f32)).astype(bf16)))
        for j in range(2):
            for tile in range(2):
                for m in range(2):
                    pltpu.matmul_acc_lhs(parts[2 * m + j], terms[tile][0], load_staged_rhs=tile)
                    pltpu.matmul_acc_lhs(parts[2 * m + j], terms[tile][1])
                    if j == 0:
                        place(m, 1, tile)
        for j in range(2):
            for m in range(2):
                x = pltpu.matmul_pop(parts[2 * m + j])
                for k in range(2):
                    spread[pl.ds(WIDTH * (2 * (2 * m + j) + k), WIDTH), :] = x[:, 128 * k : 128 * (k + 1)]

    accs = [pltpu.ACC(m)((chunk, hidden), f32) for m in (0, 1) for _ in range(CHUNKS)]
    accs += [pltpu.ACC(1)((WIDTH, hidden), f32) for _ in range(2)]
    accs += [pltpu.ACC(m)((WIDTH, hidden), f32) for m in (0, 1) for _ in range(2)]
    pl.run_scoped(body, *accs)
    part = pl.cdiv(species, PARTS)
    copies = []
    for n, begin in enumerate(range(0, species, part)):
        size = min(part, species - begin)
        for s in range(begin, begin + size):
            out_v[s] = adv[pl.ds(8 * s, 8), :] + spread[pl.ds(s, 8, stride=WIDTH), :]
        some = pl.ds(begin, size)
        copies.append(pltpu.make_async_copy(out_v.at[some], out_hbm.at[some], sem.at[n]))
        copies[-1].start()
    for copy in copies:
        copy.wait()


def shards(rows, cols, mix, diff, speed, heat, active, w1, b1, w2, b2, w3, b3):
    species, height, width = mix.shape
    padded = pl.cdiv(species, GROUP) * GROUP
    fields = padded + 2 * GROUP
    hidden, features = w1.shape
    parts = 1 + pl.cdiv(padded // GROUP, PIECE)
    vm = pltpu.VMEM
    f32, bf16 = jnp.float32, jnp.bfloat16
    held = lambda x: pltpu.with_memory_space_constraint(x, pltpu.HBM)
    capacity = 3 * (height * width // 8)
    middle = [
        ((WIDTH * height, width), f32),
        ((capacity, height * width), bf16),
        ((hidden, hidden), bf16),
        ((hidden, hidden), bf16),
        ((hidden, hidden), bf16),
        ((WIDTH, hidden), bf16),
        ((1, hidden), f32),
        ((1, hidden), f32),
        ((WIDTH, 128), f32),
    ]
    made = pl.pallas_call(
        functools.partial(transport_kernel, rows, cols, species),
        out_shape=[jax.ShapeDtypeStruct(*x) for x in middle],
        in_specs=[pl.BlockSpec(memory_space=pltpu.HBM)] * 11,
        out_specs=[pl.BlockSpec(memory_space=vm)] * len(middle),
        scratch_shapes=[
            vm((1, hidden), f32),
            vm((1, species), f32),
            vm((fields, height, width), f32),
            vm((fields, height, width), f32),
            vm((2 * GROUP, height, width), f32),
            vm((2 * GROUP, height, width), f32),
            vm((10, height, width), f32),
            vm((2 * TRANSPORT_STEPS, GROUP, height, width), f32),
            vm((height, width), f32),
            vm((height, width), jnp.int32),
            vm((features, hidden), bf16),
            vm(w2.shape, bf16),
            vm(w3.shape, bf16),
            pltpu.SemaphoreType.DMA((11,)),
            pltpu.SemaphoreType.DMA((6 + 2 * parts,)),
            pltpu.SemaphoreType.DMA((6 + 2 * parts,)),
            pltpu.SemaphoreType.REGULAR((len(ABOVE),)),
        ],
        compiler_params=pltpu.CompilerParams(collective_id=0, has_side_effects=True, vmem_limit_bytes=16 << 20),
    )(*(held(x) for x in (mix, diff, speed, heat, active, w1.T, w2, w3, b1[None], b2[None], b3[None])))
    return pl.pallas_call(
        functools.partial(chemistry_kernel, species),
        out_shape=jax.ShapeDtypeStruct(mix.shape, mix.dtype),
        in_specs=[pl.BlockSpec(memory_space=vm)] * len(middle),
        out_specs=pl.BlockSpec(memory_space=pltpu.HBM),
        scratch_shapes=[
            vm((capacity, hidden), f32),
            vm((capacity, hidden), f32),
            vm((WIDTH * height, width), f32),
            vm(mix.shape, f32),
            pltpu.SemaphoreType.DMA((PARTS,)),
        ],
        compiler_params=pltpu.CompilerParams(vmem_limit_bytes=16 << 20),
    )(*made)


def solution(mesh):
    tile = P(None, "row", "col")
    plane = P("row", "col")
    mapped = jax.shard_map(
        functools.partial(shards, mesh.shape["row"], mesh.shape["col"]),
        mesh=mesh,
        in_specs=(tile, plane, tile, plane, plane, P(), P(), P(), P(), P(), P()),
        out_specs=tile,
        check_vma=False,
    )

    def run(*args):
        with jax.sharding.use_abstract_mesh(mesh.abstract_mesh):
            return mapped(*args)

    return run
```

```python
import functools

import jax
import jax.numpy as jnp
from jax import lax
from jax.experimental import pallas as pl
from jax.experimental.pallas import tpu as pltpu
from jax.sharding import PartitionSpec as P

SUBSTEPS = 8
TRANSPORT_STEPS = 3
CHEM_STEP = 0.0625
TILE = 8
SLOT = 16
EDGE = 3
SUB = 4
CHUNKS = 4
WIDTH = 64
MESH_ID = pl.DeviceIdType.MESH
DIRECTIONS = tuple((dr, dc) for dr in (-1, 0, 1) for dc in (-1, 0, 1) if (dr, dc) != (0, 0))
ABOVE = tuple((dr, dc) for dr, dc in DIRECTIONS if (dc, dr) > (0, 0))
BELOW = tuple((-dr, -dc) for dr, dc in ABOVE)


def roll_lanes(x, shift):
    return pltpu.roll(x, shift % x.shape[-1], x.ndim - 1)


def upwind(d, v):
    return d - jnp.minimum(v, 0.0), d + jnp.maximum(v, 0.0)


def spread_row(x, i):
    return jnp.broadcast_to(x[i : i + 1], x.shape)


def step_weights(east, west, high, low, mask):
    (e, e_out), (w_out, w) = upwind(*(spread_row(east, i) for i in (0, 1))), upwind(*(spread_row(west, i) for i in (0, 1)))
    (h, h_out), (l_out, l) = high, low
    weights = (1.0 - e_out - w_out - h_out - l_out, e, w, h, l)
    return weights if mask is None else tuple(x * mask for x in weights)


def apply_step(w, own, east, west, high, low):
    return w[0] * own + w[1] * east + w[2] * west + w[3] * high + w[4] * low


def transport_kernel(
    rows, cols, species,
    mix_hbm, diff_hbm, speed_hbm, heat_hbm, active_hbm, w1_hbm, w2_hbm, w3_hbm,
    b1_hbm, b2_hbm, b3_hbm,
    adv, chosen, w1_p, w2_p, w13_p, w3_p, b13_p, b2_ref, b3_p,
    b1_ref, b3_ref,
    stage, field, halo, side_w, side_e, to_east, to_west, tile_w, face_w, joins, middle, heat_v, active_v, w1_v, w2_v, w3_v,
    local_sem, send_sem, recv_sem, ready_sem,
):
    r, c = lax.axis_index("row"), lax.axis_index("col")
    tiles = pl.cdiv(species, TILE)
    coef = tiles * TILE
    packed = coef + TILE

    loads = [
        pltpu.make_async_copy(mix_hbm, stage.at[pl.ds(0, species)], local_sem.at[0]),
        pltpu.make_async_copy(diff_hbm, stage.at[coef], local_sem.at[1]),
        pltpu.make_async_copy(speed_hbm, stage.at[pl.ds(coef + 1, 2)], local_sem.at[2]),
        pltpu.make_async_copy(heat_hbm, heat_v, local_sem.at[3]),
        pltpu.make_async_copy(active_hbm, active_v, local_sem.at[4]),
        pltpu.make_async_copy(w1_hbm, w1_v, local_sem.at[5]),
        pltpu.make_async_copy(w2_hbm, w2_v, local_sem.at[6]),
        pltpu.make_async_copy(w3_hbm, w3_v, local_sem.at[7]),
        pltpu.make_async_copy(b1_hbm, b1_ref, local_sem.at[8]),
        pltpu.make_async_copy(b2_hbm, b2_ref, local_sem.at[9]),
        pltpu.make_async_copy(b3_hbm, b3_ref, local_sem.at[10]),
    ]
    for load in loads:
        load.start()
    halo[...] = jnp.zeros_like(halo)
    side_w[...] = jnp.zeros_like(side_w)
    side_e[...] = jnp.zeros_like(side_e)

    def there(dr, dc):
        ok = jnp.bool_(True)
        if dr:
            ok = jnp.logical_and(ok, r + dr < rows if dr > 0 else r + dr >= 0)
        if dc:
            ok = jnp.logical_and(ok, c + dc < cols if dc > 0 else c + dc >= 0)
        return ok

    barrier = pltpu.get_barrier_semaphore()
    for dr, dc in ABOVE:
        @pl.when(there(dr, dc))
        def _(dr=dr, dc=dc):
            pl.semaphore_signal(barrier, inc=1, device_id=(r + dr, c + dc), device_id_type=MESH_ID)

    one = lambda ok: jnp.where(ok, 1, 0)
    below = sum(one(there(dr, dc)) for dr, dc in BELOW)

    @pl.when(below > 0)
    def _():
        pl.semaphore_wait(barrier, below)

    for n, (dr, dc) in enumerate(BELOW):
        @pl.when(there(dr, dc))
        def _(n=n, dr=dr, dc=dc):
            pl.semaphore_signal(ready_sem.at[n], inc=1, device_id=(r + dr, c + dc), device_id_type=MESH_ID)

    for s in [*range(species, coef), *range(coef + 3, coef + TILE)]:
        stage[s] = jnp.zeros(stage.shape[1:], jnp.float32)
    lane = lax.broadcasted_iota(jnp.int32, (TILE, 128), 1)
    row = lax.broadcasted_iota(jnp.int32, (TILE, 128), 0)
    west_end, east_end = lane == 0, lane == 127
    in_slot = lane % SLOT
    slot = lane // SLOT
    for load in loads[:3]:
        load.wait()
    by_row = stage.reshape(stage.shape[0] * TILE, 128)
    def packing(parts):
        pack = None
        for k, x in enumerate(parts):
            x = roll_lanes(x, SLOT * k + EDGE)
            pack = x if pack is None else jnp.where(slot == k, x, pack)
        return pack

    packs = []
    for q in range(TILE):
        parts = []
        for k in range(tiles + 1):
            parts.append(by_row[pl.ds(TILE * TILE * k + q, TILE, stride=TILE), :])
            field[q, pl.ds(TILE * k, TILE), :] = parts[-1]
        packs.append(packing(parts))
        field[q, pl.ds(packed, TILE), :] = packs[-1]
    for v in range(TILE // SUB):
        for to, shift in ((to_east, 0), (to_west, -EDGE)):
            x = None
            for i in range(SUB):
                part = roll_lanes(packs[SUB * v + i], SUB * i + shift)
                x = part if x is None else jnp.where(in_slot // SUB == i, part, x)
            to[v] = x

    pieces = [(coef, 2 * TILE), (0, coef)]

    def message(index, piece=0):
        dr, dc = DIRECTIONS[index]
        number = index if piece == 0 else len(DIRECTIONS) + (dr + 1) // 2
        rows_from = {1: pl.ds(TILE - EDGE, EDGE), -1: pl.ds(0, EDGE), 0: pl.ds(0, TILE)}[dr]
        if dc == 0:
            some = pl.ds(*pieces[piece])
            src, dst = field.at[rows_from, some], halo.at[pl.ds(0 if dr > 0 else EDGE, EDGE), some]
        else:
            target = side_w if dc > 0 else side_e
            made = to_east if dc > 0 else to_west
            some, there_ = {1: (pl.ds(1, 1), pl.ds(0, 1)), -1: (pl.ds(0, 1), pl.ds(3, 1)), 0: (pl.ds(0, 2), pl.ds(1, 2))}[dr]
            src, dst = made.at[some], target.at[there_]
        return pltpu.make_async_remote_copy(
            src_ref=src, dst_ref=dst, send_sem=send_sem.at[number], recv_sem=recv_sem.at[number],
            device_id=(r + dr, c + dc), device_id_type=MESH_ID,
        )

    def for_each(action, numbers, sign):
        for number in numbers:
            for index, (dr, dc) in enumerate(DIRECTIONS):
                if number and dc:
                    continue

                @pl.when(there(sign * dr, sign * dc))
                def _(index=index, number=number):
                    action(message(index, number))

    everything = range(len(pieces))
    for n, (dr, dc) in [(None, way) for way in BELOW] + list(enumerate(ABOVE)):
        @pl.when(there(dr, dc))
        def _(n=n, dr=dr, dc=dc):
            if n is not None:
                pl.semaphore_wait(ready_sem.at[n], 1)
            for number in everything if dc == 0 else [0]:
                message(DIRECTIONS.index((dr, dc)), number).start()


    for load in loads[3:]:
        load.wait()
    w1_p[...] = jnp.zeros_like(w1_p)
    w1_p[pl.ds(0, species + 1), :] = w1_v[...]
    w1_p[pl.ds(WIDTH, species), :] = w1_v[pl.ds(0, species), :]
    rest = b1_ref[...]
    for i in range(3):
        term = rest.astype(jnp.bfloat16)
        w1_p[pl.ds(species + 1 + i, 1), :] = term
        rest = rest - term.astype(jnp.float32)
    w2_p[...] = jnp.transpose(w2_v[...].astype(jnp.float32)).astype(jnp.bfloat16)
    w3_p[...] = jnp.zeros_like(w3_p)
    w3_p[pl.ds(0, species), :] = (CHEM_STEP * w3_v[...].astype(jnp.float32)).astype(jnp.bfloat16)
    w13_p[...] = lax.dot_general(
        w3_p[pl.ds(0, species), :], w1_v[pl.ds(0, species), :], (((0,), (0,)), ((), ())),
        preferred_element_type=jnp.float32,
    ).astype(jnp.bfloat16)
    b3_row = jnp.concatenate([CHEM_STEP * b3_ref[...], jnp.zeros((1, 128 - species), jnp.float32)], axis=1)
    rest, terms = b3_row, []
    for _ in range(3):
        terms.append(rest.astype(jnp.bfloat16).astype(jnp.float32))
        rest = rest - terms[-1]
    terms = jnp.concatenate(terms + [jnp.zeros((5, 128), jnp.float32)], axis=0).astype(jnp.bfloat16)
    b13_p[...] = jnp.sum(jnp.dot(terms[:, :species], w1_v[pl.ds(0, species), :], preferred_element_type=jnp.float32), axis=0, keepdims=True)
    b3_p[...] = SUBSTEPS * jnp.transpose(jnp.broadcast_to(b3_row, (128, 128)))[:WIDTH]

    capacity = chosen.shape[0]
    flags = jnp.where(active_v[...] == 1, 1.0, 0.0)
    upto = lax.broadcasted_iota(jnp.int32, (128, 128), 0) <= lax.broadcasted_iota(jnp.int32, (128, 128), 1)
    upto = jnp.where(upto, 1.0, 0.0).astype(jnp.bfloat16)
    within = jnp.dot(flags.astype(jnp.bfloat16), upto, preferred_element_type=jnp.float32)
    offset = jnp.dot(flags.astype(jnp.bfloat16), jnp.ones((128, 128), jnp.bfloat16), preferred_element_type=jnp.float32)
    offset = jnp.where(row >= 1, pltpu.roll(offset, 1, 0), 0.0)
    for shift in (1, 2, 4):
        offset = offset + jnp.where(row >= shift, pltpu.roll(offset, shift, 0), 0.0)
    place = jnp.where(flags > 0.0, within + offset - 1.0, -1.0)
    index = lax.broadcasted_iota(jnp.int32, (capacity, 128), 0).astype(jnp.float32)
    for q in range(8):
        hit = index == place[q : q + 1]
        chosen[:, 128 * q : 128 * (q + 1)] = jnp.where(hit, 1.0, 0.0).astype(jnp.bfloat16)

    for_each(lambda m: m.wait_recv(), [0], -1)

    def line(e, begin, size=TILE):
        some = pl.ds(begin, size)
        if EDGE <= e < EDGE + TILE:
            return field[e - EDGE, some, :]
        return halo[e if e < EDGE else e - TILE, some, :]

    def joined(x):
        return jnp.where(in_slot == 1, roll_lanes(x, -10), x)

    def beside(x, join, k):
        moved = roll_lanes(join, 126 - SLOT * k)
        return jnp.where(east_end, moved, roll_lanes(x, -1)), jnp.where(west_end, moved, roll_lanes(x, 1))

    exists = lambda ok: jnp.where(ok, 1.0, 0.0)
    from_west, from_east = in_slot < EDGE, jnp.logical_and(in_slot >= 11, in_slot < 14)
    in_cols = jnp.where(from_west, exists(c > 0), jnp.where(from_east, exists(c < cols - 1), 1.0))
    outer = {e: exists(r > 0) for e in range(EDGE)} | {e: exists(r < rows - 1) for e in range(EDGE + TILE, 2 * EDGE + TILE)}
    last = TILE + 2 * EDGE - 1

    def replicate(x):
        x = jnp.where(slot == tiles, x, 0.0)
        return sum((roll_lanes(x, SLOT * i) for i in range(1, 128 // SLOT)), x)

    faces, join = {}, {}
    for e in range(1, last):
        v, i = divmod(e + 1, SUB)
        west, east, near_ = roll_lanes(side_w[v], -SUB * i), roll_lanes(side_e[v], 11 - SUB * i), roll_lanes(side_e[v], 1 - SUB * i)
        own = line(e, packed)
        own = jnp.where(in_slot < TILE, own, roll_lanes(own, TILE))
        faces[e] = jnp.where(from_west, west, jnp.where(from_east, east, own))
        join[e] = jnp.where(in_slot == 1, near_, west)
        joins[e] = join[e]
    coefs = {e: replicate(x) for e, x in faces.items()}

    def face_between(lower, upper):
        x = 0.5 * (lower + upper)
        return upwind(spread_row(x, 0), spread_row(x, 2))

    low = None
    near = line(0, coef)
    for e in range(1, last):
        here, after = line(e, coef), line(e + 1, coef)
        if low is None:
            low = face_between(near, here)
        high = face_between(here, after)
        east, west = beside(here, join[e], tiles)
        weights = step_weights(0.5 * (here + east), 0.5 * (here + west), high, low, outer.get(e))
        for i in range(5):
            tile_w[5 * e + i] = weights[i]
        low = high
    low = None
    for e in range(2, last - 1):
        here = coefs[e]
        if low is None:
            low = face_between(coefs[e - 1], here)
        high = face_between(here, coefs[e + 1])
        east, west = roll_lanes(here, -1), roll_lanes(here, 1)
        mask = in_cols * outer[e] if e in outer else in_cols
        weights = step_weights(0.5 * (here + east), 0.5 * (here + west), high, low, mask)
        for i in range(5):
            face_w[5 * e + i] = weights[i]
        low = high
    for step in range(1, TRANSPORT_STEPS):
        new = {}
        for e in range(1 + step, last - step):
            w = [face_w[5 * e + i] for i in range(5)]
            x = faces[e]
            new[e] = apply_step(w, x, roll_lanes(x, -1), roll_lanes(x, 1), faces[e + 1], faces[e - 1])
            joins[(last + 1) * step + e] = joined(new[e])
        faces = new

    for_each(lambda m: m.wait_recv(), [1], -1)

    adv[:, pl.ds(coef, TILE), :] = jnp.broadcast_to(jnp.where(row < 2, 1.0, 0.0)[None], (TILE, TILE, 128))
    for step in range(TRANSPORT_STEPS):
        take = line if step == 0 else lambda e, begin, held=middle.at[step - 1]: held[e, pl.ds(begin, TILE), :]
        for e in range(1 + step, last - step):
            w = [tile_w[5 * e + i] for i in range(5)]
            join = joins[(last + 1) * step + e]
            for k in range(tiles):
                some = pl.ds(TILE * k, TILE)
                x = take(e, TILE * k)
                east, west = beside(x, join, k)
                x = apply_step(w, x, east, west, take(e + 1, TILE * k), take(e - 1, TILE * k))
                if step < TRANSPORT_STEPS - 1:
                    middle[step, e, some, :] = x
                    continue
                q = e - EDGE
                if k == tiles - 1:
                    heat = jnp.broadcast_to(heat_v[pl.ds(q, 1), :], (TILE, 128))
                    n = species - TILE * k
                    x = jnp.where(row < n, x, jnp.where(row == n, heat, 1.0))
                adv[q, some, :] = x

    for_each(lambda m: m.wait_send(), everything, 1)


def chemistry_kernel(
    species, adv, chosen, w1_p, w2_p, w13_p, w3_p, b13_p, b2_ref, b3_p, out_hbm,
    pre, sums, out_v, sem,
):
    capacity, cells = chosen.shape
    hidden = w2_p.shape[0]
    chunk = capacity // CHUNKS
    tail = 2 * hidden - capacity
    f32, bf16 = jnp.float32, jnp.bfloat16
    rows = lambda i: pl.ds(chunk * i, chunk)
    by_species = out_v.reshape(WIDTH * TILE, 128)

    def features(p):
        x = jnp.concatenate([adv[2 * p + j] for j in range(2)], axis=1)
        high = x.astype(bf16)
        low = (x - high.astype(f32)).astype(bf16)
        return jnp.concatenate([high, low, jnp.zeros((hidden - 2 * WIDTH, 2 * 128), bf16)], axis=0)

    def cell_tile(x, tile):
        if tile == 0:
            return x[:hidden]
        return jnp.concatenate([x[hidden:], jnp.zeros((tail, x.shape[1]), x.dtype)], axis=0)

    def body(*acc):
        acc0, acc1 = acc[:CHUNKS], acc[CHUNKS : 2 * CHUNKS]
        totals, parts = acc[2 * CHUNKS : 2 * CHUNKS + 2], acc[2 * CHUNKS + 2 :]
        for j in range(2):
            for m in range(2):
                pltpu.matmul_push_rhs(features(2 * m + j), j, m, transpose=True)
        for j in range(2):
            for i in range(CHUNKS):
                for m, accs in enumerate((acc0, acc1)):
                    p = 2 * m + j
                    pltpu.matmul_acc_lhs(accs[i], chosen[rows(i), pl.ds(256 * p, 256)], load_staged_rhs=None if i else j)
        pltpu.matmul_push_rhs(w1_p[...], 0, 1)
        pltpu.matmul_push_rhs(w2_p[...], 0, 0)
        pltpu.matmul_push_rhs(w13_p[...], 1, 1)
        for i in range(CHUNKS):
            x = (pltpu.matmul_pop(acc0[i]) + pltpu.matmul_pop(acc1[i])).astype(bf16)
            pltpu.matmul_acc_lhs(acc1[i], x, load_staged_rhs=None if i else 0)
        last = []
        for step in range(SUBSTEPS):
            for i in range(CHUNKS):
                x = pltpu.matmul_pop(acc1[i])
                if step:
                    x = x + pre[rows(i), :]
                if step < SUBSTEPS - 1:
                    pre[rows(i), :] = x + b13_p[...]
                pltpu.matmul_acc_lhs(acc0[i], jnp.tanh(x).astype(bf16), load_staged_rhs=None if step or i else 0)
            if step == SUBSTEPS - 1:
                x = sums[...]
                high = x.astype(bf16)
                low = (x - high.astype(f32)).astype(bf16)
                for tile in range(2):
                    for j, x in enumerate((high, low)):
                        pltpu.matmul_push_rhs(cell_tile(x, tile), j, 1, transpose=True)
                        pltpu.matmul_acc_lhs(totals[tile], w3_p[...], load_staged_rhs=j)
            for i in range(CHUNKS):
                h = jnp.tanh(pltpu.matmul_pop(acc0[i]) + b2_ref[...]).astype(bf16)
                if step == SUBSTEPS - 1:
                    last.append(h)
                    continue
                pltpu.matmul_acc_lhs(acc1[i], h, load_staged_rhs=None if step or i else 1)
                h = h.astype(f32)
                sums[rows(i), :] = h if step == 0 else sums[rows(i), :] + h
        h = jnp.concatenate(last, axis=0)
        for tile in range(2):
            pltpu.matmul_push_rhs(cell_tile(h, tile), tile, 1, transpose=True)
        for tile in range(2):
            pltpu.matmul_acc_lhs(totals[tile], w3_p[...], load_staged_rhs=tile)

        def place(m, j, tile):
            flags = chosen[:, pl.ds(256 * (2 * m + j), 256)]
            pltpu.matmul_push_rhs(cell_tile(flags, tile), tile, m)

        for tile in range(2):
            for m in range(2):
                place(m, 0, tile)
        terms = []
        for tile in range(2):
            x = pltpu.matmul_pop(totals[tile]) + jnp.concatenate([b3_p[...]] * 2, axis=1)
            high = x.astype(bf16)
            terms.append((high, (x - high.astype(f32)).astype(bf16)))
        for j in range(2):
            for tile in range(2):
                for m in range(2):
                    pltpu.matmul_acc_lhs(parts[2 * m + j], terms[tile][0], load_staged_rhs=tile)
                    pltpu.matmul_acc_lhs(parts[2 * m + j], terms[tile][1])
                    if j == 0:
                        place(m, 1, tile)
        for j in range(2):
            for m in range(2):
                x = pltpu.matmul_pop(parts[2 * m + j])
                for k in range(2):
                    q = 2 * (2 * m + j) + k
                    y = adv[q] + x[:, 128 * k : 128 * (k + 1)]
                    for t in range(WIDTH // TILE):
                        by_species[pl.ds(TILE * TILE * t + q, TILE, stride=TILE), :] = y[TILE * t : TILE * (t + 1)]

    accs = [pltpu.ACC(m)((chunk, hidden), f32) for m in (0, 1) for _ in range(CHUNKS)]
    accs += [pltpu.ACC(1)((WIDTH, hidden), f32) for _ in range(2)]
    accs += [pltpu.ACC(m)((WIDTH, hidden), f32) for m in (0, 1) for _ in range(2)]
    pl.run_scoped(body, *accs)
    copy = pltpu.make_async_copy(out_v.at[pl.ds(0, species)], out_hbm, sem)
    copy.start()
    copy.wait()


def shards(rows, cols, mix, diff, speed, heat, active, w1, b1, w2, b2, w3, b3):
    species, height, width = mix.shape
    tiles = pl.cdiv(species, TILE)
    lines = height + 2 * EDGE
    hidden, features = w1.shape
    vm = pltpu.VMEM
    f32, bf16 = jnp.float32, jnp.bfloat16
    held = lambda x: pltpu.with_memory_space_constraint(x, pltpu.HBM)
    capacity = 3 * (height * width // 8)
    middle = [
        ((height, WIDTH, width), f32),
        ((capacity, height * width), bf16),
        ((hidden, hidden), bf16),
        ((hidden, hidden), bf16),
        ((hidden, hidden), bf16),
        ((WIDTH, hidden), bf16),
        ((1, hidden), f32),
        ((1, hidden), f32),
        ((WIDTH, 128), f32),
    ]
    made = pl.pallas_call(
        functools.partial(transport_kernel, rows, cols, species),
        out_shape=[jax.ShapeDtypeStruct(*x) for x in middle],
        in_specs=[pl.BlockSpec(memory_space=pltpu.HBM)] * 11,
        out_specs=[pl.BlockSpec(memory_space=vm)] * len(middle),
        scratch_shapes=[
            vm((1, hidden), f32),
            vm((1, species), f32),
            vm((TILE * (tiles + 1), height, width), f32),
            vm((height, TILE * (tiles + 2), width), f32),
            vm((2 * EDGE, TILE * (tiles + 2), width), f32),
            vm((SUB, TILE, width), f32),
            vm((SUB, TILE, width), f32),
            vm((height // SUB, TILE, width), f32),
            vm((height // SUB, TILE, width), f32),
            vm((5 * lines, TILE, width), f32),
            vm((5 * lines, TILE, width), f32),
            vm((TRANSPORT_STEPS * lines, TILE, width), f32),
            vm((TRANSPORT_STEPS - 1, lines, TILE * tiles, width), f32),
            vm((height, width), f32),
            vm((height, width), jnp.int32),
            vm((features, hidden), bf16),
            vm(w2.shape, bf16),
            vm(w3.shape, bf16),
            pltpu.SemaphoreType.DMA((11,)),
            pltpu.SemaphoreType.DMA((len(DIRECTIONS) + 2,)),
            pltpu.SemaphoreType.DMA((len(DIRECTIONS) + 2,)),
            pltpu.SemaphoreType.REGULAR((len(ABOVE),)),
        ],
        compiler_params=pltpu.CompilerParams(collective_id=0, has_side_effects=True, vmem_limit_bytes=16 << 20),
    )(*(held(x) for x in (mix, diff, speed, heat, active, w1.T, w2, w3, b1[None], b2[None], b3[None])))
    return pl.pallas_call(
        functools.partial(chemistry_kernel, species),
        out_shape=jax.ShapeDtypeStruct(mix.shape, mix.dtype),
        in_specs=[pl.BlockSpec(memory_space=vm)] * len(middle),
        out_specs=pl.BlockSpec(memory_space=pltpu.HBM),
        scratch_shapes=[
            vm((capacity, hidden), f32),
            vm((capacity, hidden), f32),
            vm((WIDTH, height, width), f32),
            pltpu.SemaphoreType.DMA,
        ],
        compiler_params=pltpu.CompilerParams(vmem_limit_bytes=16 << 20),
    )(*made)


def solution(mesh):
    tile = P(None, "row", "col")
    plane = P("row", "col")
    mapped = jax.shard_map(
        functools.partial(shards, mesh.shape["row"], mesh.shape["col"]),
        mesh=mesh,
        in_specs=(tile, plane, tile, plane, plane, P(), P(), P(), P(), P(), P()),
        out_specs=tile,
        check_vma=False,
    )

    def run(*args):
        with jax.sharding.use_abstract_mesh(mesh.abstract_mesh):
            return mapped(*args)

    return run
```

```python
import functools

import jax
import jax.numpy as jnp
from jax import lax
from jax.experimental import pallas as pl
from jax.experimental.pallas import tpu as pltpu
from jax.sharding import PartitionSpec as P

SUBSTEPS = 8
TRANSPORT_STEPS = 3
CHEM_STEP = 0.0625
TILE = 8
SLOT = 16
EDGE = 3
SUB = 4
CHUNKS = 4
WIDTH = 64
MESH_ID = pl.DeviceIdType.MESH
DIRECTIONS = tuple((dr, dc) for dr in (-1, 0, 1) for dc in (-1, 0, 1) if (dr, dc) != (0, 0))
ABOVE = ((0, 1), (1, 0), (1, 1))
BELOW = tuple((-dr, -dc) for dr, dc in ABOVE)
CORNERS = ((-1, 1), (1, -1))

def roll_lanes(x, shift):
    return pltpu.roll(x, shift % x.shape[-1], x.ndim - 1)


def upwind(d, v):
    return d - jnp.minimum(v, 0.0), d + jnp.maximum(v, 0.0)


def spread_row(x, i):
    return jnp.broadcast_to(x[i : i + 1], x.shape)


def step_weights(east, west, high, low, mask):
    (e, e_out), (w_out, w) = upwind(*(spread_row(east, i) for i in (0, 1))), upwind(*(spread_row(west, i) for i in (0, 1)))
    (h, h_out), (l_out, l) = high, low
    weights = (1.0 - e_out - w_out - h_out - l_out, e, w, h, l)
    return weights if mask is None else tuple(x * mask for x in weights)


def apply_step(w, own, east, west, high, low):
    return w[0] * own + w[1] * east + w[2] * west + w[3] * high + w[4] * low


def transport_kernel(
    rows, cols, species,
    mix_hbm, diff_hbm, speed_hbm, heat_hbm, active_hbm, w1_hbm, w2_hbm, w3_hbm,
    b1_hbm, b2_hbm, b3_hbm,
    adv, chosen, w1_p, w2_p, w13_p, w3_p, b13_p, b2_ref, b3_p,
    b1_ref, b3_ref,
    stage, field, halo, side_w, side_e, to_east, to_west, tile_w, face_w, joins, middle, shifts, beside_v, heat_v, active_v, w1_v, w2_v, w3_v,
    local_sem, send_sem, recv_sem, ready_sem, corner_sem,
):
    r, c = lax.axis_index("row"), lax.axis_index("col")
    tiles = pl.cdiv(species, TILE)
    coef = tiles * TILE
    packed = coef + TILE

    loads = [
        pltpu.make_async_copy(mix_hbm, stage.at[pl.ds(0, species)], local_sem.at[0]),
        pltpu.make_async_copy(diff_hbm, stage.at[coef], local_sem.at[1]),
        pltpu.make_async_copy(speed_hbm, stage.at[pl.ds(coef + 1, 2)], local_sem.at[2]),
        pltpu.make_async_copy(heat_hbm, heat_v, local_sem.at[3]),
        pltpu.make_async_copy(active_hbm, active_v, local_sem.at[4]),
        pltpu.make_async_copy(w1_hbm, w1_v, local_sem.at[5]),
        pltpu.make_async_copy(w2_hbm, w2_v, local_sem.at[6]),
        pltpu.make_async_copy(w3_hbm, w3_v, local_sem.at[7]),
        pltpu.make_async_copy(b1_hbm, b1_ref, local_sem.at[8]),
        pltpu.make_async_copy(b2_hbm, b2_ref, local_sem.at[9]),
        pltpu.make_async_copy(b3_hbm, b3_ref, local_sem.at[10]),
    ]
    for load in loads:
        load.start()
    halo[...] = jnp.zeros_like(halo)
    side_w[...] = jnp.zeros_like(side_w)
    side_e[...] = jnp.zeros_like(side_e)

    def there(dr, dc):
        ok = jnp.bool_(True)
        if dr:
            ok = jnp.logical_and(ok, r + dr < rows if dr > 0 else r + dr >= 0)
        if dc:
            ok = jnp.logical_and(ok, c + dc < cols if dc > 0 else c + dc >= 0)
        return ok

    barrier = pltpu.get_barrier_semaphore()
    for dr, dc in ABOVE:
        @pl.when(there(dr, dc))
        def _(dr=dr, dc=dc):
            pl.semaphore_signal(barrier, inc=1, device_id=(r + dr, c + dc), device_id_type=MESH_ID)

    one = lambda ok: jnp.where(ok, 1, 0)
    below = sum(one(there(dr, dc)) for dr, dc in BELOW)

    @pl.when(below > 0)
    def _():
        pl.semaphore_wait(barrier, below)

    for n, (dr, dc) in enumerate(BELOW):
        @pl.when(there(dr, dc))
        def _(n=n, dr=dr, dc=dc):
            pl.semaphore_signal(ready_sem.at[n], inc=1, device_id=(r + dr, c + dc), device_id_type=MESH_ID)

    @pl.when(there(-1, -1))
    def _():
        for n, way in enumerate(((0, -1), (-1, 0))):
            pl.semaphore_signal(corner_sem.at[n], inc=1, device_id=(r + way[0], c + way[1]), device_id_type=MESH_ID)

    for s in [*range(species, coef), *range(coef + 3, coef + TILE)]:
        stage[s] = jnp.zeros(stage.shape[1:], jnp.float32)
    lane = lax.broadcasted_iota(jnp.int32, (TILE, 128), 1)
    row = lax.broadcasted_iota(jnp.int32, (TILE, 128), 0)
    west_end, east_end = lane == 0, lane == 127
    in_slot = lane % SLOT
    slot = lane // SLOT
    for load in loads[:3]:
        load.wait()
    by_row = stage.reshape(stage.shape[0] * TILE, 128)
    def packing(parts):
        pack = None
        for k, x in enumerate(parts):
            x = roll_lanes(x, SLOT * k + EDGE)
            pack = x if pack is None else jnp.where(slot == k, x, pack)
        return pack

    packs = []
    for q in range(TILE):
        parts = []
        for k in range(tiles + 1):
            parts.append(by_row[pl.ds(TILE * TILE * k + q, TILE, stride=TILE), :])
            field[q, pl.ds(TILE * k, TILE), :] = parts[-1]
        packs.append(packing(parts))
        field[q, pl.ds(packed, TILE), :] = packs[-1]
    for v in range(TILE // SUB):
        for to, shift in ((to_east, 0), (to_west, -EDGE)):
            x = None
            for i in range(SUB):
                part = roll_lanes(packs[SUB * v + i], SUB * i + shift)
                x = part if x is None else jnp.where(in_slot // SUB == i, part, x)
            to[v] = x

    pieces = [(coef, 2 * TILE), (0, coef)]

    def message(index, piece=0):
        dr, dc = DIRECTIONS[index]
        number = index if piece == 0 else len(DIRECTIONS) + (dr + 1) // 2
        rows_from = {1: pl.ds(TILE - EDGE, EDGE), -1: pl.ds(0, EDGE), 0: pl.ds(0, TILE)}[dr]
        if dc == 0:
            some = pl.ds(*pieces[piece])
            src, dst = field.at[rows_from, some], halo.at[pl.ds(0 if dr > 0 else EDGE, EDGE), some]
        else:
            target = side_w if dc > 0 else side_e
            made = to_east if dc > 0 else to_west
            some, there_ = {1: (pl.ds(1, 1), pl.ds(0, 1)), -1: (pl.ds(0, 1), pl.ds(3, 1)), 0: (pl.ds(0, 2), pl.ds(1, 2))}[dr]
            src, dst = made.at[some], target.at[there_]
        return pltpu.make_async_remote_copy(
            src_ref=src, dst_ref=dst, send_sem=send_sem.at[number], recv_sem=recv_sem.at[number],
            device_id=(r + dr, c + dc), device_id_type=MESH_ID,
        )

    def for_each(action, numbers, sign):
        for number in numbers:
            for index, (dr, dc) in enumerate(DIRECTIONS):
                if number and dc:
                    continue

                @pl.when(there(sign * dr, sign * dc))
                def _(index=index, number=number):
                    action(message(index, number))

    everything = range(len(pieces))
    def send(dr, dc):
        @pl.when(there(dr, dc))
        def _():
            if (dr, dc) in ABOVE:
                pl.semaphore_wait(ready_sem.at[ABOVE.index((dr, dc))], 1)
            elif (dr, dc) in CORNERS:
                pl.semaphore_wait(corner_sem.at[CORNERS.index((dr, dc))], 1)
            for number in everything if dc == 0 else [0]:
                message(DIRECTIONS.index((dr, dc)), number).start()

    for way in ((-1, -1), (0, -1), (-1, 0), (0, 1), (-1, 1), (1, 0), (1, -1), (1, 1)):
        send(*way)

    for load in loads[3:]:
        load.wait()
    w1_p[...] = jnp.zeros_like(w1_p)
    w1_p[pl.ds(0, species + 1), :] = w1_v[...]
    w1_p[pl.ds(WIDTH, species), :] = w1_v[pl.ds(0, species), :]
    rest = b1_ref[...]
    for i in range(3):
        term = rest.astype(jnp.bfloat16)
        w1_p[pl.ds(species + 1 + i, 1), :] = term
        rest = rest - term.astype(jnp.float32)
    w2_p[...] = jnp.transpose(w2_v[...].astype(jnp.float32)).astype(jnp.bfloat16)
    w3_p[...] = jnp.zeros_like(w3_p)
    w3_p[pl.ds(0, species), :] = (CHEM_STEP * w3_v[...].astype(jnp.float32)).astype(jnp.bfloat16)
    w13_p[...] = lax.dot_general(
        w3_p[pl.ds(0, species), :], w1_v[pl.ds(0, species), :], (((0,), (0,)), ((), ())),
        preferred_element_type=jnp.float32,
    ).astype(jnp.bfloat16)
    b3_row = jnp.concatenate([CHEM_STEP * b3_ref[...], jnp.zeros((1, 128 - species), jnp.float32)], axis=1)
    rest, terms = b3_row, []
    for _ in range(3):
        terms.append(rest.astype(jnp.bfloat16).astype(jnp.float32))
        rest = rest - terms[-1]
    terms = jnp.concatenate(terms + [jnp.zeros((5, 128), jnp.float32)], axis=0).astype(jnp.bfloat16)
    b13_p[...] = jnp.sum(jnp.dot(terms[:, :species], w1_v[pl.ds(0, species), :], preferred_element_type=jnp.float32), axis=0, keepdims=True)
    b3_p[...] = SUBSTEPS * jnp.transpose(jnp.broadcast_to(b3_row, (128, 128)))[:WIDTH]

    capacity = chosen.shape[0]
    flags = jnp.where(active_v[...] == 1, 1.0, 0.0)
    upto = lax.broadcasted_iota(jnp.int32, (128, 128), 0) <= lax.broadcasted_iota(jnp.int32, (128, 128), 1)
    upto = jnp.where(upto, 1.0, 0.0).astype(jnp.bfloat16)
    within = jnp.dot(flags.astype(jnp.bfloat16), upto, preferred_element_type=jnp.float32)
    offset = jnp.dot(flags.astype(jnp.bfloat16), jnp.ones((128, 128), jnp.bfloat16), preferred_element_type=jnp.float32)
    offset = jnp.where(row >= 1, pltpu.roll(offset, 1, 0), 0.0)
    for shift in (1, 2, 4):
        offset = offset + jnp.where(row >= shift, pltpu.roll(offset, shift, 0), 0.0)
    place = jnp.where(flags > 0.0, within + offset - 1.0, -1.0)
    index = lax.broadcasted_iota(jnp.int32, (capacity, 128), 0).astype(jnp.float32)
    for q in range(8):
        hit = index == place[q : q + 1]
        chosen[:, 128 * q : 128 * (q + 1)] = jnp.where(hit, 1.0, 0.0).astype(jnp.bfloat16)

    inward = lax.broadcasted_iota(jnp.int32, (2 * 128, 2 * 128), 0) % 128
    outward = lax.broadcasted_iota(jnp.int32, (2 * 128, 2 * 128), 1)
    outward = jnp.where(outward < 128, outward + 1, outward - 129)
    shifts[...] = jnp.where(inward == outward, 1.0, 0.0).astype(jnp.bfloat16)

    def shift(step, e, x):
        high = x.astype(jnp.bfloat16)
        low = (x - high.astype(jnp.float32)).astype(jnp.bfloat16)
        x = jnp.dot(jnp.concatenate([high, low], axis=1), shifts[...], preferred_element_type=jnp.float32)
        beside_v[step, pl.ds(e, x.shape[0] // coef)] = x.reshape(-1, coef, 2 * 128)

    def lines_of(ref, begin, count):
        return jnp.concatenate([ref[begin + i, pl.ds(0, coef), :] for i in range(count)], axis=0)

    for half in range(2):
        shift(0, EDGE + TILE // 2 * half, lines_of(field, TILE // 2 * half, TILE // 2))

    for_each(lambda m: m.wait_recv(), [0], -1)

    def line(e, begin, size=TILE):
        some = pl.ds(begin, size)
        if EDGE <= e < EDGE + TILE:
            return field[e - EDGE, some, :]
        return halo[e if e < EDGE else e - TILE, some, :]

    def joined(x):
        return jnp.where(in_slot == 1, roll_lanes(x, -10), x)

    def beside(x, join, k):
        moved = roll_lanes(join, 126 - SLOT * k)
        return jnp.where(east_end, moved, roll_lanes(x, -1)), jnp.where(west_end, moved, roll_lanes(x, 1))

    exists = lambda ok: jnp.where(ok, 1.0, 0.0)
    from_west, from_east = in_slot < EDGE, jnp.logical_and(in_slot >= 11, in_slot < 14)
    in_cols = jnp.where(from_west, exists(c > 0), jnp.where(from_east, exists(c < cols - 1), 1.0))
    outer = {e: exists(r > 0) for e in range(EDGE)} | {e: exists(r < rows - 1) for e in range(EDGE + TILE, 2 * EDGE + TILE)}
    last = TILE + 2 * EDGE - 1

    def replicate(x):
        x = jnp.where(slot == tiles, x, 0.0)
        for step in (16, 32, 64):
            x = x + roll_lanes(x, step)
        return x

    faces, join = {}, {}
    for e in range(1, last):
        v, i = divmod(e + 1, SUB)
        west, east, near_ = roll_lanes(side_w[v], -SUB * i), roll_lanes(side_e[v], 11 - SUB * i), roll_lanes(side_e[v], 1 - SUB * i)
        own = line(e, packed)
        own = jnp.where(in_slot < TILE, own, roll_lanes(own, TILE))
        faces[e] = jnp.where(from_west, west, jnp.where(from_east, east, own))
        join[e] = jnp.where(in_slot == 1, near_, west)
        joins[e] = join[e]
    coefs = {e: replicate(x) for e, x in faces.items()}

    def face_between(lower, upper):
        x = 0.5 * (lower + upper)
        return upwind(spread_row(x, 0), spread_row(x, 2))

    low = None
    near = line(0, coef)
    for e in range(1, last):
        here, after = line(e, coef), line(e + 1, coef)
        if low is None:
            low = face_between(near, here)
        high = face_between(here, after)
        east, west = beside(here, join[e], tiles)
        weights = step_weights(0.5 * (here + east), 0.5 * (here + west), high, low, outer.get(e))
        for i in range(5):
            tile_w[5 * e + i] = weights[i]
        low = high
    low = None
    for e in range(2, last - 1):
        here = coefs[e]
        if low is None:
            low = face_between(coefs[e - 1], here)
        high = face_between(here, coefs[e + 1])
        east, west = roll_lanes(here, -1), roll_lanes(here, 1)
        mask = in_cols * outer[e] if e in outer else in_cols
        weights = step_weights(0.5 * (here + east), 0.5 * (here + west), high, low, mask)
        for i in range(5):
            face_w[5 * e + i] = weights[i]
        low = high
    for step in range(1, TRANSPORT_STEPS):
        new = {}
        for e in range(1 + step, last - step):
            w = [face_w[5 * e + i] for i in range(5)]
            x = faces[e]
            new[e] = apply_step(w, x, roll_lanes(x, -1), roll_lanes(x, 1), faces[e + 1], faces[e - 1])
            joins[(last + 1) * step + e] = joined(new[e])
        faces = new

    for_each(lambda m: m.wait_recv(), [1], -1)

    shift(0, 1, lines_of(halo, 1, EDGE - 1))
    shift(0, EDGE + TILE, lines_of(halo, EDGE, EDGE - 1))
    adv[:, pl.ds(coef, TILE), :] = jnp.broadcast_to(jnp.where(row < 2, 1.0, 0.0)[None], (TILE, TILE, 128))
    for step in range(TRANSPORT_STEPS):
        take = line if step == 0 else lambda e, begin, held=middle.at[step - 1]: held[e, pl.ds(begin, TILE), :]
        if step:
            begin, count = 1 + step, last - 1 - 2 * step
            first_half = count // 4 * 2 + count % 4
            for e, n in ((begin, first_half), (begin + first_half, count - first_half)):
                shift(step, e, lines_of(middle.at[step - 1], e, n))
        for e in range(1 + step, last - step):
            w = [tile_w[5 * e + i] for i in range(5)]
            join = joins[(last + 1) * step + e]
            for k in range(tiles):
                some = pl.ds(TILE * k, TILE)
                x = take(e, TILE * k)
                moved = roll_lanes(join, 126 - SLOT * k)
                east = jnp.where(east_end, moved, beside_v[step, e, some, pl.ds(0, 128)])
                west = jnp.where(west_end, moved, beside_v[step, e, some, pl.ds(128, 128)])
                x = apply_step(w, x, east, west, take(e + 1, TILE * k), take(e - 1, TILE * k))
                if step < TRANSPORT_STEPS - 1:
                    middle[step, e, some, :] = x
                    continue
                q = e - EDGE
                if k == tiles - 1:
                    heat = jnp.broadcast_to(heat_v[pl.ds(q, 1), :], (TILE, 128))
                    n = species - TILE * k
                    x = jnp.where(row < n, x, jnp.where(row == n, heat, 1.0))
                adv[q, some, :] = x

    for_each(lambda m: m.wait_send(), everything, 1)


def chemistry_kernel(
    species, adv, chosen, w1_p, w2_p, w13_p, w3_p, b13_p, b2_ref, b3_p, out_hbm,
    pre, sums, out_v, sem,
):
    capacity, cells = chosen.shape
    hidden = w2_p.shape[0]
    chunk = capacity // CHUNKS
    tail = 2 * hidden - capacity
    f32, bf16 = jnp.float32, jnp.bfloat16
    rows = lambda i: pl.ds(chunk * i, chunk)
    by_species = out_v.reshape(WIDTH * TILE, 128)

    def features(p):
        x = jnp.concatenate([adv[2 * p + j] for j in range(2)], axis=1)
        high = x.astype(bf16)
        low = (x - high.astype(f32)).astype(bf16)
        return jnp.concatenate([high, low, jnp.zeros((hidden - 2 * WIDTH, 2 * 128), bf16)], axis=0)

    def cell_tile(x, tile):
        if tile == 0:
            return x[:hidden]
        return jnp.concatenate([x[hidden:], jnp.zeros((tail, x.shape[1]), x.dtype)], axis=0)

    def body(*acc):
        acc0, acc1 = acc[:CHUNKS], acc[CHUNKS : 2 * CHUNKS]
        totals, parts = acc[2 * CHUNKS : 2 * CHUNKS + 2], acc[2 * CHUNKS + 2 :]
        for j in range(2):
            for m in range(2):
                pltpu.matmul_push_rhs(features(2 * m + j), j, m, transpose=True)
        for j in range(2):
            for i in range(CHUNKS):
                for m, accs in enumerate((acc0, acc1)):
                    p = 2 * m + j
                    pltpu.matmul_acc_lhs(accs[i], chosen[rows(i), pl.ds(256 * p, 256)], load_staged_rhs=None if i else j)
        pltpu.matmul_push_rhs(w1_p[...], 0, 1)
        pltpu.matmul_push_rhs(w2_p[...], 0, 0)
        pltpu.matmul_push_rhs(w13_p[...], 1, 1)
        for i in range(CHUNKS):
            x = (pltpu.matmul_pop(acc0[i]) + pltpu.matmul_pop(acc1[i])).astype(bf16)
            pltpu.matmul_acc_lhs(acc1[i], x, load_staged_rhs=None if i else 0)
        last = []
        for step in range(SUBSTEPS):
            for i in range(CHUNKS):
                x = pltpu.matmul_pop(acc1[i])
                if step:
                    x = x + pre[rows(i), :]
                if step < SUBSTEPS - 1:
                    pre[rows(i), :] = x + b13_p[...]
                pltpu.matmul_acc_lhs(acc0[i], jnp.tanh(x).astype(bf16), load_staged_rhs=None if step or i else 0)
            if step == SUBSTEPS - 1:
                x = sums[...]
                high = x.astype(bf16)
                low = (x - high.astype(f32)).astype(bf16)
                for tile in range(2):
                    for j, x in enumerate((high, low)):
                        pltpu.matmul_push_rhs(cell_tile(x, tile), j, 1, transpose=True)
                        pltpu.matmul_acc_lhs(totals[tile], w3_p[...], load_staged_rhs=j)
            for i in range(CHUNKS):
                h = jnp.tanh(pltpu.matmul_pop(acc0[i]) + b2_ref[...]).astype(bf16)
                if step == SUBSTEPS - 1:
                    last.append(h)
                    continue
                pltpu.matmul_acc_lhs(acc1[i], h, load_staged_rhs=None if step or i else 1)
                h = h.astype(f32)
                sums[rows(i), :] = h if step == 0 else sums[rows(i), :] + h
        h = jnp.concatenate(last, axis=0)
        for tile in range(2):
            pltpu.matmul_push_rhs(cell_tile(h, tile), tile, 1, transpose=True)
        for tile in range(2):
            pltpu.matmul_acc_lhs(totals[tile], w3_p[...], load_staged_rhs=tile)

        def place(m, j, tile):
            flags = chosen[:, pl.ds(256 * (2 * m + j), 256)]
            pltpu.matmul_push_rhs(cell_tile(flags, tile), tile, m)

        for tile in range(2):
            for m in range(2):
                place(m, 0, tile)
        terms = []
        for tile in range(2):
            x = pltpu.matmul_pop(totals[tile]) + jnp.concatenate([b3_p[...]] * 2, axis=1)
            high = x.astype(bf16)
            terms.append((high, (x - high.astype(f32)).astype(bf16)))
        for j in range(2):
            for tile in range(2):
                for m in range(2):
                    pltpu.matmul_acc_lhs(parts[2 * m + j], terms[tile][0], load_staged_rhs=tile)
                    pltpu.matmul_acc_lhs(parts[2 * m + j], terms[tile][1])
                    if j == 0:
                        place(m, 1, tile)
        for j in range(2):
            for m in range(2):
                x = pltpu.matmul_pop(parts[2 * m + j])
                for k in range(2):
                    q = 2 * (2 * m + j) + k
                    y = adv[q] + x[:, 128 * k : 128 * (k + 1)]
                    for t in range(WIDTH // TILE):
                        by_species[pl.ds(TILE * TILE * t + q, TILE, stride=TILE), :] = y[TILE * t : TILE * (t + 1)]

    accs = [pltpu.ACC(m)((chunk, hidden), f32) for m in (0, 1) for _ in range(CHUNKS)]
    accs += [pltpu.ACC(1)((WIDTH, hidden), f32) for _ in range(2)]
    accs += [pltpu.ACC(m)((WIDTH, hidden), f32) for m in (0, 1) for _ in range(2)]
    pl.run_scoped(body, *accs)
    copy = pltpu.make_async_copy(out_v.at[pl.ds(0, species)], out_hbm, sem)
    copy.start()
    copy.wait()


def shards(rows, cols, mix, diff, speed, heat, active, w1, b1, w2, b2, w3, b3):
    species, height, width = mix.shape
    tiles = pl.cdiv(species, TILE)
    lines = height + 2 * EDGE
    hidden, features = w1.shape
    vm = pltpu.VMEM
    f32, bf16 = jnp.float32, jnp.bfloat16
    held = lambda x: pltpu.with_memory_space_constraint(x, pltpu.HBM)
    capacity = 3 * (height * width // 8)
    middle = [
        ((height, WIDTH, width), f32),
        ((capacity, height * width), bf16),
        ((hidden, hidden), bf16),
        ((hidden, hidden), bf16),
        ((hidden, hidden), bf16),
        ((WIDTH, hidden), bf16),
        ((1, hidden), f32),
        ((1, hidden), f32),
        ((WIDTH, 128), f32),
    ]
    made = pl.pallas_call(
        functools.partial(transport_kernel, rows, cols, species),
        out_shape=[jax.ShapeDtypeStruct(*x) for x in middle],
        in_specs=[pl.BlockSpec(memory_space=pltpu.HBM)] * 11,
        out_specs=[pl.BlockSpec(memory_space=vm)] * len(middle),
        scratch_shapes=[
            vm((1, hidden), f32),
            vm((1, species), f32),
            vm((TILE * (tiles + 1), height, width), f32),
            vm((height, TILE * (tiles + 2), width), f32),
            vm((2 * EDGE, TILE * (tiles + 2), width), f32),
            vm((SUB, TILE, width), f32),
            vm((SUB, TILE, width), f32),
            vm((height // SUB, TILE, width), f32),
            vm((height // SUB, TILE, width), f32),
            vm((5 * lines, TILE, width), f32),
            vm((5 * lines, TILE, width), f32),
            vm((TRANSPORT_STEPS * lines, TILE, width), f32),
            vm((TRANSPORT_STEPS - 1, lines, TILE * tiles, width), f32),
            vm((2 * width, 2 * width), bf16),
            vm((TRANSPORT_STEPS, lines, TILE * tiles, 2 * width), f32),
            vm((height, width), f32),
            vm((height, width), jnp.int32),
            vm((features, hidden), bf16),
            vm(w2.shape, bf16),
            vm(w3.shape, bf16),
            pltpu.SemaphoreType.DMA((11,)),
            pltpu.SemaphoreType.DMA((len(DIRECTIONS) + 2,)),
            pltpu.SemaphoreType.DMA((len(DIRECTIONS) + 2,)),
            pltpu.SemaphoreType.REGULAR((len(ABOVE),)),
            pltpu.SemaphoreType.REGULAR((len(CORNERS),)),
        ],
        compiler_params=pltpu.CompilerParams(collective_id=0, has_side_effects=True, vmem_limit_bytes=24 << 20),
    )(*(held(x) for x in (mix, diff, speed, heat, active, w1.T, w2, w3, b1[None], b2[None], b3[None])))
    return pl.pallas_call(
        functools.partial(chemistry_kernel, species),
        out_shape=jax.ShapeDtypeStruct(mix.shape, mix.dtype),
        in_specs=[pl.BlockSpec(memory_space=vm)] * len(middle),
        out_specs=pl.BlockSpec(memory_space=pltpu.HBM),
        scratch_shapes=[
            vm((capacity, hidden), f32),
            vm((capacity, hidden), f32),
            vm((WIDTH, height, width), f32),
            pltpu.SemaphoreType.DMA,
        ],
        compiler_params=pltpu.CompilerParams(vmem_limit_bytes=16 << 20),
    )(*made)


def solution(mesh):
    tile = P(None, "row", "col")
    plane = P("row", "col")
    mapped = jax.shard_map(
        functools.partial(shards, mesh.shape["row"], mesh.shape["col"]),
        mesh=mesh,
        in_specs=(tile, plane, tile, plane, plane, P(), P(), P(), P(), P(), P()),
        out_specs=tile,
        check_vma=False,
    )

    def run(*args):
        with jax.sharding.use_abstract_mesh(mesh.abstract_mesh):
            return mapped(*args)

    return run
```

```python
import functools

import jax
import jax.numpy as jnp
from jax import lax
from jax.experimental import pallas as pl
from jax.experimental.pallas import tpu as pltpu
from jax.sharding import PartitionSpec as P

SUBSTEPS = 8
TRANSPORT_STEPS = 3
CHEM_STEP = 0.0625
TILE = 8
SLOT = 16
EDGE = 3
SUB = 4
CHUNKS = 4
WIDTH = 64
MESH_ID = pl.DeviceIdType.MESH
DIRECTIONS = tuple((dr, dc) for dr in (-1, 0, 1) for dc in (-1, 0, 1) if (dr, dc) != (0, 0))
ABOVE = ((0, 1), (1, 0), (1, 1))
BELOW = tuple((-dr, -dc) for dr, dc in ABOVE)
CORNERS = ((-1, 1), (1, -1))

def roll_lanes(x, shift):
    return pltpu.roll(x, shift % x.shape[-1], x.ndim - 1)


def upwind(d, v):
    return d - jnp.minimum(v, 0.0), d + jnp.maximum(v, 0.0)


def spread_row(x, i):
    return jnp.broadcast_to(x[i : i + 1], x.shape)


def step_weights(east, west, high, low, mask):
    (e, e_out), (w_out, w) = upwind(*(spread_row(east, i) for i in (0, 1))), upwind(*(spread_row(west, i) for i in (0, 1)))
    (h, h_out), (l_out, l) = high, low
    weights = (1.0 - e_out - w_out - h_out - l_out, e, w, h, l)
    return weights if mask is None else tuple(x * mask for x in weights)


def apply_step(w, own, east, west, high, low):
    return w[0] * own + w[1] * east + w[2] * west + w[3] * high + w[4] * low


def transport_kernel(
    rows, cols, species,
    mix_hbm, diff_hbm, speed_hbm, heat_hbm, active_hbm, w1_hbm, w2_hbm, w3_hbm,
    b1_hbm, b2_hbm, b3_hbm,
    adv, chosen, w1_p, w2_p, w13_p, w3_p, b13_p, b2_ref, b3_p,
    b1_ref, b3_ref,
    stage, field, halo, side_w, side_e, to_east, to_west, tile_w, face_w, joins, middle, shifts, beside_v, heat_v, active_v, w1_v, w2_v, w3_v,
    local_sem, send_sem, recv_sem, ready_sem, corner_sem,
):
    r, c = lax.axis_index("row"), lax.axis_index("col")
    tiles = pl.cdiv(species, TILE)
    coef = tiles * TILE
    packed = coef + TILE

    loads = [
        pltpu.make_async_copy(mix_hbm, stage.at[pl.ds(0, species)], local_sem.at[0]),
        pltpu.make_async_copy(diff_hbm, stage.at[coef], local_sem.at[1]),
        pltpu.make_async_copy(speed_hbm, stage.at[pl.ds(coef + 1, 2)], local_sem.at[2]),
        pltpu.make_async_copy(heat_hbm, heat_v, local_sem.at[3]),
        pltpu.make_async_copy(active_hbm, active_v, local_sem.at[4]),
        pltpu.make_async_copy(w1_hbm, w1_v, local_sem.at[5]),
        pltpu.make_async_copy(w2_hbm, w2_v, local_sem.at[6]),
        pltpu.make_async_copy(w3_hbm, w3_v, local_sem.at[7]),
        pltpu.make_async_copy(b1_hbm, b1_ref, local_sem.at[8]),
        pltpu.make_async_copy(b2_hbm, b2_ref, local_sem.at[9]),
        pltpu.make_async_copy(b3_hbm, b3_ref, local_sem.at[10]),
    ]
    for load in loads:
        load.start()
    halo[...] = jnp.zeros_like(halo)
    side_w[...] = jnp.zeros_like(side_w)
    side_e[...] = jnp.zeros_like(side_e)

    def there(dr, dc):
        ok = jnp.bool_(True)
        if dr:
            ok = jnp.logical_and(ok, r + dr < rows if dr > 0 else r + dr >= 0)
        if dc:
            ok = jnp.logical_and(ok, c + dc < cols if dc > 0 else c + dc >= 0)
        return ok

    barrier = pltpu.get_barrier_semaphore()
    for dr, dc in ABOVE:
        @pl.when(there(dr, dc))
        def _(dr=dr, dc=dc):
            pl.semaphore_signal(barrier, inc=1, device_id=(r + dr, c + dc), device_id_type=MESH_ID)

    one = lambda ok: jnp.where(ok, 1, 0)
    below = sum(one(there(dr, dc)) for dr, dc in BELOW)

    @pl.when(below > 0)
    def _():
        pl.semaphore_wait(barrier, below)

    for n, (dr, dc) in enumerate(BELOW):
        @pl.when(there(dr, dc))
        def _(n=n, dr=dr, dc=dc):
            pl.semaphore_signal(ready_sem.at[n], inc=1, device_id=(r + dr, c + dc), device_id_type=MESH_ID)

    @pl.when(there(-1, -1))
    def _():
        for n, way in enumerate(((0, -1), (-1, 0))):
            pl.semaphore_signal(corner_sem.at[n], inc=1, device_id=(r + way[0], c + way[1]), device_id_type=MESH_ID)

    for s in [*range(species, coef), *range(coef + 3, coef + TILE)]:
        stage[s] = jnp.zeros(stage.shape[1:], jnp.float32)
    lane = lax.broadcasted_iota(jnp.int32, (TILE, 128), 1)
    row = lax.broadcasted_iota(jnp.int32, (TILE, 128), 0)
    west_end, east_end = lane == 0, lane == 127
    in_slot = lane % SLOT
    slot = lane // SLOT
    for load in loads[:3]:
        load.wait()
    by_row = stage.reshape(stage.shape[0] * TILE, 128)
    def packing(parts):
        pack = None
        for k, x in enumerate(parts):
            x = roll_lanes(x, SLOT * k + EDGE)
            pack = x if pack is None else jnp.where(slot == k, x, pack)
        return pack

    packs = []
    for q in range(TILE):
        parts = []
        for k in range(tiles + 1):
            parts.append(by_row[pl.ds(TILE * TILE * k + q, TILE, stride=TILE), :])
            field[q, pl.ds(TILE * k, TILE), :] = parts[-1]
        packs.append(packing(parts))
        field[q, pl.ds(packed, TILE), :] = packs[-1]
    for v in range(TILE // SUB):
        for to, shift in ((to_east, 0), (to_west, -EDGE)):
            x = None
            for i in range(SUB):
                part = roll_lanes(packs[SUB * v + i], SUB * i + shift)
                x = part if x is None else jnp.where(in_slot // SUB == i, part, x)
            to[v] = x

    pieces = [(coef, 2 * TILE), (0, coef)]

    def message(index, piece=0):
        dr, dc = DIRECTIONS[index]
        number = index if piece == 0 else len(DIRECTIONS) + (dr + 1) // 2
        rows_from = {1: pl.ds(TILE - EDGE, EDGE), -1: pl.ds(0, EDGE), 0: pl.ds(0, TILE)}[dr]
        if dc == 0:
            some = pl.ds(*pieces[piece])
            src, dst = field.at[rows_from, some], halo.at[pl.ds(0 if dr > 0 else EDGE, EDGE), some]
        else:
            target = side_w if dc > 0 else side_e
            made = to_east if dc > 0 else to_west
            some, there_ = {1: (pl.ds(1, 1), pl.ds(0, 1)), -1: (pl.ds(0, 1), pl.ds(3, 1)), 0: (pl.ds(0, 2), pl.ds(1, 2))}[dr]
            src, dst = made.at[some], target.at[there_]
        return pltpu.make_async_remote_copy(
            src_ref=src, dst_ref=dst, send_sem=send_sem.at[number], recv_sem=recv_sem.at[number],
            device_id=(r + dr, c + dc), device_id_type=MESH_ID,
        )

    straight = tuple(way for way in DIRECTIONS if 0 in way)
    corners = tuple(way for way in DIRECTIONS if 0 not in way)

    def for_each(action, numbers, sign, ways=DIRECTIONS):
        for number in numbers:
            for index, (dr, dc) in enumerate(DIRECTIONS):
                if (number and dc) or (dr, dc) not in ways:
                    continue

                @pl.when(there(sign * dr, sign * dc))
                def _(index=index, number=number):
                    action(message(index, number))

    everything = range(len(pieces))
    def send(dr, dc):
        @pl.when(there(dr, dc))
        def _():
            if (dr, dc) in ABOVE:
                pl.semaphore_wait(ready_sem.at[ABOVE.index((dr, dc))], 1)
            elif (dr, dc) in CORNERS:
                pl.semaphore_wait(corner_sem.at[CORNERS.index((dr, dc))], 1)
            for number in everything if dc == 0 else [0]:
                message(DIRECTIONS.index((dr, dc)), number).start()

    for way in ((-1, -1), (0, -1), (-1, 0), (0, 1), (-1, 1), (1, 0), (1, -1), (1, 1)):
        send(*way)

    for load in loads[3:]:
        load.wait()
    w1_p[...] = jnp.zeros_like(w1_p)
    w1_p[pl.ds(0, species + 1), :] = w1_v[...]
    w1_p[pl.ds(WIDTH, species), :] = w1_v[pl.ds(0, species), :]
    rest = b1_ref[...]
    for i in range(3):
        term = rest.astype(jnp.bfloat16)
        w1_p[pl.ds(species + 1 + i, 1), :] = term
        rest = rest - term.astype(jnp.float32)
    w2_p[...] = jnp.transpose(w2_v[...].astype(jnp.float32)).astype(jnp.bfloat16)
    w3_p[...] = jnp.zeros_like(w3_p)
    w3_p[pl.ds(0, species), :] = (CHEM_STEP * w3_v[...].astype(jnp.float32)).astype(jnp.bfloat16)
    w13_p[...] = lax.dot_general(
        w3_p[pl.ds(0, species), :], w1_v[pl.ds(0, species), :], (((0,), (0,)), ((), ())),
        preferred_element_type=jnp.float32,
    ).astype(jnp.bfloat16)
    b3_row = jnp.concatenate([CHEM_STEP * b3_ref[...], jnp.zeros((1, 128 - species), jnp.float32)], axis=1)
    rest, terms = b3_row, []
    for _ in range(3):
        terms.append(rest.astype(jnp.bfloat16).astype(jnp.float32))
        rest = rest - terms[-1]
    terms = jnp.concatenate(terms + [jnp.zeros((5, 128), jnp.float32)], axis=0).astype(jnp.bfloat16)
    b13_p[...] = jnp.sum(jnp.dot(terms[:, :species], w1_v[pl.ds(0, species), :], preferred_element_type=jnp.float32), axis=0, keepdims=True)
    b3_p[...] = SUBSTEPS * jnp.transpose(jnp.broadcast_to(b3_row, (128, 128)))[:WIDTH]

    capacity = chosen.shape[0]
    flags = jnp.where(active_v[...] == 1, 1.0, 0.0)
    upto = lax.broadcasted_iota(jnp.int32, (128, 128), 0) <= lax.broadcasted_iota(jnp.int32, (128, 128), 1)
    upto = jnp.where(upto, 1.0, 0.0).astype(jnp.bfloat16)
    within = jnp.dot(flags.astype(jnp.bfloat16), upto, preferred_element_type=jnp.float32)
    offset = jnp.dot(flags.astype(jnp.bfloat16), jnp.ones((128, 128), jnp.bfloat16), preferred_element_type=jnp.float32)
    offset = jnp.where(row >= 1, pltpu.roll(offset, 1, 0), 0.0)
    for shift in (1, 2, 4):
        offset = offset + jnp.where(row >= shift, pltpu.roll(offset, shift, 0), 0.0)
    place = jnp.where(flags > 0.0, within + offset - 1.0, -1.0)
    index = lax.broadcasted_iota(jnp.int32, (capacity, 128), 0).astype(jnp.float32)
    for q in range(8):
        hit = index == place[q : q + 1]
        chosen[:, 128 * q : 128 * (q + 1)] = jnp.where(hit, 1.0, 0.0).astype(jnp.bfloat16)

    inward = lax.broadcasted_iota(jnp.int32, (2 * 128, 2 * 128), 0) % 128
    outward = lax.broadcasted_iota(jnp.int32, (2 * 128, 2 * 128), 1)
    outward = jnp.where(outward < 128, outward + 1, outward - 129)
    shifts[...] = jnp.where(inward == outward, 1.0, 0.0).astype(jnp.bfloat16)

    def shift(step, e, x):
        high = x.astype(jnp.bfloat16)
        low = (x - high.astype(jnp.float32)).astype(jnp.bfloat16)
        x = jnp.dot(jnp.concatenate([high, low], axis=1), shifts[...], preferred_element_type=jnp.float32)
        beside_v[step, pl.ds(e, x.shape[0] // coef)] = x.reshape(-1, coef, 2 * 128)

    def lines_of(ref, begin, count):
        return jnp.concatenate([ref[begin + i, pl.ds(0, coef), :] for i in range(count)], axis=0)

    for half in range(2):
        shift(0, EDGE + TILE // 2 * half, lines_of(field, TILE // 2 * half, TILE // 2))

    for_each(lambda m: m.wait_recv(), [0], -1, straight)

    def line(e, begin, size=TILE):
        some = pl.ds(begin, size)
        if EDGE <= e < EDGE + TILE:
            return field[e - EDGE, some, :]
        return halo[e if e < EDGE else e - TILE, some, :]

    def joined(x):
        return jnp.where(in_slot == 1, roll_lanes(x, -10), x)

    def beside(x, join, k):
        moved = roll_lanes(join, 126 - SLOT * k)
        return jnp.where(east_end, moved, roll_lanes(x, -1)), jnp.where(west_end, moved, roll_lanes(x, 1))

    exists = lambda ok: jnp.where(ok, 1.0, 0.0)
    from_west, from_east = in_slot < EDGE, jnp.logical_and(in_slot >= 11, in_slot < 14)
    in_cols = jnp.where(from_west, exists(c > 0), jnp.where(from_east, exists(c < cols - 1), 1.0))
    outer = {e: exists(r > 0) for e in range(EDGE)} | {e: exists(r < rows - 1) for e in range(EDGE + TILE, 2 * EDGE + TILE)}
    last = TILE + 2 * EDGE - 1

    def replicate(x, doubling):
        x = jnp.where(slot == tiles, x, 0.0)
        if not doubling:
            return sum((roll_lanes(x, SLOT * i) for i in range(1, 128 // SLOT)), x)
        for step in (16, 32, 64):
            x = x + roll_lanes(x, step)
        return x

    faces, join, coefs = {}, {}, {}

    def face_row(e):
        v, i = divmod(e + 1, SUB)
        west, east, near_ = roll_lanes(side_w[v], -SUB * i), roll_lanes(side_e[v], 11 - SUB * i), roll_lanes(side_e[v], 1 - SUB * i)
        own = line(e, packed)
        own = jnp.where(in_slot < TILE, own, roll_lanes(own, TILE))
        faces[e] = jnp.where(from_west, west, jnp.where(from_east, east, own))
        join[e] = jnp.where(in_slot == 1, near_, west)
        joins[e] = join[e]
        coefs[e] = replicate(faces[e], e in inner)

    def face_between(lower, upper):
        x = 0.5 * (lower + upper)
        return upwind(spread_row(x, 0), spread_row(x, 2))

    def tile_row(e):
        here = line(e, coef)
        high, low = face_between(here, line(e + 1, coef)), face_between(line(e - 1, coef), here)
        east, west = beside(here, join[e], tiles)
        weights = step_weights(0.5 * (here + east), 0.5 * (here + west), high, low, outer.get(e))
        for i in range(5):
            tile_w[5 * e + i] = weights[i]

    def edge_row(e):
        here = coefs[e]
        high, low = face_between(here, coefs[e + 1]), face_between(coefs[e - 1], here)
        east, west = roll_lanes(here, -1), roll_lanes(here, 1)
        mask = in_cols * outer[e] if e in outer else in_cols
        weights = step_weights(0.5 * (here + east), 0.5 * (here + west), high, low, mask)
        for i in range(5):
            face_w[5 * e + i] = weights[i]

    def update_row(step, e):
        take = line if step == 0 else lambda e, begin: middle[step - 1, e, pl.ds(begin, TILE), :]
        w = [tile_w[5 * e + i] for i in range(5)]
        edge = joins[(last + 1) * step + e]
        for k in range(tiles):
            some = pl.ds(TILE * k, TILE)
            moved = roll_lanes(edge, 126 - SLOT * k)
            east = jnp.where(east_end, moved, beside_v[step, e, some, pl.ds(0, 128)])
            west = jnp.where(west_end, moved, beside_v[step, e, some, pl.ds(128, 128)])
            x = apply_step(w, take(e, TILE * k), east, west, take(e + 1, TILE * k), take(e - 1, TILE * k))
            if step < TRANSPORT_STEPS - 1:
                middle[step, e, some, :] = x
                continue
            q = e - EDGE
            if k == tiles - 1:
                heat = jnp.broadcast_to(heat_v[pl.ds(q, 1), :], (TILE, 128))
                n = species - TILE * k
                x = jnp.where(row < n, x, jnp.where(row == n, heat, 1.0))
            adv[q, some, :] = x

    inner = range(EDGE, EDGE + TILE)
    outside = [e for e in range(1, last) if e not in inner]
    for e in inner:
        face_row(e)
        tile_row(e)
    for e in inner[1:-1]:
        edge_row(e)
    adv[:, pl.ds(coef, TILE), :] = jnp.broadcast_to(jnp.where(row < 2, 1.0, 0.0)[None], (TILE, TILE, 128))
    for_each(lambda m: m.wait_recv(), [0], -1, corners)
    for e in outside:
        face_row(e)
        tile_row(e)
    for e in range(2, last - 1):
        if e not in inner[1:-1]:
            edge_row(e)
    for step in range(1, TRANSPORT_STEPS):
        new = {}
        for e in range(1 + step, last - step):
            w = [face_w[5 * e + i] for i in range(5)]
            x = faces[e]
            new[e] = apply_step(w, x, roll_lanes(x, -1), roll_lanes(x, 1), faces[e + 1], faces[e - 1])
            joins[(last + 1) * step + e] = joined(new[e])
        faces = new
    def move(step, *spans):
        for e, n in spans:
            shift(step, e, lines_of(middle.at[step - 1], e, n))

    for e in range(EDGE + 1, EDGE + TILE - 1):
        update_row(0, e)
    move(1, (EDGE + 2, TILE - 4))
    for e in range(EDGE + 2, EDGE + TILE - 2):
        update_row(1, e)
    move(2, (EDGE + 3, TILE - 6))
    for e in range(EDGE + 3, EDGE + TILE - 3):
        update_row(2, e)
    for_each(lambda m: m.wait_recv(), [1], -1)
    shift(0, 1, lines_of(halo, 1, EDGE - 1))
    shift(0, EDGE + TILE, lines_of(halo, EDGE, EDGE - 1))
    for step in range(TRANSPORT_STEPS):
        ahead = EDGE + 1 + step if step <= 2 else last
        if step:
            move(step, (1 + step, 4), (last - step - 4, 4)) if step <= 2 else move(step, (1 + step, (last - 1 - 2 * step) // 4 * 2), (1 + step + (last - 1 - 2 * step) // 4 * 2, last - 1 - 2 * step - (last - 1 - 2 * step) // 4 * 2))
        for e in range(1 + step, last - step):
            if not ahead <= e < last + 1 - ahead:
                update_row(step, e)

    for_each(lambda m: m.wait_send(), everything, 1)


def chemistry_kernel(
    species, adv, chosen, w1_p, w2_p, w13_p, w3_p, b13_p, b2_ref, b3_p, out_hbm,
    pre, sums, out_v, sem,
):
    capacity, cells = chosen.shape
    hidden = w2_p.shape[0]
    chunk = capacity // CHUNKS
    tail = 2 * hidden - capacity
    f32, bf16 = jnp.float32, jnp.bfloat16
    rows = lambda i: pl.ds(chunk * i, chunk)
    by_species = out_v.reshape(WIDTH * TILE, 128)

    def features(p):
        x = jnp.concatenate([adv[2 * p + j] for j in range(2)], axis=1)
        high = x.astype(bf16)
        low = (x - high.astype(f32)).astype(bf16)
        return jnp.concatenate([high, low, jnp.zeros((hidden - 2 * WIDTH, 2 * 128), bf16)], axis=0)

    def cell_tile(x, tile):
        if tile == 0:
            return x[:hidden]
        return jnp.concatenate([x[hidden:], jnp.zeros((tail, x.shape[1]), x.dtype)], axis=0)

    def body(*acc):
        acc0, acc1 = acc[:CHUNKS], acc[CHUNKS : 2 * CHUNKS]
        totals, parts = acc[2 * CHUNKS : 2 * CHUNKS + 2], acc[2 * CHUNKS + 2 :]
        for j in range(2):
            for m in range(2):
                pltpu.matmul_push_rhs(features(2 * m + j), j, m, transpose=True)
        for j in range(2):
            for i in range(CHUNKS):
                for m, accs in enumerate((acc0, acc1)):
                    p = 2 * m + j
                    pltpu.matmul_acc_lhs(accs[i], chosen[rows(i), pl.ds(256 * p, 256)], load_staged_rhs=None if i else j)
        pltpu.matmul_push_rhs(w1_p[...], 0, 1)
        pltpu.matmul_push_rhs(w2_p[...], 0, 0)
        pltpu.matmul_push_rhs(w13_p[...], 1, 1)
        for i in range(CHUNKS):
            x = (pltpu.matmul_pop(acc0[i]) + pltpu.matmul_pop(acc1[i])).astype(bf16)
            pltpu.matmul_acc_lhs(acc1[i], x, load_staged_rhs=None if i else 0)
        last = []
        for step in range(SUBSTEPS):
            for i in range(CHUNKS):
                x = pltpu.matmul_pop(acc1[i])
                if step:
                    x = x + pre[rows(i), :]
                if step < SUBSTEPS - 1:
                    pre[rows(i), :] = x + b13_p[...]
                pltpu.matmul_acc_lhs(acc0[i], jnp.tanh(x).astype(bf16), load_staged_rhs=None if step or i else 0)
            if step == SUBSTEPS - 1:
                x = sums[...]
                high = x.astype(bf16)
                low = (x - high.astype(f32)).astype(bf16)
                for tile in range(2):
                    for j, x in enumerate((high, low)):
                        pltpu.matmul_push_rhs(cell_tile(x, tile), j, 1, transpose=True)
                        pltpu.matmul_acc_lhs(totals[tile], w3_p[...], load_staged_rhs=j)
            for i in range(CHUNKS):
                h = jnp.tanh(pltpu.matmul_pop(acc0[i]) + b2_ref[...]).astype(bf16)
                if step == SUBSTEPS - 1:
                    last.append(h)
                    continue
                pltpu.matmul_acc_lhs(acc1[i], h, load_staged_rhs=None if step or i else 1)
                h = h.astype(f32)
                sums[rows(i), :] = h if step == 0 else sums[rows(i), :] + h
        h = jnp.concatenate(last, axis=0)
        for tile in range(2):
            pltpu.matmul_push_rhs(cell_tile(h, tile), tile, 1, transpose=True)
        for tile in range(2):
            pltpu.matmul_acc_lhs(totals[tile], w3_p[...], load_staged_rhs=tile)

        def place(m, j, tile):
            flags = chosen[:, pl.ds(256 * (2 * m + j), 256)]
            pltpu.matmul_push_rhs(cell_tile(flags, tile), tile, m)

        for tile in range(2):
            for m in range(2):
                place(m, 0, tile)
        terms = []
        for tile in range(2):
            x = pltpu.matmul_pop(totals[tile]) + jnp.concatenate([b3_p[...]] * 2, axis=1)
            high = x.astype(bf16)
            terms.append((high, (x - high.astype(f32)).astype(bf16)))
        for j in range(2):
            for tile in range(2):
                for m in range(2):
                    pltpu.matmul_acc_lhs(parts[2 * m + j], terms[tile][0], load_staged_rhs=tile)
                    pltpu.matmul_acc_lhs(parts[2 * m + j], terms[tile][1])
                    if j == 0:
                        place(m, 1, tile)
        for j in range(2):
            for m in range(2):
                x = pltpu.matmul_pop(parts[2 * m + j])
                for k in range(2):
                    q = 2 * (2 * m + j) + k
                    y = adv[q] + x[:, 128 * k : 128 * (k + 1)]
                    for t in range(WIDTH // TILE):
                        by_species[pl.ds(TILE * TILE * t + q, TILE, stride=TILE), :] = y[TILE * t : TILE * (t + 1)]

    accs = [pltpu.ACC(m)((chunk, hidden), f32) for m in (0, 1) for _ in range(CHUNKS)]
    accs += [pltpu.ACC(1)((WIDTH, hidden), f32) for _ in range(2)]
    accs += [pltpu.ACC(m)((WIDTH, hidden), f32) for m in (0, 1) for _ in range(2)]
    pl.run_scoped(body, *accs)
    copy = pltpu.make_async_copy(out_v.at[pl.ds(0, species)], out_hbm, sem)
    copy.start()
    copy.wait()


def shards(rows, cols, mix, diff, speed, heat, active, w1, b1, w2, b2, w3, b3):
    species, height, width = mix.shape
    tiles = pl.cdiv(species, TILE)
    lines = height + 2 * EDGE
    hidden, features = w1.shape
    vm = pltpu.VMEM
    f32, bf16 = jnp.float32, jnp.bfloat16
    held = lambda x: pltpu.with_memory_space_constraint(x, pltpu.HBM)
    capacity = 3 * (height * width // 8)
    middle = [
        ((height, WIDTH, width), f32),
        ((capacity, height * width), bf16),
        ((hidden, hidden), bf16),
        ((hidden, hidden), bf16),
        ((hidden, hidden), bf16),
        ((WIDTH, hidden), bf16),
        ((1, hidden), f32),
        ((1, hidden), f32),
        ((WIDTH, 128), f32),
    ]
    made = pl.pallas_call(
        functools.partial(transport_kernel, rows, cols, species),
        out_shape=[jax.ShapeDtypeStruct(*x) for x in middle],
        in_specs=[pl.BlockSpec(memory_space=pltpu.HBM)] * 11,
        out_specs=[pl.BlockSpec(memory_space=vm)] * len(middle),
        scratch_shapes=[
            vm((1, hidden), f32),
            vm((1, species), f32),
            vm((TILE * (tiles + 1), height, width), f32),
            vm((height, TILE * (tiles + 2), width), f32),
            vm((2 * EDGE, TILE * (tiles + 2), width), f32),
            vm((SUB, TILE, width), f32),
            vm((SUB, TILE, width), f32),
            vm((height // SUB, TILE, width), f32),
            vm((height // SUB, TILE, width), f32),
            vm((5 * lines, TILE, width), f32),
            vm((5 * lines, TILE, width), f32),
            vm((TRANSPORT_STEPS * lines, TILE, width), f32),
            vm((TRANSPORT_STEPS - 1, lines, TILE * tiles, width), f32),
            vm((2 * width, 2 * width), bf16),
            vm((TRANSPORT_STEPS, lines, TILE * tiles, 2 * width), f32),
            vm((height, width), f32),
            vm((height, width), jnp.int32),
            vm((features, hidden), bf16),
            vm(w2.shape, bf16),
            vm(w3.shape, bf16),
            pltpu.SemaphoreType.DMA((11,)),
            pltpu.SemaphoreType.DMA((len(DIRECTIONS) + 2,)),
            pltpu.SemaphoreType.DMA((len(DIRECTIONS) + 2,)),
            pltpu.SemaphoreType.REGULAR((len(ABOVE),)),
            pltpu.SemaphoreType.REGULAR((len(CORNERS),)),
        ],
        compiler_params=pltpu.CompilerParams(collective_id=0, has_side_effects=True, vmem_limit_bytes=24 << 20),
    )(*(held(x) for x in (mix, diff, speed, heat, active, w1.T, w2, w3, b1[None], b2[None], b3[None])))
    return pl.pallas_call(
        functools.partial(chemistry_kernel, species),
        out_shape=jax.ShapeDtypeStruct(mix.shape, mix.dtype),
        in_specs=[pl.BlockSpec(memory_space=vm)] * len(middle),
        out_specs=pl.BlockSpec(memory_space=pltpu.HBM),
        scratch_shapes=[
            vm((capacity, hidden), f32),
            vm((capacity, hidden), f32),
            vm((WIDTH, height, width), f32),
            pltpu.SemaphoreType.DMA,
        ],
        compiler_params=pltpu.CompilerParams(vmem_limit_bytes=16 << 20),
    )(*made)


def solution(mesh):
    tile = P(None, "row", "col")
    plane = P("row", "col")
    mapped = jax.shard_map(
        functools.partial(shards, mesh.shape["row"], mesh.shape["col"]),
        mesh=mesh,
        in_specs=(tile, plane, tile, plane, plane, P(), P(), P(), P(), P(), P()),
        out_specs=tile,
        check_vma=False,
    )

    def run(*args):
        with jax.sharding.use_abstract_mesh(mesh.abstract_mesh):
            return mapped(*args)

    return run
```

```python
import functools

import jax
import jax.numpy as jnp
from jax import lax
from jax.experimental import pallas as pl
from jax.experimental.pallas import tpu as pltpu
from jax.sharding import PartitionSpec as P

SUBSTEPS = 8
TRANSPORT_STEPS = 3
CHEM_STEP = 0.0625
TILE = 8
SLOT = 16
EDGE = 3
SUB = 4
CHUNKS = 4
WIDTH = 64
MESH_ID = pl.DeviceIdType.MESH
DIRECTIONS = tuple((dr, dc) for dr in (-1, 0, 1) for dc in (-1, 0, 1) if (dr, dc) != (0, 0))
ABOVE = ((0, 1), (1, 0), (1, 1))
BELOW = tuple((-dr, -dc) for dr, dc in ABOVE)
CORNERS = ((-1, 1), (1, -1))

def roll_lanes(x, shift):
    return pltpu.roll(x, shift % x.shape[-1], x.ndim - 1)


def upwind(d, v):
    return d - jnp.minimum(v, 0.0), d + jnp.maximum(v, 0.0)


def spread_row(x, i):
    return jnp.broadcast_to(x[i : i + 1], x.shape)


def step_weights(east, west, high, low, mask):
    (e, e_out), (w_out, w) = upwind(*(spread_row(east, i) for i in (0, 1))), upwind(*(spread_row(west, i) for i in (0, 1)))
    (h, h_out), (l_out, l) = high, low
    weights = (1.0 - e_out - w_out - h_out - l_out, e, w, h, l)
    return weights if mask is None else tuple(x * mask for x in weights)


def apply_step(w, own, east, west, high, low):
    return w[0] * own + w[1] * east + w[2] * west + w[3] * high + w[4] * low


def transport_kernel(
    rows, cols, species,
    mix_hbm, diff_hbm, speed_hbm, heat_hbm, active_hbm, w1_hbm, w2_hbm, w3_hbm,
    b1_hbm, b2_hbm, b3_hbm,
    adv, chosen, w1_p, w2_p, w13_p, w3_p, b13_p, b2_ref, b3_p,
    b1_ref, b3_ref,
    stage, field, halo, side_w, side_e, to_east, to_west, tile_w, face_w, joins, middle, shifts, beside_v, heat_v, active_v, w1_v, w2_v, w3_v,
    local_sem, send_sem, recv_sem, ready_sem, corner_sem,
):
    r, c = lax.axis_index("row"), lax.axis_index("col")
    tiles = pl.cdiv(species, TILE)
    coef = tiles * TILE
    packed = coef + TILE

    loads = [
        pltpu.make_async_copy(mix_hbm, stage.at[pl.ds(0, species)], local_sem.at[0]),
        pltpu.make_async_copy(diff_hbm, stage.at[coef], local_sem.at[1]),
        pltpu.make_async_copy(speed_hbm, stage.at[pl.ds(coef + 1, 2)], local_sem.at[2]),
        pltpu.make_async_copy(heat_hbm, heat_v, local_sem.at[3]),
        pltpu.make_async_copy(active_hbm, active_v, local_sem.at[4]),
        pltpu.make_async_copy(w1_hbm, w1_v, local_sem.at[5]),
        pltpu.make_async_copy(w2_hbm, w2_v, local_sem.at[6]),
        pltpu.make_async_copy(w3_hbm, w3_v, local_sem.at[7]),
        pltpu.make_async_copy(b1_hbm, b1_ref, local_sem.at[8]),
        pltpu.make_async_copy(b2_hbm, b2_ref, local_sem.at[9]),
        pltpu.make_async_copy(b3_hbm, b3_ref, local_sem.at[10]),
    ]
    for load in loads:
        load.start()
    halo[...] = jnp.zeros_like(halo)
    side_w[...] = jnp.zeros_like(side_w)
    side_e[...] = jnp.zeros_like(side_e)

    def there(dr, dc):
        ok = jnp.bool_(True)
        if dr:
            ok = jnp.logical_and(ok, r + dr < rows if dr > 0 else r + dr >= 0)
        if dc:
            ok = jnp.logical_and(ok, c + dc < cols if dc > 0 else c + dc >= 0)
        return ok

    barrier = pltpu.get_barrier_semaphore()
    for dr, dc in ABOVE:
        @pl.when(there(dr, dc))
        def _(dr=dr, dc=dc):
            pl.semaphore_signal(barrier, inc=1, device_id=(r + dr, c + dc), device_id_type=MESH_ID)

    one = lambda ok: jnp.where(ok, 1, 0)
    below = sum(one(there(dr, dc)) for dr, dc in BELOW)

    @pl.when(below > 0)
    def _():
        pl.semaphore_wait(barrier, below)

    for n, (dr, dc) in enumerate(BELOW):
        @pl.when(there(dr, dc))
        def _(n=n, dr=dr, dc=dc):
            pl.semaphore_signal(ready_sem.at[n], inc=1, device_id=(r + dr, c + dc), device_id_type=MESH_ID)

    @pl.when(there(-1, -1))
    def _():
        for n, way in enumerate(((0, -1), (-1, 0))):
            pl.semaphore_signal(corner_sem.at[n], inc=1, device_id=(r + way[0], c + way[1]), device_id_type=MESH_ID)

    for s in [*range(species, coef), *range(coef + 3, coef + TILE)]:
        stage[s] = jnp.zeros(stage.shape[1:], jnp.float32)
    lane = lax.broadcasted_iota(jnp.int32, (TILE, 128), 1)
    row = lax.broadcasted_iota(jnp.int32, (TILE, 128), 0)
    west_end, east_end = lane == 0, lane == 127
    in_slot = lane % SLOT
    slot = lane // SLOT
    for load in loads[:3]:
        load.wait()
    by_row = stage.reshape(stage.shape[0] * TILE, 128)
    ahead = lambda n: (lane + 128 - n) % 128
    packs = []
    for q in range(TILE):
        pack, offset = None, SUB * (q % SUB)
        at = ahead(offset) // SLOT
        for k in range(tiles + 1):
            x = by_row[pl.ds(TILE * TILE * k + q, TILE, stride=TILE), :]
            field[q, pl.ds(TILE * k, TILE), :] = x
            x = roll_lanes(x, SLOT * k + EDGE + offset)
            pack = x if pack is None else jnp.where(at == k, x, pack)
        packs.append(pack)
        field[q, pl.ds(packed, TILE), :] = pack
    for v in range(TILE // SUB):
        for to, offset in ((to_east, 0), (to_west, EDGE)):
            x = packs[SUB * v]
            for i in range(1, SUB):
                x = jnp.where(ahead(offset) % SLOT // SUB == i, packs[SUB * v + i], x)
            to[v] = x

    pieces = [(coef, 2 * TILE), (0, coef)]

    def message(index, piece=0):
        dr, dc = DIRECTIONS[index]
        number = index if piece == 0 else len(DIRECTIONS) + (dr + 1) // 2
        rows_from = {1: pl.ds(TILE - EDGE, EDGE), -1: pl.ds(0, EDGE), 0: pl.ds(0, TILE)}[dr]
        if dc == 0:
            some = pl.ds(*pieces[piece])
            src, dst = field.at[rows_from, some], halo.at[pl.ds(0 if dr > 0 else EDGE, EDGE), some]
        else:
            target = side_w if dc > 0 else side_e
            made = to_east if dc > 0 else to_west
            some, there_ = {1: (pl.ds(1, 1), pl.ds(0, 1)), -1: (pl.ds(0, 1), pl.ds(3, 1)), 0: (pl.ds(0, 2), pl.ds(1, 2))}[dr]
            src, dst = made.at[some], target.at[there_]
        return pltpu.make_async_remote_copy(
            src_ref=src, dst_ref=dst, send_sem=send_sem.at[number], recv_sem=recv_sem.at[number],
            device_id=(r + dr, c + dc), device_id_type=MESH_ID,
        )

    straight = tuple(way for way in DIRECTIONS if 0 in way)
    corners = tuple(way for way in DIRECTIONS if 0 not in way)

    def for_each(action, numbers, sign, ways=DIRECTIONS):
        for number in numbers:
            for index, (dr, dc) in enumerate(DIRECTIONS):
                if (number and dc) or (dr, dc) not in ways:
                    continue

                @pl.when(there(sign * dr, sign * dc))
                def _(index=index, number=number):
                    action(message(index, number))

    everything = range(len(pieces))
    def send(dr, dc):
        @pl.when(there(dr, dc))
        def _():
            if (dr, dc) in ABOVE:
                pl.semaphore_wait(ready_sem.at[ABOVE.index((dr, dc))], 1)
            elif (dr, dc) in CORNERS:
                pl.semaphore_wait(corner_sem.at[CORNERS.index((dr, dc))], 1)
            for number in everything if dc == 0 else [0]:
                message(DIRECTIONS.index((dr, dc)), number).start()

    for way in ((-1, -1), (0, -1), (-1, 0), (0, 1), (-1, 1), (1, 0), (1, -1), (1, 1)):
        send(*way)

    for load in loads[3:]:
        load.wait()
    w1_p[...] = jnp.zeros_like(w1_p)
    w1_p[pl.ds(0, species + 1), :] = w1_v[...]
    w1_p[pl.ds(WIDTH, species), :] = w1_v[pl.ds(0, species), :]
    rest = b1_ref[...]
    for i in range(3):
        term = rest.astype(jnp.bfloat16)
        w1_p[pl.ds(species + 1 + i, 1), :] = term
        rest = rest - term.astype(jnp.float32)
    w2_p[...] = jnp.transpose(w2_v[...].astype(jnp.float32)).astype(jnp.bfloat16)
    w3_p[...] = jnp.zeros_like(w3_p)
    w3_p[pl.ds(0, species), :] = (CHEM_STEP * w3_v[...].astype(jnp.float32)).astype(jnp.bfloat16)
    w13_p[...] = lax.dot_general(
        w3_p[pl.ds(0, species), :], w1_v[pl.ds(0, species), :], (((0,), (0,)), ((), ())),
        preferred_element_type=jnp.float32,
    ).astype(jnp.bfloat16)
    b3_row = jnp.concatenate([CHEM_STEP * b3_ref[...], jnp.zeros((1, 128 - species), jnp.float32)], axis=1)
    rest, terms = b3_row, []
    for _ in range(3):
        terms.append(rest.astype(jnp.bfloat16).astype(jnp.float32))
        rest = rest - terms[-1]
    terms = jnp.concatenate(terms + [jnp.zeros((5, 128), jnp.float32)], axis=0).astype(jnp.bfloat16)
    b13_p[...] = jnp.sum(jnp.dot(terms[:, :species], w1_v[pl.ds(0, species), :], preferred_element_type=jnp.float32), axis=0, keepdims=True)
    b3_p[...] = SUBSTEPS * jnp.transpose(jnp.broadcast_to(b3_row, (128, 128)))[:WIDTH]

    capacity = chosen.shape[0]
    flags = jnp.where(active_v[...] == 1, 1.0, 0.0)
    upto = lax.broadcasted_iota(jnp.int32, (128, 128), 0) <= lax.broadcasted_iota(jnp.int32, (128, 128), 1)
    upto = jnp.where(upto, 1.0, 0.0).astype(jnp.bfloat16)
    within = jnp.dot(flags.astype(jnp.bfloat16), upto, preferred_element_type=jnp.float32)
    offset = jnp.dot(flags.astype(jnp.bfloat16), jnp.ones((128, 128), jnp.bfloat16), preferred_element_type=jnp.float32)
    offset = jnp.where(row >= 1, pltpu.roll(offset, 1, 0), 0.0)
    for shift in (1, 2, 4):
        offset = offset + jnp.where(row >= shift, pltpu.roll(offset, shift, 0), 0.0)
    place = jnp.where(flags > 0.0, within + offset - 1.0, -1.0)
    index = lax.broadcasted_iota(jnp.int32, (capacity, 128), 0).astype(jnp.float32)
    for q in range(8):
        hit = index == place[q : q + 1]
        chosen[:, 128 * q : 128 * (q + 1)] = jnp.where(hit, 1.0, 0.0).astype(jnp.bfloat16)

    inward = lax.broadcasted_iota(jnp.int32, (2 * 128, 2 * 128), 0) % 128
    outward = lax.broadcasted_iota(jnp.int32, (2 * 128, 2 * 128), 1)
    outward = jnp.where(outward < 128, outward + 1, outward - 129)
    shifts[...] = jnp.where(inward == outward, 1.0, 0.0).astype(jnp.bfloat16)

    def shift(step, e, x):
        high = x.astype(jnp.bfloat16)
        low = (x - high.astype(jnp.float32)).astype(jnp.bfloat16)
        x = jnp.dot(jnp.concatenate([high, low], axis=1), shifts[...], preferred_element_type=jnp.float32)
        beside_v[step, pl.ds(e, x.shape[0] // coef)] = x.reshape(-1, coef, 2 * 128)

    def lines_of(ref, begin, count):
        return jnp.concatenate([ref[begin + i, pl.ds(0, coef), :] for i in range(count)], axis=0)

    for half in range(2):
        shift(0, EDGE + TILE // 2 * half, lines_of(field, TILE // 2 * half, TILE // 2))

    for_each(lambda m: m.wait_recv(), [0], -1, straight)

    def line(e, begin, size=TILE):
        some = pl.ds(begin, size)
        if EDGE <= e < EDGE + TILE:
            return field[e - EDGE, some, :]
        return halo[e if e < EDGE else e - TILE, some, :]

    def joined(x):
        return jnp.where(in_slot == 1, roll_lanes(x, -10), x)

    def beside(x, join, k):
        moved = roll_lanes(join, 126 - SLOT * k)
        return jnp.where(east_end, moved, roll_lanes(x, -1)), jnp.where(west_end, moved, roll_lanes(x, 1))

    exists = lambda ok: jnp.where(ok, 1.0, 0.0)
    from_west, from_east = in_slot < EDGE, jnp.logical_and(in_slot >= 11, in_slot < 14)
    in_cols = jnp.where(from_west, exists(c > 0), jnp.where(from_east, exists(c < cols - 1), 1.0))
    outer = {e: exists(r > 0) for e in range(EDGE)} | {e: exists(r < rows - 1) for e in range(EDGE + TILE, 2 * EDGE + TILE)}
    last = TILE + 2 * EDGE - 1

    def replicate(x, doubling):
        x = jnp.where(slot == tiles, x, 0.0)
        if not doubling:
            return sum((roll_lanes(x, SLOT * i) for i in range(1, 128 // SLOT)), x)
        for step in (16, 32, 64):
            x = x + roll_lanes(x, step)
        return x

    faces, join, coefs = {}, {}, {}

    def face_row(e):
        v, i = divmod(e + 1, SUB)
        west, east, near_ = roll_lanes(side_w[v], -SUB * i), roll_lanes(side_e[v], 8 - SUB * i), roll_lanes(side_e[v], -2 - SUB * i)
        own = line(e, packed)
        own = jnp.where(in_slot < TILE, roll_lanes(own, -SUB * i), roll_lanes(own, TILE - SUB * i))
        faces[e] = jnp.where(from_west, west, jnp.where(from_east, east, own))
        join[e] = jnp.where(in_slot == 1, near_, west)
        joins[e] = join[e]
        coefs[e] = replicate(faces[e], e in inner)

    def face_between(lower, upper):
        x = 0.5 * (lower + upper)
        return upwind(spread_row(x, 0), spread_row(x, 2))

    def tile_row(e):
        here = line(e, coef)
        high, low = face_between(here, line(e + 1, coef)), face_between(line(e - 1, coef), here)
        east, west = beside(here, join[e], tiles)
        weights = step_weights(0.5 * (here + east), 0.5 * (here + west), high, low, outer.get(e))
        for i in range(5):
            tile_w[5 * e + i] = weights[i]

    def edge_row(e):
        here = coefs[e]
        high, low = face_between(here, coefs[e + 1]), face_between(coefs[e - 1], here)
        east, west = roll_lanes(here, -1), roll_lanes(here, 1)
        mask = in_cols * outer[e] if e in outer else in_cols
        weights = step_weights(0.5 * (here + east), 0.5 * (here + west), high, low, mask)
        for i in range(5):
            face_w[5 * e + i] = weights[i]

    def update_row(step, e):
        take = line if step == 0 else lambda e, begin: middle[step - 1, e, pl.ds(begin, TILE), :]
        w = [tile_w[5 * e + i] for i in range(5)]
        edge = joins[(last + 1) * step + e]
        for k in range(tiles):
            some = pl.ds(TILE * k, TILE)
            moved = roll_lanes(edge, 126 - SLOT * k)
            east = jnp.where(east_end, moved, beside_v[step, e, some, pl.ds(0, 128)])
            west = jnp.where(west_end, moved, beside_v[step, e, some, pl.ds(128, 128)])
            x = apply_step(w, take(e, TILE * k), east, west, take(e + 1, TILE * k), take(e - 1, TILE * k))
            if step < TRANSPORT_STEPS - 1:
                middle[step, e, some, :] = x
                continue
            q = e - EDGE
            if k == tiles - 1:
                heat = jnp.broadcast_to(heat_v[pl.ds(q, 1), :], (TILE, 128))
                n = species - TILE * k
                x = jnp.where(row < n, x, jnp.where(row == n, heat, 1.0))
            adv[q, some, :] = x

    inner = range(EDGE, EDGE + TILE)
    outside = [e for e in range(1, last) if e not in inner]
    for e in inner:
        face_row(e)
        tile_row(e)
    for e in inner[1:-1]:
        edge_row(e)
    adv[:, pl.ds(coef, TILE), :] = jnp.broadcast_to(jnp.where(row < 2, 1.0, 0.0)[None], (TILE, TILE, 128))
    for_each(lambda m: m.wait_recv(), [0], -1, corners)
    for e in outside:
        face_row(e)
        tile_row(e)
    for e in range(2, last - 1):
        if e not in inner[1:-1]:
            edge_row(e)
    for step in range(1, TRANSPORT_STEPS):
        new = {}
        for e in range(1 + step, last - step):
            w = [face_w[5 * e + i] for i in range(5)]
            x = faces[e]
            new[e] = apply_step(w, x, roll_lanes(x, -1), roll_lanes(x, 1), faces[e + 1], faces[e - 1])
            joins[(last + 1) * step + e] = joined(new[e])
        faces = new
    def move(step, *spans):
        for e, n in spans:
            shift(step, e, lines_of(middle.at[step - 1], e, n))

    for e in range(EDGE + 1, EDGE + TILE - 1):
        update_row(0, e)
    move(1, (EDGE + 2, TILE - 4))
    for e in range(EDGE + 2, EDGE + TILE - 2):
        update_row(1, e)
    move(2, (EDGE + 3, TILE - 6))
    for e in range(EDGE + 3, EDGE + TILE - 3):
        update_row(2, e)
    for_each(lambda m: m.wait_recv(), [1], -1)
    shift(0, 1, lines_of(halo, 1, EDGE - 1))
    shift(0, EDGE + TILE, lines_of(halo, EDGE, EDGE - 1))
    for step in range(TRANSPORT_STEPS):
        ahead = EDGE + 1 + step if step <= 2 else last
        if step:
            move(step, (1 + step, 4), (last - step - 4, 4)) if step <= 2 else move(step, (1 + step, (last - 1 - 2 * step) // 4 * 2), (1 + step + (last - 1 - 2 * step) // 4 * 2, last - 1 - 2 * step - (last - 1 - 2 * step) // 4 * 2))
        for e in range(1 + step, last - step):
            if not ahead <= e < last + 1 - ahead:
                update_row(step, e)

    for_each(lambda m: m.wait_send(), everything, 1)


def chemistry_kernel(
    species, adv, chosen, w1_p, w2_p, w13_p, w3_p, b13_p, b2_ref, b3_p, out_hbm,
    pre, sums, out_v, sem,
):
    capacity, cells = chosen.shape
    hidden = w2_p.shape[0]
    chunk = capacity // CHUNKS
    tail = 2 * hidden - capacity
    f32, bf16 = jnp.float32, jnp.bfloat16
    rows = lambda i: pl.ds(chunk * i, chunk)
    by_species = out_v.reshape(WIDTH * TILE, 128)

    def features(p):
        x = jnp.concatenate([adv[2 * p + j] for j in range(2)], axis=1)
        high = x.astype(bf16)
        low = (x - high.astype(f32)).astype(bf16)
        return jnp.concatenate([high, low, jnp.zeros((hidden - 2 * WIDTH, 2 * 128), bf16)], axis=0)

    def cell_tile(x, tile):
        if tile == 0:
            return x[:hidden]
        return jnp.concatenate([x[hidden:], jnp.zeros((tail, x.shape[1]), x.dtype)], axis=0)

    def body(*acc):
        acc0, acc1 = acc[:CHUNKS], acc[CHUNKS : 2 * CHUNKS]
        totals, parts = acc[2 * CHUNKS : 2 * CHUNKS + 2], acc[2 * CHUNKS + 2 :]
        for j in range(2):
            for m in range(2):
                pltpu.matmul_push_rhs(features(2 * m + j), j, m, transpose=True)
        for j in range(2):
            for i in range(CHUNKS):
                for m, accs in enumerate((acc0, acc1)):
                    p = 2 * m + j
                    pltpu.matmul_acc_lhs(accs[i], chosen[rows(i), pl.ds(256 * p, 256)], load_staged_rhs=None if i else j)
        pltpu.matmul_push_rhs(w1_p[...], 0, 1)
        pltpu.matmul_push_rhs(w2_p[...], 0, 0)
        pltpu.matmul_push_rhs(w13_p[...], 1, 1)
        for i in range(CHUNKS):
            x = (pltpu.matmul_pop(acc0[i]) + pltpu.matmul_pop(acc1[i])).astype(bf16)
            pltpu.matmul_acc_lhs(acc1[i], x, load_staged_rhs=None if i else 0)
        last = []
        for step in range(SUBSTEPS):
            for i in range(CHUNKS):
                x = pltpu.matmul_pop(acc1[i])
                if step:
                    x = x + pre[rows(i), :]
                if step < SUBSTEPS - 1:
                    pre[rows(i), :] = x + b13_p[...]
                pltpu.matmul_acc_lhs(acc0[i], jnp.tanh(x).astype(bf16), load_staged_rhs=None if step or i else 0)
            if step == SUBSTEPS - 1:
                x = sums[...]
                high = x.astype(bf16)
                low = (x - high.astype(f32)).astype(bf16)
                for tile in range(2):
                    for j, x in enumerate((high, low)):
                        pltpu.matmul_push_rhs(cell_tile(x, tile), j, 1, transpose=True)
                        pltpu.matmul_acc_lhs(totals[tile], w3_p[...], load_staged_rhs=j)
            for i in range(CHUNKS):
                h = jnp.tanh(pltpu.matmul_pop(acc0[i]) + b2_ref[...]).astype(bf16)
                if step == SUBSTEPS - 1:
                    last.append(h)
                    continue
                pltpu.matmul_acc_lhs(acc1[i], h, load_staged_rhs=None if step or i else 1)
                h = h.astype(f32)
                sums[rows(i), :] = h if step == 0 else sums[rows(i), :] + h
        h = jnp.concatenate(last, axis=0)
        for tile in range(2):
            pltpu.matmul_push_rhs(cell_tile(h, tile), tile, 1, transpose=True)
        for tile in range(2):
            pltpu.matmul_acc_lhs(totals[tile], w3_p[...], load_staged_rhs=tile)

        def place(m, j, tile):
            flags = chosen[:, pl.ds(256 * (2 * m + j), 256)]
            pltpu.matmul_push_rhs(cell_tile(flags, tile), tile, m)

        for tile in range(2):
            for m in range(2):
                place(m, 0, tile)
        terms = []
        for tile in range(2):
            x = pltpu.matmul_pop(totals[tile]) + jnp.concatenate([b3_p[...]] * 2, axis=1)
            high = x.astype(bf16)
            terms.append((high, (x - high.astype(f32)).astype(bf16)))
        for j in range(2):
            for tile in range(2):
                for m in range(2):
                    pltpu.matmul_acc_lhs(parts[2 * m + j], terms[tile][0], load_staged_rhs=tile)
                    pltpu.matmul_acc_lhs(parts[2 * m + j], terms[tile][1])
                    if j == 0:
                        place(m, 1, tile)
        for j in range(2):
            for m in range(2):
                x = pltpu.matmul_pop(parts[2 * m + j])
                for k in range(2):
                    q = 2 * (2 * m + j) + k
                    y = adv[q] + x[:, 128 * k : 128 * (k + 1)]
                    for t in range(WIDTH // TILE):
                        by_species[pl.ds(TILE * TILE * t + q, TILE, stride=TILE), :] = y[TILE * t : TILE * (t + 1)]

    accs = [pltpu.ACC(m)((chunk, hidden), f32) for m in (0, 1) for _ in range(CHUNKS)]
    accs += [pltpu.ACC(1)((WIDTH, hidden), f32) for _ in range(2)]
    accs += [pltpu.ACC(m)((WIDTH, hidden), f32) for m in (0, 1) for _ in range(2)]
    pl.run_scoped(body, *accs)
    copy = pltpu.make_async_copy(out_v.at[pl.ds(0, species)], out_hbm, sem)
    copy.start()
    copy.wait()


def shards(rows, cols, mix, diff, speed, heat, active, w1, b1, w2, b2, w3, b3):
    species, height, width = mix.shape
    tiles = pl.cdiv(species, TILE)
    lines = height + 2 * EDGE
    hidden, features = w1.shape
    vm = pltpu.VMEM
    f32, bf16 = jnp.float32, jnp.bfloat16
    held = lambda x: pltpu.with_memory_space_constraint(x, pltpu.HBM)
    capacity = 3 * (height * width // 8)
    middle = [
        ((height, WIDTH, width), f32),
        ((capacity, height * width), bf16),
        ((hidden, hidden), bf16),
        ((hidden, hidden), bf16),
        ((hidden, hidden), bf16),
        ((WIDTH, hidden), bf16),
        ((1, hidden), f32),
        ((1, hidden), f32),
        ((WIDTH, 128), f32),
    ]
    made = pl.pallas_call(
        functools.partial(transport_kernel, rows, cols, species),
        out_shape=[jax.ShapeDtypeStruct(*x) for x in middle],
        in_specs=[pl.BlockSpec(memory_space=pltpu.HBM)] * 11,
        out_specs=[pl.BlockSpec(memory_space=vm)] * len(middle),
        scratch_shapes=[
            vm((1, hidden), f32),
            vm((1, species), f32),
            vm((TILE * (tiles + 1), height, width), f32),
            vm((height, TILE * (tiles + 2), width), f32),
            vm((2 * EDGE, TILE * (tiles + 2), width), f32),
            vm((SUB, TILE, width), f32),
            vm((SUB, TILE, width), f32),
            vm((height // SUB, TILE, width), f32),
            vm((height // SUB, TILE, width), f32),
            vm((5 * lines, TILE, width), f32),
            vm((5 * lines, TILE, width), f32),
            vm((TRANSPORT_STEPS * lines, TILE, width), f32),
            vm((TRANSPORT_STEPS - 1, lines, TILE * tiles, width), f32),
            vm((2 * width, 2 * width), bf16),
            vm((TRANSPORT_STEPS, lines, TILE * tiles, 2 * width), f32),
            vm((height, width), f32),
            vm((height, width), jnp.int32),
            vm((features, hidden), bf16),
            vm(w2.shape, bf16),
            vm(w3.shape, bf16),
            pltpu.SemaphoreType.DMA((11,)),
            pltpu.SemaphoreType.DMA((len(DIRECTIONS) + 2,)),
            pltpu.SemaphoreType.DMA((len(DIRECTIONS) + 2,)),
            pltpu.SemaphoreType.REGULAR((len(ABOVE),)),
            pltpu.SemaphoreType.REGULAR((len(CORNERS),)),
        ],
        compiler_params=pltpu.CompilerParams(collective_id=0, has_side_effects=True, vmem_limit_bytes=24 << 20),
    )(*(held(x) for x in (mix, diff, speed, heat, active, w1.T, w2, w3, b1[None], b2[None], b3[None])))
    return pl.pallas_call(
        functools.partial(chemistry_kernel, species),
        out_shape=jax.ShapeDtypeStruct(mix.shape, mix.dtype),
        in_specs=[pl.BlockSpec(memory_space=vm)] * len(middle),
        out_specs=pl.BlockSpec(memory_space=pltpu.HBM),
        scratch_shapes=[
            vm((capacity, hidden), f32),
            vm((capacity, hidden), f32),
            vm((WIDTH, height, width), f32),
            pltpu.SemaphoreType.DMA,
        ],
        compiler_params=pltpu.CompilerParams(vmem_limit_bytes=16 << 20),
    )(*made)


def solution(mesh):
    tile = P(None, "row", "col")
    plane = P("row", "col")
    mapped = jax.shard_map(
        functools.partial(shards, mesh.shape["row"], mesh.shape["col"]),
        mesh=mesh,
        in_specs=(tile, plane, tile, plane, plane, P(), P(), P(), P(), P(), P()),
        out_specs=tile,
        check_vma=False,
    )

    def run(*args):
        with jax.sharding.use_abstract_mesh(mesh.abstract_mesh):
            return mapped(*args)

    return run
```

```python
import functools

import jax
import jax.numpy as jnp
from jax import lax
from jax.experimental import pallas as pl
from jax.experimental.pallas import tpu as pltpu
from jax.sharding import PartitionSpec as P

SUBSTEPS = 8
TRANSPORT_STEPS = 3
CHEM_STEP = 0.0625
TILE = 8
SLOT = 16
EDGE = 3
SUB = 4
CHUNKS = 4
WIDTH = 64
MESH_ID = pl.DeviceIdType.MESH
DIRECTIONS = tuple((dr, dc) for dr in (-1, 0, 1) for dc in (-1, 0, 1) if (dr, dc) != (0, 0))
ABOVE = ((0, 1), (1, 0), (1, 1))
BELOW = tuple((-dr, -dc) for dr, dc in ABOVE)
CORNERS = ((-1, 1), (1, -1))

def roll_lanes(x, shift):
    return pltpu.roll(x, shift % x.shape[-1], x.ndim - 1)


def upwind(d, v):
    return d - jnp.minimum(v, 0.0), d + jnp.maximum(v, 0.0)


def spread_row(x, i):
    return jnp.broadcast_to(x[i : i + 1], x.shape)


def step_weights(east, west, high, low, mask):
    (e, e_out), (w_out, w) = upwind(*(spread_row(east, i) for i in (0, 1))), upwind(*(spread_row(west, i) for i in (0, 1)))
    (h, h_out), (l_out, l) = high, low
    weights = (1.0 - e_out - w_out - h_out - l_out, e, w, h, l)
    return weights if mask is None else tuple(x * mask for x in weights)


def apply_step(w, own, east, west, high, low):
    return w[0] * own + w[1] * east + w[2] * west + w[3] * high + w[4] * low


def transport_kernel(
    rows, cols, species,
    mix_hbm, diff_hbm, speed_hbm, heat_hbm, active_hbm, w1_hbm, w2_hbm, w3_hbm,
    b1_hbm, b2_hbm, b3_hbm,
    adv, chosen, w1_p, w2_p, w13_p, w3_p, b13_p, b2_ref, b3_p,
    b1_ref, b3_ref,
    stage, field, halo, side_w, side_e, to_east, to_west, tile_w, face_w, joins, middle, shifts, beside_v, heat_v, active_v, w1_v, w2_v, w3_v,
    local_sem, recv_sem, ready_sem, corner_sem,
):
    r, c = lax.axis_index("row"), lax.axis_index("col")
    tiles = pl.cdiv(species, TILE)
    coef = tiles * TILE
    packed = coef + TILE

    loads = [
        pltpu.make_async_copy(mix_hbm, stage.at[pl.ds(0, species)], local_sem.at[0]),
        pltpu.make_async_copy(diff_hbm, stage.at[coef], local_sem.at[1]),
        pltpu.make_async_copy(speed_hbm, stage.at[pl.ds(coef + 1, 2)], local_sem.at[2]),
        pltpu.make_async_copy(heat_hbm, heat_v, local_sem.at[3]),
        pltpu.make_async_copy(active_hbm, active_v, local_sem.at[4]),
        pltpu.make_async_copy(w1_hbm, w1_v, local_sem.at[5]),
        pltpu.make_async_copy(w2_hbm, w2_v, local_sem.at[6]),
        pltpu.make_async_copy(w3_hbm, w3_v, local_sem.at[7]),
        pltpu.make_async_copy(b1_hbm, b1_ref, local_sem.at[8]),
        pltpu.make_async_copy(b2_hbm, b2_ref, local_sem.at[9]),
        pltpu.make_async_copy(b3_hbm, b3_ref, local_sem.at[10]),
    ]
    for load in loads:
        load.start()
    halo[...] = jnp.zeros_like(halo)
    side_w[...] = jnp.zeros_like(side_w)
    side_e[...] = jnp.zeros_like(side_e)

    def there(dr, dc):
        ok = jnp.bool_(True)
        if dr:
            ok = jnp.logical_and(ok, r + dr < rows if dr > 0 else r + dr >= 0)
        if dc:
            ok = jnp.logical_and(ok, c + dc < cols if dc > 0 else c + dc >= 0)
        return ok

    barrier = pltpu.get_barrier_semaphore()
    for dr, dc in ABOVE:
        @pl.when(there(dr, dc))
        def _(dr=dr, dc=dc):
            pl.semaphore_signal(barrier, inc=1, device_id=(r + dr, c + dc), device_id_type=MESH_ID)

    one = lambda ok: jnp.where(ok, 1, 0)
    below = sum(one(there(dr, dc)) for dr, dc in BELOW)

    @pl.when(below > 0)
    def _():
        pl.semaphore_wait(barrier, below)

    for n, (dr, dc) in enumerate(BELOW):
        @pl.when(there(dr, dc))
        def _(n=n, dr=dr, dc=dc):
            pl.semaphore_signal(ready_sem.at[n], inc=1, device_id=(r + dr, c + dc), device_id_type=MESH_ID)

    @pl.when(there(-1, -1))
    def _():
        for n, way in enumerate(((0, -1), (-1, 0))):
            pl.semaphore_signal(corner_sem.at[n], inc=1, device_id=(r + way[0], c + way[1]), device_id_type=MESH_ID)

    for s in [*range(species, coef), *range(coef + 3, coef + TILE)]:
        stage[s] = jnp.zeros(stage.shape[1:], jnp.float32)
    lane = lax.broadcasted_iota(jnp.int32, (TILE, 128), 1)
    row = lax.broadcasted_iota(jnp.int32, (TILE, 128), 0)
    west_end, east_end = lane == 0, lane == 127
    in_slot = lane % SLOT
    slot = lane // SLOT
    for load in loads[:3]:
        load.wait()
    by_row = stage.reshape(stage.shape[0] * TILE, 128)
    ahead = lambda n: (lane + 128 - n) % 128
    packs = []
    for q in range(TILE):
        pack, offset = None, SUB * (q % SUB)
        at = ahead(offset) // SLOT
        for k in range(tiles + 1):
            x = by_row[pl.ds(TILE * TILE * k + q, TILE, stride=TILE), :]
            field[q, pl.ds(TILE * k, TILE), :] = x
            x = roll_lanes(x, SLOT * k + EDGE + offset)
            pack = x if pack is None else jnp.where(at == k, x, pack)
        packs.append(pack)
        field[q, pl.ds(packed, TILE), :] = pack
    for v in range(TILE // SUB):
        for to, offset in ((to_east, 0), (to_west, EDGE)):
            x = packs[SUB * v]
            for i in range(1, SUB):
                x = jnp.where(ahead(offset) % SLOT // SUB == i, packs[SUB * v + i], x)
            to[v] = x

    pieces = [(coef, 2 * TILE), (0, coef)]

    def message(index, piece=0):
        dr, dc = DIRECTIONS[index]
        number = index if piece == 0 else len(DIRECTIONS) + (dr + 1) // 2
        rows_from = {1: pl.ds(TILE - EDGE, EDGE), -1: pl.ds(0, EDGE), 0: pl.ds(0, TILE)}[dr]
        if dc == 0:
            some = pl.ds(*pieces[piece])
            src, dst = field.at[rows_from, some], halo.at[pl.ds(0 if dr > 0 else EDGE, EDGE), some]
        else:
            target = side_w if dc > 0 else side_e
            made = to_east if dc > 0 else to_west
            some, there_ = {1: (pl.ds(1, 1), pl.ds(0, 1)), -1: (pl.ds(0, 1), pl.ds(3, 1)), 0: (pl.ds(0, 2), pl.ds(1, 2))}[dr]
            src, dst = made.at[some], target.at[there_]
        return pltpu.make_async_remote_copy(
            src_ref=src, dst_ref=dst, send_sem=local_sem.at[number], recv_sem=recv_sem.at[number],
            device_id=(r + dr, c + dc), device_id_type=MESH_ID,
        )

    straight = tuple(way for way in DIRECTIONS if 0 in way)
    corners = tuple(way for way in DIRECTIONS if 0 not in way)

    def for_each(action, numbers, sign, ways=DIRECTIONS):
        for number in numbers:
            for index, (dr, dc) in enumerate(DIRECTIONS):
                if (number and dc) or (dr, dc) not in ways:
                    continue

                @pl.when(there(sign * dr, sign * dc))
                def _(index=index, number=number):
                    action(message(index, number))

    everything = range(len(pieces))
    def send(dr, dc):
        @pl.when(there(dr, dc))
        def _():
            if (dr, dc) in ABOVE:
                pl.semaphore_wait(ready_sem.at[ABOVE.index((dr, dc))], 1)
            elif (dr, dc) in CORNERS:
                pl.semaphore_wait(corner_sem.at[CORNERS.index((dr, dc))], 1)
            for number in everything if dc == 0 else [0]:
                message(DIRECTIONS.index((dr, dc)), number).start()

    for load in loads[3:]:
        load.wait()
    for way in ((-1, -1), (0, -1), (-1, 0), (0, 1), (-1, 1), (1, 0), (1, -1), (1, 1)):
        send(*way)

    w1_p[...] = jnp.zeros_like(w1_p)
    w1_p[pl.ds(0, species + 1), :] = w1_v[...]
    w1_p[pl.ds(WIDTH, species), :] = w1_v[pl.ds(0, species), :]
    rest = b1_ref[...]
    for i in range(3):
        term = rest.astype(jnp.bfloat16)
        w1_p[pl.ds(species + 1 + i, 1), :] = term
        rest = rest - term.astype(jnp.float32)
    w2_p[...] = jnp.transpose(w2_v[...].astype(jnp.float32)).astype(jnp.bfloat16)
    w3_p[...] = jnp.zeros_like(w3_p)
    w3_p[pl.ds(0, species), :] = (CHEM_STEP * w3_v[...].astype(jnp.float32)).astype(jnp.bfloat16)
    w13_p[...] = lax.dot_general(
        w3_p[pl.ds(0, species), :], w1_v[pl.ds(0, species), :], (((0,), (0,)), ((), ())),
        preferred_element_type=jnp.float32,
    ).astype(jnp.bfloat16)
    b3_row = jnp.concatenate([CHEM_STEP * b3_ref[...], jnp.zeros((1, 128 - species), jnp.float32)], axis=1)
    rest, terms = b3_row, []
    for _ in range(3):
        terms.append(rest.astype(jnp.bfloat16).astype(jnp.float32))
        rest = rest - terms[-1]
    terms = jnp.concatenate(terms + [jnp.zeros((5, 128), jnp.float32)], axis=0).astype(jnp.bfloat16)
    b13_p[...] = jnp.sum(jnp.dot(terms[:, :species], w1_v[pl.ds(0, species), :], preferred_element_type=jnp.float32), axis=0, keepdims=True)
    b3_p[...] = SUBSTEPS * jnp.transpose(jnp.broadcast_to(b3_row, (128, 128)))[:WIDTH]

    capacity = chosen.shape[0]
    flags = jnp.where(active_v[...] == 1, 1.0, 0.0)
    upto = lax.broadcasted_iota(jnp.int32, (128, 128), 0) <= lax.broadcasted_iota(jnp.int32, (128, 128), 1)
    upto = jnp.where(upto, 1.0, 0.0).astype(jnp.bfloat16)
    within = jnp.dot(flags.astype(jnp.bfloat16), upto, preferred_element_type=jnp.float32)
    offset = jnp.dot(flags.astype(jnp.bfloat16), jnp.ones((128, 128), jnp.bfloat16), preferred_element_type=jnp.float32)
    offset = jnp.where(row >= 1, pltpu.roll(offset, 1, 0), 0.0)
    for shift in (1, 2, 4):
        offset = offset + jnp.where(row >= shift, pltpu.roll(offset, shift, 0), 0.0)
    place = jnp.where(flags > 0.0, within + offset - 1.0, -1.0)
    index = lax.broadcasted_iota(jnp.int32, (capacity, 128), 0).astype(jnp.float32)
    for q in range(8):
        hit = index == place[q : q + 1]
        chosen[:, 128 * q : 128 * (q + 1)] = jnp.where(hit, 1.0, 0.0).astype(jnp.bfloat16)

    inward = lax.broadcasted_iota(jnp.int32, (2 * 128, 2 * 128), 0) % 128
    outward = lax.broadcasted_iota(jnp.int32, (2 * 128, 2 * 128), 1)
    outward = jnp.where(outward < 128, outward + 1, outward - 129)
    shifts[...] = jnp.where(inward == outward, 1.0, 0.0).astype(jnp.bfloat16)

    def shift(step, e, x):
        high = x.astype(jnp.bfloat16)
        low = (x - high.astype(jnp.float32)).astype(jnp.bfloat16)
        x = jnp.dot(jnp.concatenate([high, low], axis=1), shifts[...], preferred_element_type=jnp.float32)
        beside_v[step, pl.ds(e, x.shape[0] // coef)] = x.reshape(-1, coef, 2 * 128)

    def lines_of(ref, begin, count):
        return jnp.concatenate([ref[begin + i, pl.ds(0, coef), :] for i in range(count)], axis=0)

    for half in range(2):
        shift(0, EDGE + TILE // 2 * half, lines_of(field, TILE // 2 * half, TILE // 2))

    for_each(lambda m: m.wait_recv(), [0], -1, straight)

    def line(e, begin, size=TILE):
        some = pl.ds(begin, size)
        if EDGE <= e < EDGE + TILE:
            return field[e - EDGE, some, :]
        return halo[e if e < EDGE else e - TILE, some, :]

    def joined(x):
        return jnp.where(in_slot == 1, roll_lanes(x, -10), x)

    def beside(x, join, k):
        moved = roll_lanes(join, 126 - SLOT * k)
        return jnp.where(east_end, moved, roll_lanes(x, -1)), jnp.where(west_end, moved, roll_lanes(x, 1))

    exists = lambda ok: jnp.where(ok, 1.0, 0.0)
    from_west, from_east = in_slot < EDGE, jnp.logical_and(in_slot >= 11, in_slot < 14)
    in_cols = jnp.where(from_west, exists(c > 0), jnp.where(from_east, exists(c < cols - 1), 1.0))
    outer = {e: exists(r > 0) for e in range(EDGE)} | {e: exists(r < rows - 1) for e in range(EDGE + TILE, 2 * EDGE + TILE)}
    last = TILE + 2 * EDGE - 1

    def replicate(x, doubling):
        x = jnp.where(slot == tiles, x, 0.0)
        if not doubling:
            return sum((roll_lanes(x, SLOT * i) for i in range(1, 128 // SLOT)), x)
        for step in (16, 32, 64):
            x = x + roll_lanes(x, step)
        return x

    faces, join, coefs = {}, {}, {}

    def face_row(e):
        v, i = divmod(e + 1, SUB)
        west, east, near_ = roll_lanes(side_w[v], -SUB * i), roll_lanes(side_e[v], 8 - SUB * i), roll_lanes(side_e[v], -2 - SUB * i)
        own = line(e, packed)
        own = jnp.where(in_slot < TILE, roll_lanes(own, -SUB * i), roll_lanes(own, TILE - SUB * i))
        faces[e] = jnp.where(from_west, west, jnp.where(from_east, east, own))
        join[e] = jnp.where(in_slot == 1, near_, west)
        joins[e] = join[e]
        coefs[e] = replicate(faces[e], e in inner)

    def face_between(lower, upper):
        x = 0.5 * (lower + upper)
        return upwind(spread_row(x, 0), spread_row(x, 2))

    def tile_row(e):
        here = line(e, coef)
        high, low = face_between(here, line(e + 1, coef)), face_between(line(e - 1, coef), here)
        east, west = beside(here, join[e], tiles)
        weights = step_weights(0.5 * (here + east), 0.5 * (here + west), high, low, outer.get(e))
        for i in range(5):
            tile_w[5 * e + i] = weights[i]

    def edge_row(e):
        here = coefs[e]
        high, low = face_between(here, coefs[e + 1]), face_between(coefs[e - 1], here)
        east, west = roll_lanes(here, -1), roll_lanes(here, 1)
        mask = in_cols * outer[e] if e in outer else in_cols
        weights = step_weights(0.5 * (here + east), 0.5 * (here + west), high, low, mask)
        for i in range(5):
            face_w[5 * e + i] = weights[i]

    def update_row(step, e):
        take = line if step == 0 else lambda e, begin: middle[step - 1, e, pl.ds(begin, TILE), :]
        w = [tile_w[5 * e + i] for i in range(5)]
        edge = joins[(last + 1) * step + e]
        for k in range(tiles):
            some = pl.ds(TILE * k, TILE)
            moved = roll_lanes(edge, 126 - SLOT * k)
            east = jnp.where(east_end, moved, beside_v[step, e, some, pl.ds(0, 128)])
            west = jnp.where(west_end, moved, beside_v[step, e, some, pl.ds(128, 128)])
            x = apply_step(w, take(e, TILE * k), east, west, take(e + 1, TILE * k), take(e - 1, TILE * k))
            if step < TRANSPORT_STEPS - 1:
                middle[step, e, some, :] = x
                continue
            q = e - EDGE
            if k == tiles - 1:
                heat = jnp.broadcast_to(heat_v[pl.ds(q, 1), :], (TILE, 128))
                n = species - TILE * k
                x = jnp.where(row < n, x, jnp.where(row == n, heat, 1.0))
            adv[q, some, :] = x

    inner = range(EDGE, EDGE + TILE)
    outside = [e for e in range(1, last) if e not in inner]
    for e in inner:
        face_row(e)
        tile_row(e)
    for e in inner[1:-1]:
        edge_row(e)
    adv[:, pl.ds(coef, TILE), :] = jnp.broadcast_to(jnp.where(row < 2, 1.0, 0.0)[None], (TILE, TILE, 128))
    for_each(lambda m: m.wait_recv(), [0], -1, corners)
    for e in outside:
        face_row(e)
        tile_row(e)
    for e in range(2, last - 1):
        if e not in inner[1:-1]:
            edge_row(e)
    for step in range(1, TRANSPORT_STEPS):
        new = {}
        for e in range(1 + step, last - step):
            w = [face_w[5 * e + i] for i in range(5)]
            x = faces[e]
            new[e] = apply_step(w, x, roll_lanes(x, -1), roll_lanes(x, 1), faces[e + 1], faces[e - 1])
            joins[(last + 1) * step + e] = joined(new[e])
        faces = new
    def move(step, *spans):
        for e, n in spans:
            shift(step, e, lines_of(middle.at[step - 1], e, n))

    for e in range(EDGE + 1, EDGE + TILE - 1):
        update_row(0, e)
    move(1, (EDGE + 2, TILE - 4))
    for e in range(EDGE + 2, EDGE + TILE - 2):
        update_row(1, e)
    move(2, (EDGE + 3, TILE - 6))
    for e in range(EDGE + 3, EDGE + TILE - 3):
        update_row(2, e)
    for_each(lambda m: m.wait_recv(), [1], -1)
    shift(0, 1, lines_of(halo, 1, EDGE - 1))
    shift(0, EDGE + TILE, lines_of(halo, EDGE, EDGE - 1))
    for step in range(TRANSPORT_STEPS):
        ahead = EDGE + 1 + step if step <= 2 else last
        if step:
            move(step, (1 + step, 4), (last - step - 4, 4)) if step <= 2 else move(step, (1 + step, (last - 1 - 2 * step) // 4 * 2), (1 + step + (last - 1 - 2 * step) // 4 * 2, last - 1 - 2 * step - (last - 1 - 2 * step) // 4 * 2))
        for e in range(1 + step, last - step):
            if not ahead <= e < last + 1 - ahead:
                update_row(step, e)

    for_each(lambda m: m.wait_send(), everything, 1)


def chemistry_kernel(
    species, adv, chosen, w1_p, w2_p, w13_p, w3_p, b13_p, b2_ref, b3_p, out_hbm,
    pre, sums, out_v, sem,
):
    capacity, cells = chosen.shape
    hidden = w2_p.shape[0]
    chunk = capacity // CHUNKS
    tail = 2 * hidden - capacity
    f32, bf16 = jnp.float32, jnp.bfloat16
    rows = lambda i: pl.ds(chunk * i, chunk)
    by_species = out_v.reshape(WIDTH * TILE, 128)

    def features(p):
        x = jnp.concatenate([adv[2 * p + j] for j in range(2)], axis=1)
        high = x.astype(bf16)
        low = (x - high.astype(f32)).astype(bf16)
        return jnp.concatenate([high, low, jnp.zeros((hidden - 2 * WIDTH, 2 * 128), bf16)], axis=0)

    def cell_tile(x, tile):
        if tile == 0:
            return x[:hidden]
        return jnp.concatenate([x[hidden:], jnp.zeros((tail, x.shape[1]), x.dtype)], axis=0)

    def body(*acc):
        acc0, acc1 = acc[:CHUNKS], acc[CHUNKS : 2 * CHUNKS]
        totals, parts = acc[2 * CHUNKS : 2 * CHUNKS + 2], acc[2 * CHUNKS + 2 :]
        for j in range(2):
            for m in range(2):
                pltpu.matmul_push_rhs(features(2 * m + j), j, m, transpose=True)
        for j in range(2):
            for i in range(CHUNKS):
                for m, accs in enumerate((acc0, acc1)):
                    p = 2 * m + j
                    pltpu.matmul_acc_lhs(accs[i], chosen[rows(i), pl.ds(256 * p, 256)], load_staged_rhs=None if i else j)
        pltpu.matmul_push_rhs(w1_p[...], 0, 1)
        pltpu.matmul_push_rhs(w2_p[...], 0, 0)
        pltpu.matmul_push_rhs(w13_p[...], 1, 1)
        for i in range(CHUNKS):
            x = (pltpu.matmul_pop(acc0[i]) + pltpu.matmul_pop(acc1[i])).astype(bf16)
            pltpu.matmul_acc_lhs(acc1[i], x, load_staged_rhs=None if i else 0)
        last = []
        for step in range(SUBSTEPS):
            for i in range(CHUNKS):
                x = pltpu.matmul_pop(acc1[i])
                if step:
                    x = x + pre[rows(i), :]
                if step < SUBSTEPS - 1:
                    pre[rows(i), :] = x + b13_p[...]
                pltpu.matmul_acc_lhs(acc0[i], jnp.tanh(x).astype(bf16), load_staged_rhs=None if step or i else 0)
            if step == SUBSTEPS - 1:
                x = sums[...]
                high = x.astype(bf16)
                low = (x - high.astype(f32)).astype(bf16)
                for tile in range(2):
                    for j, x in enumerate((high, low)):
                        pltpu.matmul_push_rhs(cell_tile(x, tile), j, 1, transpose=True)
                        pltpu.matmul_acc_lhs(totals[tile], w3_p[...], load_staged_rhs=j)
            for i in range(CHUNKS):
                h = jnp.tanh(pltpu.matmul_pop(acc0[i]) + b2_ref[...]).astype(bf16)
                if step == SUBSTEPS - 1:
                    last.append(h)
                    continue
                pltpu.matmul_acc_lhs(acc1[i], h, load_staged_rhs=None if step or i else 1)
                h = h.astype(f32)
                sums[rows(i), :] = h if step == 0 else sums[rows(i), :] + h
        h = jnp.concatenate(last, axis=0)
        for tile in range(2):
            pltpu.matmul_push_rhs(cell_tile(h, tile), tile, 1, transpose=True)
        for tile in range(2):
            pltpu.matmul_acc_lhs(totals[tile], w3_p[...], load_staged_rhs=tile)

        def place(m, j, tile):
            flags = chosen[:, pl.ds(256 * (2 * m + j), 256)]
            pltpu.matmul_push_rhs(cell_tile(flags, tile), tile, m)

        for tile in range(2):
            for m in range(2):
                place(m, 0, tile)
        terms = []
        for tile in range(2):
            x = pltpu.matmul_pop(totals[tile]) + jnp.concatenate([b3_p[...]] * 2, axis=1)
            high = x.astype(bf16)
            terms.append((high, (x - high.astype(f32)).astype(bf16)))
        for j in range(2):
            for tile in range(2):
                for m in range(2):
                    pltpu.matmul_acc_lhs(parts[2 * m + j], terms[tile][0], load_staged_rhs=tile)
                    pltpu.matmul_acc_lhs(parts[2 * m + j], terms[tile][1])
                    if j == 0:
                        place(m, 1, tile)
        for j in range(2):
            for m in range(2):
                x = pltpu.matmul_pop(parts[2 * m + j])
                for k in range(2):
                    q = 2 * (2 * m + j) + k
                    y = adv[q] + x[:, 128 * k : 128 * (k + 1)]
                    for t in range(WIDTH // TILE):
                        by_species[pl.ds(TILE * TILE * t + q, TILE, stride=TILE), :] = y[TILE * t : TILE * (t + 1)]

    accs = [pltpu.ACC(m)((chunk, hidden), f32) for m in (0, 1) for _ in range(CHUNKS)]
    accs += [pltpu.ACC(1)((WIDTH, hidden), f32) for _ in range(2)]
    accs += [pltpu.ACC(m)((WIDTH, hidden), f32) for m in (0, 1) for _ in range(2)]
    pl.run_scoped(body, *accs)
    copy = pltpu.make_async_copy(out_v.at[pl.ds(0, species)], out_hbm, sem)
    copy.start()
    copy.wait()


def shards(rows, cols, mix, diff, speed, heat, active, w1, b1, w2, b2, w3, b3):
    species, height, width = mix.shape
    tiles = pl.cdiv(species, TILE)
    lines = height + 2 * EDGE
    hidden, features = w1.shape
    vm = pltpu.VMEM
    f32, bf16 = jnp.float32, jnp.bfloat16
    held = lambda x: pltpu.with_memory_space_constraint(x, pltpu.HBM)
    capacity = 3 * (height * width // 8)
    middle = [
        ((height, WIDTH, width), f32),
        ((capacity, height * width), bf16),
        ((hidden, hidden), bf16),
        ((hidden, hidden), bf16),
        ((hidden, hidden), bf16),
        ((WIDTH, hidden), bf16),
        ((1, hidden), f32),
        ((1, hidden), f32),
        ((WIDTH, 128), f32),
    ]
    made = pl.pallas_call(
        functools.partial(transport_kernel, rows, cols, species),
        out_shape=[jax.ShapeDtypeStruct(*x) for x in middle],
        in_specs=[pl.BlockSpec(memory_space=pltpu.HBM)] * 11,
        out_specs=[pl.BlockSpec(memory_space=vm)] * len(middle),
        scratch_shapes=[
            vm((1, hidden), f32),
            vm((1, species), f32),
            vm((TILE * (tiles + 1), height, width), f32),
            vm((height, TILE * (tiles + 2), width), f32),
            vm((2 * EDGE, TILE * (tiles + 2), width), f32),
            vm((SUB, TILE, width), f32),
            vm((SUB, TILE, width), f32),
            vm((height // SUB, TILE, width), f32),
            vm((height // SUB, TILE, width), f32),
            vm((5 * lines, TILE, width), f32),
            vm((5 * lines, TILE, width), f32),
            vm((TRANSPORT_STEPS * lines, TILE, width), f32),
            vm((TRANSPORT_STEPS - 1, lines, TILE * tiles, width), f32),
            vm((2 * width, 2 * width), bf16),
            vm((TRANSPORT_STEPS, lines, TILE * tiles, 2 * width), f32),
            vm((height, width), f32),
            vm((height, width), jnp.int32),
            vm((features, hidden), bf16),
            vm(w2.shape, bf16),
            vm(w3.shape, bf16),
            pltpu.SemaphoreType.DMA((11,)),
            pltpu.SemaphoreType.DMA((len(DIRECTIONS) + 2,)),
            pltpu.SemaphoreType.REGULAR((len(ABOVE),)),
            pltpu.SemaphoreType.REGULAR((len(CORNERS),)),
        ],
        compiler_params=pltpu.CompilerParams(collective_id=0, has_side_effects=True, vmem_limit_bytes=24 << 20),
    )(*(held(x) for x in (mix, diff, speed, heat, active, w1.T, w2, w3, b1[None], b2[None], b3[None])))
    return pl.pallas_call(
        functools.partial(chemistry_kernel, species),
        out_shape=jax.ShapeDtypeStruct(mix.shape, mix.dtype),
        in_specs=[pl.BlockSpec(memory_space=vm)] * len(middle),
        out_specs=pl.BlockSpec(memory_space=pltpu.HBM),
        scratch_shapes=[
            vm((capacity, hidden), f32),
            vm((capacity, hidden), f32),
            vm((WIDTH, height, width), f32),
            pltpu.SemaphoreType.DMA,
        ],
        compiler_params=pltpu.CompilerParams(vmem_limit_bytes=16 << 20),
    )(*made)


def solution(mesh):
    tile = P(None, "row", "col")
    plane = P("row", "col")
    mapped = jax.shard_map(
        functools.partial(shards, mesh.shape["row"], mesh.shape["col"]),
        mesh=mesh,
        in_specs=(tile, plane, tile, plane, plane, P(), P(), P(), P(), P(), P()),
        out_specs=tile,
        check_vma=False,
    )

    def run(*args):
        with jax.sharding.use_abstract_mesh(mesh.abstract_mesh):
            return mapped(*args)

    return run
```

```python
import functools

import jax
import jax.numpy as jnp
from jax import lax
from jax.experimental import pallas as pl
from jax.experimental.pallas import tpu as pltpu
from jax.sharding import PartitionSpec as P

SUBSTEPS = 8
TRANSPORT_STEPS = 3
CHEM_STEP = 0.0625
TILE = 8
SLOT = 16
EDGE = 3
SUB = 4
CHUNKS = 4
WIDTH = 64
MESH_ID = pl.DeviceIdType.MESH
DIRECTIONS = tuple((dr, dc) for dr in (-1, 0, 1) for dc in (-1, 0, 1) if (dr, dc) != (0, 0))
ABOVE = ((0, 1), (1, 0), (1, 1))
BELOW = tuple((-dr, -dc) for dr, dc in ABOVE)
CORNERS = ((-1, 1), (1, -1))

def roll_lanes(x, shift):
    return pltpu.roll(x, shift % x.shape[-1], x.ndim - 1)


def upwind(d, v):
    return d - jnp.minimum(v, 0.0), d + jnp.maximum(v, 0.0)


def spread_row(x, i):
    return jnp.broadcast_to(x[i : i + 1], x.shape)


def step_weights(east, west, high, low, mask):
    (e, e_out), (w_out, w) = upwind(*(spread_row(east, i) for i in (0, 1))), upwind(*(spread_row(west, i) for i in (0, 1)))
    (h, h_out), (l_out, l) = high, low
    weights = (1.0 - e_out - w_out - h_out - l_out, e, w, h, l)
    return weights if mask is None else tuple(x * mask for x in weights)


def apply_step(w, own, east, west, high, low):
    return w[0] * own + w[1] * east + w[2] * west + w[3] * high + w[4] * low


def transport_kernel(
    rows, cols, species,
    mix_hbm, diff_hbm, speed_hbm, heat_hbm, active_hbm, w1_hbm, w2_hbm, w3_hbm,
    b1_hbm, b2_hbm, b3_hbm,
    adv, chosen, w1_p, w2_p, w13_p, w3_p, b13_p, b2_ref, b3_p,
    b1_ref, b3_ref,
    stage, field, halo, side_w, side_e, to_east, to_west, tile_w, face_w, joins, middle, shifts, beside_v, heat_v, active_v, w1_v, w2_v, w3_v,
    local_sem, recv_sem, ready_sem, corner_sem,
):
    r, c = lax.axis_index("row"), lax.axis_index("col")
    tiles = pl.cdiv(species, TILE)
    coef = tiles * TILE
    packed = coef + TILE

    loads = [
        pltpu.make_async_copy(mix_hbm, stage.at[pl.ds(0, species)], local_sem.at[0]),
        pltpu.make_async_copy(diff_hbm, stage.at[coef], local_sem.at[0]),
        pltpu.make_async_copy(speed_hbm, stage.at[pl.ds(coef + 1, 2)], local_sem.at[0]),
        pltpu.make_async_copy(heat_hbm, heat_v, local_sem.at[1]),
        pltpu.make_async_copy(active_hbm, active_v, local_sem.at[2]),
        pltpu.make_async_copy(w1_hbm, w1_v, local_sem.at[3]),
        pltpu.make_async_copy(w2_hbm, w2_v, local_sem.at[4]),
        pltpu.make_async_copy(w3_hbm, w3_v, local_sem.at[5]),
        pltpu.make_async_copy(b1_hbm, b1_ref, local_sem.at[6]),
        pltpu.make_async_copy(b2_hbm, b2_ref, local_sem.at[7]),
        pltpu.make_async_copy(b3_hbm, b3_ref, local_sem.at[8]),
    ]
    for load in loads:
        load.start()
    halo[...] = jnp.zeros_like(halo)
    side_w[...] = jnp.zeros_like(side_w)
    side_e[...] = jnp.zeros_like(side_e)

    def there(dr, dc):
        ok = jnp.bool_(True)
        if dr:
            ok = jnp.logical_and(ok, r + dr < rows if dr > 0 else r + dr >= 0)
        if dc:
            ok = jnp.logical_and(ok, c + dc < cols if dc > 0 else c + dc >= 0)
        return ok

    barrier = pltpu.get_barrier_semaphore()
    for dr, dc in ABOVE:
        @pl.when(there(dr, dc))
        def _(dr=dr, dc=dc):
            pl.semaphore_signal(barrier, inc=1, device_id=(r + dr, c + dc), device_id_type=MESH_ID)

    one = lambda ok: jnp.where(ok, 1, 0)
    below = sum(one(there(dr, dc)) for dr, dc in BELOW)

    @pl.when(below > 0)
    def _():
        pl.semaphore_wait(barrier, below)

    for n, (dr, dc) in enumerate(BELOW):
        @pl.when(there(dr, dc))
        def _(n=n, dr=dr, dc=dc):
            pl.semaphore_signal(ready_sem.at[n], inc=1, device_id=(r + dr, c + dc), device_id_type=MESH_ID)

    @pl.when(there(-1, -1))
    def _():
        for n, way in enumerate(((0, -1), (-1, 0))):
            pl.semaphore_signal(corner_sem.at[n], inc=1, device_id=(r + way[0], c + way[1]), device_id_type=MESH_ID)

    for s in [*range(species, coef), *range(coef + 3, coef + TILE)]:
        stage[s] = jnp.zeros(stage.shape[1:], jnp.float32)
    lane = lax.broadcasted_iota(jnp.int32, (TILE, 128), 1)
    row = lax.broadcasted_iota(jnp.int32, (TILE, 128), 0)
    west_end, east_end = lane == 0, lane == 127
    in_slot = lane % SLOT
    slot = lane // SLOT
    fields = stage.at[pl.ds(0, species + 3)]
    pltpu.make_async_copy(fields, fields, local_sem.at[0]).wait()
    by_row = stage.reshape(stage.shape[0] * TILE, 128)
    ahead = lambda n: (lane + 128 - n) % 128
    packs = []
    for q in range(TILE):
        pack, offset = None, SUB * (q % SUB)
        at = ahead(offset) // SLOT
        for k in range(tiles + 1):
            x = by_row[pl.ds(TILE * TILE * k + q, TILE, stride=TILE), :]
            field[q, pl.ds(TILE * k, TILE), :] = x
            x = roll_lanes(x, SLOT * k + EDGE + offset)
            pack = x if pack is None else jnp.where(at == k, x, pack)
        packs.append(pack)
        field[q, pl.ds(packed, TILE), :] = pack
    for v in range(TILE // SUB):
        for to, offset in ((to_east, 0), (to_west, EDGE)):
            x = packs[SUB * v]
            for i in range(1, SUB):
                x = jnp.where(ahead(offset) % SLOT // SUB == i, packs[SUB * v + i], x)
            to[v] = x

    pieces = [(coef, 2 * TILE), (0, coef)]

    def message(index, piece=0):
        dr, dc = DIRECTIONS[index]
        number = index if piece == 0 else len(DIRECTIONS) + (dr + 1) // 2
        rows_from = {1: pl.ds(TILE - EDGE, EDGE), -1: pl.ds(0, EDGE), 0: pl.ds(0, TILE)}[dr]
        if dc == 0:
            some = pl.ds(*pieces[piece])
            src, dst = field.at[rows_from, some], halo.at[pl.ds(0 if dr > 0 else EDGE, EDGE), some]
        else:
            target = side_w if dc > 0 else side_e
            made = to_east if dc > 0 else to_west
            some, there_ = {1: (pl.ds(1, 1), pl.ds(0, 1)), -1: (pl.ds(0, 1), pl.ds(3, 1)), 0: (pl.ds(0, 2), pl.ds(1, 2))}[dr]
            src, dst = made.at[some], target.at[there_]
        return pltpu.make_async_remote_copy(
            src_ref=src, dst_ref=dst, send_sem=local_sem.at[index], recv_sem=recv_sem.at[number],
            device_id=(r + dr, c + dc), device_id_type=MESH_ID,
        )

    straight = tuple(way for way in DIRECTIONS if 0 in way)
    corners = tuple(way for way in DIRECTIONS if 0 not in way)

    def for_each(action, numbers, sign, ways=DIRECTIONS):
        for number in numbers:
            for index, (dr, dc) in enumerate(DIRECTIONS):
                if (number and dc) or (dr, dc) not in ways:
                    continue

                @pl.when(there(sign * dr, sign * dc))
                def _(index=index, number=number):
                    action(message(index, number))

    everything = range(len(pieces))
    def send(dr, dc):
        @pl.when(there(dr, dc))
        def _():
            if (dr, dc) in ABOVE:
                pl.semaphore_wait(ready_sem.at[ABOVE.index((dr, dc))], 1)
            elif (dr, dc) in CORNERS:
                pl.semaphore_wait(corner_sem.at[CORNERS.index((dr, dc))], 1)
            for number in everything if dc == 0 else [0]:
                message(DIRECTIONS.index((dr, dc)), number).start()

    for load in loads[3:]:
        load.wait()
    for way in ((-1, -1), (0, -1), (-1, 0), (0, 1), (-1, 1), (1, 0), (1, -1), (1, 1)):
        send(*way)

    w1_p[...] = jnp.zeros_like(w1_p)
    w1_p[pl.ds(0, species + 1), :] = w1_v[...]
    w1_p[pl.ds(WIDTH, species), :] = w1_v[pl.ds(0, species), :]
    rest = b1_ref[...]
    for i in range(3):
        term = rest.astype(jnp.bfloat16)
        w1_p[pl.ds(species + 1 + i, 1), :] = term
        rest = rest - term.astype(jnp.float32)
    w2_p[...] = jnp.transpose(w2_v[...].astype(jnp.float32)).astype(jnp.bfloat16)
    w3_p[...] = jnp.zeros_like(w3_p)
    w3_p[pl.ds(0, species), :] = (CHEM_STEP * w3_v[...].astype(jnp.float32)).astype(jnp.bfloat16)
    w13_p[...] = lax.dot_general(
        w3_p[pl.ds(0, species), :], w1_v[pl.ds(0, species), :], (((0,), (0,)), ((), ())),
        preferred_element_type=jnp.float32,
    ).astype(jnp.bfloat16)
    b3_row = jnp.concatenate([CHEM_STEP * b3_ref[...], jnp.zeros((1, 128 - species), jnp.float32)], axis=1)
    rest, terms = b3_row, []
    for _ in range(3):
        terms.append(rest.astype(jnp.bfloat16).astype(jnp.float32))
        rest = rest - terms[-1]
    terms = jnp.concatenate(terms + [jnp.zeros((5, 128), jnp.float32)], axis=0).astype(jnp.bfloat16)
    b13_p[...] = jnp.sum(jnp.dot(terms[:, :species], w1_v[pl.ds(0, species), :], preferred_element_type=jnp.float32), axis=0, keepdims=True)
    b3_p[...] = SUBSTEPS * jnp.transpose(jnp.broadcast_to(b3_row, (128, 128)))[:WIDTH]

    capacity = chosen.shape[0]
    flags = jnp.where(active_v[...] == 1, 1.0, 0.0)
    upto = lax.broadcasted_iota(jnp.int32, (128, 128), 0) <= lax.broadcasted_iota(jnp.int32, (128, 128), 1)
    upto = jnp.where(upto, 1.0, 0.0).astype(jnp.bfloat16)
    within = jnp.dot(flags.astype(jnp.bfloat16), upto, preferred_element_type=jnp.float32)
    offset = jnp.dot(flags.astype(jnp.bfloat16), jnp.ones((128, 128), jnp.bfloat16), preferred_element_type=jnp.float32)
    offset = jnp.where(row >= 1, pltpu.roll(offset, 1, 0), 0.0)
    for shift in (1, 2, 4):
        offset = offset + jnp.where(row >= shift, pltpu.roll(offset, shift, 0), 0.0)
    place = jnp.where(flags > 0.0, within + offset - 1.0, -1.0)
    index = lax.broadcasted_iota(jnp.int32, (capacity, 128), 0).astype(jnp.float32)
    for q in range(8):
        hit = index == place[q : q + 1]
        chosen[:, 128 * q : 128 * (q + 1)] = jnp.where(hit, 1.0, 0.0).astype(jnp.bfloat16)

    inward = lax.broadcasted_iota(jnp.int32, (2 * 128, 2 * 128), 0) % 128
    outward = lax.broadcasted_iota(jnp.int32, (2 * 128, 2 * 128), 1)
    outward = jnp.where(outward < 128, outward + 1, outward - 129)
    shifts[...] = jnp.where(inward == outward, 1.0, 0.0).astype(jnp.bfloat16)

    def shift(step, e, x):
        high = x.astype(jnp.bfloat16)
        low = (x - high.astype(jnp.float32)).astype(jnp.bfloat16)
        x = jnp.dot(jnp.concatenate([high, low], axis=1), shifts[...], preferred_element_type=jnp.float32)
        beside_v[step, pl.ds(e, x.shape[0] // coef)] = x.reshape(-1, coef, 2 * 128)

    def lines_of(ref, begin, count):
        return jnp.concatenate([ref[begin + i, pl.ds(0, coef), :] for i in range(count)], axis=0)

    for half in range(2):
        shift(0, EDGE + TILE // 2 * half, lines_of(field, TILE // 2 * half, TILE // 2))

    for_each(lambda m: m.wait_recv(), [0], -1, straight)

    def line(e, begin, size=TILE):
        some = pl.ds(begin, size)
        if EDGE <= e < EDGE + TILE:
            return field[e - EDGE, some, :]
        return halo[e if e < EDGE else e - TILE, some, :]

    def joined(x):
        return jnp.where(in_slot == 1, roll_lanes(x, -10), x)

    def beside(x, join, k):
        moved = roll_lanes(join, 126 - SLOT * k)
        return jnp.where(east_end, moved, roll_lanes(x, -1)), jnp.where(west_end, moved, roll_lanes(x, 1))

    exists = lambda ok: jnp.where(ok, 1.0, 0.0)
    from_west, from_east = in_slot < EDGE, jnp.logical_and(in_slot >= 11, in_slot < 14)
    in_cols = jnp.where(from_west, exists(c > 0), jnp.where(from_east, exists(c < cols - 1), 1.0))
    outer = {e: exists(r > 0) for e in range(EDGE)} | {e: exists(r < rows - 1) for e in range(EDGE + TILE, 2 * EDGE + TILE)}
    last = TILE + 2 * EDGE - 1

    def replicate(x, doubling):
        x = jnp.where(slot == tiles, x, 0.0)
        if not doubling:
            return sum((roll_lanes(x, SLOT * i) for i in range(1, 128 // SLOT)), x)
        for step in (16, 32, 64):
            x = x + roll_lanes(x, step)
        return x

    faces, join, coefs = {}, {}, {}

    def face_row(e):
        v, i = divmod(e + 1, SUB)
        west, east, near_ = roll_lanes(side_w[v], -SUB * i), roll_lanes(side_e[v], 8 - SUB * i), roll_lanes(side_e[v], -2 - SUB * i)
        own = line(e, packed)
        own = jnp.where(in_slot < TILE, roll_lanes(own, -SUB * i), roll_lanes(own, TILE - SUB * i))
        faces[e] = jnp.where(from_west, west, jnp.where(from_east, east, own))
        join[e] = jnp.where(in_slot == 1, near_, west)
        joins[e] = join[e]
        coefs[e] = replicate(faces[e], e in inner)

    def face_between(lower, upper):
        x = 0.5 * (lower + upper)
        return upwind(spread_row(x, 0), spread_row(x, 2))

    def tile_row(e):
        here = line(e, coef)
        high, low = face_between(here, line(e + 1, coef)), face_between(line(e - 1, coef), here)
        east, west = beside(here, join[e], tiles)
        weights = step_weights(0.5 * (here + east), 0.5 * (here + west), high, low, outer.get(e))
        for i in range(5):
            tile_w[5 * e + i] = weights[i]

    def edge_row(e):
        here = coefs[e]
        high, low = face_between(here, coefs[e + 1]), face_between(coefs[e - 1], here)
        east, west = roll_lanes(here, -1), roll_lanes(here, 1)
        mask = in_cols * outer[e] if e in outer else in_cols
        weights = step_weights(0.5 * (here + east), 0.5 * (here + west), high, low, mask)
        for i in range(5):
            face_w[5 * e + i] = weights[i]

    def update_row(step, e):
        take = line if step == 0 else lambda e, begin: middle[step - 1, e, pl.ds(begin, TILE), :]
        w = [tile_w[5 * e + i] for i in range(5)]
        edge = joins[(last + 1) * step + e]
        for k in range(tiles):
            some = pl.ds(TILE * k, TILE)
            moved = roll_lanes(edge, 126 - SLOT * k)
            east = jnp.where(east_end, moved, beside_v[step, e, some, pl.ds(0, 128)])
            west = jnp.where(west_end, moved, beside_v[step, e, some, pl.ds(128, 128)])
            x = apply_step(w, take(e, TILE * k), east, west, take(e + 1, TILE * k), take(e - 1, TILE * k))
            if step < TRANSPORT_STEPS - 1:
                middle[step, e, some, :] = x
                continue
            q = e - EDGE
            if k == tiles - 1:
                heat = jnp.broadcast_to(heat_v[pl.ds(q, 1), :], (TILE, 128))
                n = species - TILE * k
                x = jnp.where(row < n, x, jnp.where(row == n, heat, 1.0))
            adv[q, some, :] = x

    inner = range(EDGE, EDGE + TILE)
    outside = [e for e in range(1, last) if e not in inner]
    for e in inner:
        face_row(e)
        tile_row(e)
    for e in inner[1:-1]:
        edge_row(e)
    adv[:, pl.ds(coef, TILE), :] = jnp.broadcast_to(jnp.where(row < 2, 1.0, 0.0)[None], (TILE, TILE, 128))
    for_each(lambda m: m.wait_recv(), [0], -1, corners)
    for e in outside:
        face_row(e)
        tile_row(e)
    for e in range(2, last - 1):
        if e not in inner[1:-1]:
            edge_row(e)
    for step in range(1, TRANSPORT_STEPS):
        new = {}
        for e in range(1 + step, last - step):
            w = [face_w[5 * e + i] for i in range(5)]
            x = faces[e]
            new[e] = apply_step(w, x, roll_lanes(x, -1), roll_lanes(x, 1), faces[e + 1], faces[e - 1])
            joins[(last + 1) * step + e] = joined(new[e])
        faces = new
    def move(step, *spans):
        for e, n in spans:
            shift(step, e, lines_of(middle.at[step - 1], e, n))

    for e in range(EDGE + 1, EDGE + TILE - 1):
        update_row(0, e)
    move(1, (EDGE + 2, TILE - 4))
    for e in range(EDGE + 2, EDGE + TILE - 2):
        update_row(1, e)
    move(2, (EDGE + 3, TILE - 6))
    for e in range(EDGE + 3, EDGE + TILE - 3):
        update_row(2, e)
    for_each(lambda m: m.wait_recv(), [1], -1)
    shift(0, 1, lines_of(halo, 1, EDGE - 1))
    shift(0, EDGE + TILE, lines_of(halo, EDGE, EDGE - 1))
    for step in range(TRANSPORT_STEPS):
        ahead = EDGE + 1 + step if step <= 2 else last
        if step:
            move(step, (1 + step, 4), (last - step - 4, 4)) if step <= 2 else move(step, (1 + step, (last - 1 - 2 * step) // 4 * 2), (1 + step + (last - 1 - 2 * step) // 4 * 2, last - 1 - 2 * step - (last - 1 - 2 * step) // 4 * 2))
        for e in range(1 + step, last - step):
            if not ahead <= e < last + 1 - ahead:
                update_row(step, e)

    for index, (dr, dc) in enumerate(DIRECTIONS):
        @pl.when(there(dr, dc))
        def _(index=index, dr=dr, dc=dc):
            if dc:
                message(index).wait_send()
            else:
                sent = field.at[pl.ds(TILE - EDGE if dr > 0 else 0, EDGE)]
                pltpu.make_async_copy(sent, sent, local_sem.at[index]).wait()


def chemistry_kernel(
    species, adv, chosen, w1_p, w2_p, w13_p, w3_p, b13_p, b2_ref, b3_p, out_hbm,
    pre, sums, out_v, sem,
):
    capacity, cells = chosen.shape
    hidden = w2_p.shape[0]
    chunk = capacity // CHUNKS
    tail = 2 * hidden - capacity
    f32, bf16 = jnp.float32, jnp.bfloat16
    rows = lambda i: pl.ds(chunk * i, chunk)
    by_species = out_v.reshape(WIDTH * TILE, 128)

    def features(p):
        x = jnp.concatenate([adv[2 * p + j] for j in range(2)], axis=1)
        high = x.astype(bf16)
        low = (x - high.astype(f32)).astype(bf16)
        return jnp.concatenate([high, low, jnp.zeros((hidden - 2 * WIDTH, 2 * 128), bf16)], axis=0)

    def cell_tile(x, tile):
        if tile == 0:
            return x[:hidden]
        return jnp.concatenate([x[hidden:], jnp.zeros((tail, x.shape[1]), x.dtype)], axis=0)

    def body(*acc):
        acc0, acc1 = acc[:CHUNKS], acc[CHUNKS : 2 * CHUNKS]
        totals, parts = acc[2 * CHUNKS : 2 * CHUNKS + 2], acc[2 * CHUNKS + 2 :]
        for j in range(2):
            for m in range(2):
                pltpu.matmul_push_rhs(features(2 * m + j), j, m, transpose=True)
        for j in range(2):
            for i in range(CHUNKS):
                for m, accs in enumerate((acc0, acc1)):
                    p = 2 * m + j
                    pltpu.matmul_acc_lhs(accs[i], chosen[rows(i), pl.ds(256 * p, 256)], load_staged_rhs=None if i else j)
        pltpu.matmul_push_rhs(w1_p[...], 0, 1)
        pltpu.matmul_push_rhs(w2_p[...], 0, 0)
        pltpu.matmul_push_rhs(w13_p[...], 1, 1)
        for i in range(CHUNKS):
            x = (pltpu.matmul_pop(acc0[i]) + pltpu.matmul_pop(acc1[i])).astype(bf16)
            pltpu.matmul_acc_lhs(acc1[i], x, load_staged_rhs=None if i else 0)
        last = []
        for step in range(SUBSTEPS):
            for i in range(CHUNKS):
                x = pltpu.matmul_pop(acc1[i])
                if step:
                    x = x + pre[rows(i), :]
                if step < SUBSTEPS - 1:
                    pre[rows(i), :] = x + b13_p[...]
                pltpu.matmul_acc_lhs(acc0[i], jnp.tanh(x).astype(bf16), load_staged_rhs=None if step or i else 0)
            if step == SUBSTEPS - 1:
                x = sums[...]
                high = x.astype(bf16)
                low = (x - high.astype(f32)).astype(bf16)
                for tile in range(2):
                    for j, x in enumerate((high, low)):
                        pltpu.matmul_push_rhs(cell_tile(x, tile), j, 1, transpose=True)
                        pltpu.matmul_acc_lhs(totals[tile], w3_p[...], load_staged_rhs=j)
            for i in range(CHUNKS):
                h = jnp.tanh(pltpu.matmul_pop(acc0[i]) + b2_ref[...]).astype(bf16)
                if step == SUBSTEPS - 1:
                    last.append(h)
                    continue
                pltpu.matmul_acc_lhs(acc1[i], h, load_staged_rhs=None if step or i else 1)
                h = h.astype(f32)
                sums[rows(i), :] = h if step == 0 else sums[rows(i), :] + h
        h = jnp.concatenate(last, axis=0)
        for tile in range(2):
            pltpu.matmul_push_rhs(cell_tile(h, tile), tile, 1, transpose=True)
        for tile in range(2):
            pltpu.matmul_acc_lhs(totals[tile], w3_p[...], load_staged_rhs=tile)

        def place(m, j, tile):
            flags = chosen[:, pl.ds(256 * (2 * m + j), 256)]
            pltpu.matmul_push_rhs(cell_tile(flags, tile), tile, m)

        for tile in range(2):
            for m in range(2):
                place(m, 0, tile)
        terms = []
        for tile in range(2):
            x = pltpu.matmul_pop(totals[tile]) + jnp.concatenate([b3_p[...]] * 2, axis=1)
            high = x.astype(bf16)
            terms.append((high, (x - high.astype(f32)).astype(bf16)))
        for j in range(2):
            for tile in range(2):
                for m in range(2):
                    pltpu.matmul_acc_lhs(parts[2 * m + j], terms[tile][0], load_staged_rhs=tile)
                    pltpu.matmul_acc_lhs(parts[2 * m + j], terms[tile][1])
                    if j == 0:
                        place(m, 1, tile)
        for j in range(2):
            for m in range(2):
                x = pltpu.matmul_pop(parts[2 * m + j])
                for k in range(2):
                    q = 2 * (2 * m + j) + k
                    y = adv[q] + x[:, 128 * k : 128 * (k + 1)]
                    for t in range(WIDTH // TILE):
                        by_species[pl.ds(TILE * TILE * t + q, TILE, stride=TILE), :] = y[TILE * t : TILE * (t + 1)]

    accs = [pltpu.ACC(m)((chunk, hidden), f32) for m in (0, 1) for _ in range(CHUNKS)]
    accs += [pltpu.ACC(1)((WIDTH, hidden), f32) for _ in range(2)]
    accs += [pltpu.ACC(m)((WIDTH, hidden), f32) for m in (0, 1) for _ in range(2)]
    pl.run_scoped(body, *accs)
    copy = pltpu.make_async_copy(out_v.at[pl.ds(0, species)], out_hbm, sem)
    copy.start()
    copy.wait()


def shards(rows, cols, mix, diff, speed, heat, active, w1, b1, w2, b2, w3, b3):
    species, height, width = mix.shape
    tiles = pl.cdiv(species, TILE)
    lines = height + 2 * EDGE
    hidden, features = w1.shape
    vm = pltpu.VMEM
    f32, bf16 = jnp.float32, jnp.bfloat16
    held = lambda x: pltpu.with_memory_space_constraint(x, pltpu.HBM)
    capacity = 3 * (height * width // 8)
    middle = [
        ((height, WIDTH, width), f32),
        ((capacity, height * width), bf16),
        ((hidden, hidden), bf16),
        ((hidden, hidden), bf16),
        ((hidden, hidden), bf16),
        ((WIDTH, hidden), bf16),
        ((1, hidden), f32),
        ((1, hidden), f32),
        ((WIDTH, 128), f32),
    ]
    made = pl.pallas_call(
        functools.partial(transport_kernel, rows, cols, species),
        out_shape=[jax.ShapeDtypeStruct(*x) for x in middle],
        in_specs=[pl.BlockSpec(memory_space=pltpu.HBM)] * 11,
        out_specs=[pl.BlockSpec(memory_space=vm)] * len(middle),
        scratch_shapes=[
            vm((1, hidden), f32),
            vm((1, species), f32),
            vm((TILE * (tiles + 1), height, width), f32),
            vm((height, TILE * (tiles + 2), width), f32),
            vm((2 * EDGE, TILE * (tiles + 2), width), f32),
            vm((SUB, TILE, width), f32),
            vm((SUB, TILE, width), f32),
            vm((height // SUB, TILE, width), f32),
            vm((height // SUB, TILE, width), f32),
            vm((5 * lines, TILE, width), f32),
            vm((5 * lines, TILE, width), f32),
            vm((TRANSPORT_STEPS * lines, TILE, width), f32),
            vm((TRANSPORT_STEPS - 1, lines, TILE * tiles, width), f32),
            vm((2 * width, 2 * width), bf16),
            vm((TRANSPORT_STEPS, lines, TILE * tiles, 2 * width), f32),
            vm((height, width), f32),
            vm((height, width), jnp.int32),
            vm((features, hidden), bf16),
            vm(w2.shape, bf16),
            vm(w3.shape, bf16),
            pltpu.SemaphoreType.DMA((9,)),
            pltpu.SemaphoreType.DMA((len(DIRECTIONS) + 2,)),
            pltpu.SemaphoreType.REGULAR((len(ABOVE),)),
            pltpu.SemaphoreType.REGULAR((len(CORNERS),)),
        ],
        compiler_params=pltpu.CompilerParams(collective_id=0, has_side_effects=True, vmem_limit_bytes=24 << 20),
    )(*(held(x) for x in (mix, diff, speed, heat, active, w1.T, w2, w3, b1[None], b2[None], b3[None])))
    return pl.pallas_call(
        functools.partial(chemistry_kernel, species),
        out_shape=jax.ShapeDtypeStruct(mix.shape, mix.dtype),
        in_specs=[pl.BlockSpec(memory_space=vm)] * len(middle),
        out_specs=pl.BlockSpec(memory_space=pltpu.HBM),
        scratch_shapes=[
            vm((capacity, hidden), f32),
            vm((capacity, hidden), f32),
            vm((WIDTH, height, width), f32),
            pltpu.SemaphoreType.DMA,
        ],
        compiler_params=pltpu.CompilerParams(vmem_limit_bytes=16 << 20),
    )(*made)


def solution(mesh):
    tile = P(None, "row", "col")
    plane = P("row", "col")
    mapped = jax.shard_map(
        functools.partial(shards, mesh.shape["row"], mesh.shape["col"]),
        mesh=mesh,
        in_specs=(tile, plane, tile, plane, plane, P(), P(), P(), P(), P(), P()),
        out_specs=tile,
        check_vma=False,
    )

    def run(*args):
        with jax.sharding.use_abstract_mesh(mesh.abstract_mesh):
            return mapped(*args)

    return run
```
